32 devices in a mesh: dp: 8 (over z, y), mp: 4 (over x, core).
Axes of the slice: x: 2, y: 2, z: 4, core: 2. Of those that a mesh axis runs over, the one named last changes fastest.
Arguments:
- features: bfloat16 [5120, 512], P(('dp', 'mp')), may hold values from -6 to 6
- crop_index: int32 [5120], P('dp'), may hold values from 0 to 255, as said below
- grid_size: int32 [5120], P('dp'), may hold values from 3 to 7, as said below
- position: int32 [5120], P('dp'), may hold values from 0 to 49, as said below
- cpe_weight: float32 [2, 9, 512], replicated, may hold values from -1.5 to 1.5
- shared_bias: float32 [2, 3, 512], replicated, may hold values from -3 to 3
- norm_gain: float32 [2, 2, 512], replicated, may hold values from 0.1 to 1.9
- norm_bias: float32 [2, 2, 512], replicated, may hold values from -2 to 2
- qkv_weight: bfloat16 [2, 512, 3, 512], P(None, None, None, 'mp'), may hold values from -0.25 to 0.25
- head_bias: float32 [2, 3, 512], P(None, None, 'mp'), may hold values from -3 to 3
- crpe_weight: float32 [2, 49, 512], P(None, None, 'mp'), may hold values from -1.2 to 1.2
- proj_weight: bfloat16 [2, 512, 512], P(None, 'mp'), may hold values from -0.5 to 0.5
- fc1_weight: bfloat16 [2, 512, 2048], P(None, None, 'mp'), may hold values from -0.25 to 0.25
- fc1_bias: float32 [2, 2048], P(None, 'mp'), may hold values from -3 to 3
- fc2_weight: bfloat16 [2, 2048, 512], P(None, 'mp'), may hold values from -0.1875 to 0.1875
- out_grad: bfloat16 [5120, 512], P(('dp', 'mp')), may hold values from -6 to 6
Outputs:
- output: bfloat16 [5120, 512], P(('dp', 'mp'))
- features_grad: float32 [5120, 512], P(('dp', 'mp'))
- cpe_weight_grad: float32 [2, 9, 512], replicated
- shared_bias_grad: float32 [2, 3, 512], replicated
- norm_gain_grad: float32 [2, 2, 512], replicated
- norm_bias_grad: float32 [2, 2, 512], replicated
- qkv_weight_grad: float32 [2, 512, 3, 512], P(None, None, None, 'mp')
- head_bias_grad: float32 [2, 3, 512], P(None, None, 'mp')
- crpe_weight_grad: float32 [2, 49, 512], P(None, None, 'mp')
- proj_weight_grad: float32 [2, 512, 512], P(None, 'mp')
- fc1_weight_grad: float32 [2, 512, 2048], P(None, None, 'mp')
- fc1_bias_grad: float32 [2, 2048], P(None, 'mp')
- fc2_weight_grad: float32 [2, 2048, 512], P(None, 'mp')
The draws below stay inside these ranges and needn't reach their ends.
Inputs may be any that keep to these rules, and one draw needn't show every extreme that they name: `crop_index`: each image is 160 consecutive rows starting at a multiple of 160; it holds 8 crops of consecutive rows, numbered 8 i to 8 i + 7 in row order for image i, two of grid side 7 and six of side 3, in an order drawn for each image. `grid_size`: the side of the grid of the row's crop, 3 or 7. `position`: 0 on a crop's first row (its class row), then 1 to side times side over its grid cells in row-major order.
All inputs are finite; a program needn't handle non-finite values.
Results may differ from the reference program's by a relative error of at most 0.025.
Values may be sent and summed in bfloat16 or wider, within the bound.
A program may use at most 320 MiB of HBM per device.

```python
import jax
import jax.numpy as jnp
import numpy as np
from jax import lax

D = 512
HEADS = 8
HD = 64
FF = 2048
LAYERS = 2
ROWS_IMG = 160
TOKENS = 5120


def crop_layout(key):
    images = TOKENS // ROWS_IMG
    crop_kinds = jnp.array([7, 7, 3, 3, 3, 3, 3, 3], dtype=jnp.int32)
    image_keys = jax.random.split(key, images)
    orders = jax.vmap(lambda one_key: jax.random.permutation(one_key, 8))(image_keys)
    crop_sides = crop_kinds[orders]
    lengths = crop_sides * crop_sides + 1
    starts = jnp.cumsum(lengths, axis=1) - lengths
    rows_in = jnp.arange(ROWS_IMG, dtype=jnp.int32)
    local_crop = jnp.sum((rows_in[None, :, None] >= starts[:, None, :]).astype(jnp.int32), axis=2) - 1
    crop_ids = local_crop + 8 * jnp.arange(images, dtype=jnp.int32)[:, None]
    grid_rows = jnp.take_along_axis(crop_sides, local_crop, axis=1)
    place_rows = rows_in[None, :] - jnp.take_along_axis(starts, local_crop, axis=1)
    return (crop_ids.reshape(-1).astype(jnp.int32), grid_rows.reshape(-1).astype(jnp.int32), place_rows.reshape(-1).astype(jnp.int32))


def draw_crop_index(key, part):
    return crop_layout(jax.random.fold_in(key, 11))[0]


def draw_grid_size(key, part):
    return crop_layout(jax.random.fold_in(key, 11))[1]


def draw_position(key, part):
    return crop_layout(jax.random.fold_in(key, 11))[2]


def level_of(stream_key, dims, cuts, low, largest):
    gain = 1.0
    for dim, blocks in cuts:
        draws = jax.random.uniform(jax.random.fold_in(jax.random.fold_in(stream_key, 6), dim), (blocks,), jnp.float32, low / len(cuts), largest / len(cuts))
        gain = gain * jnp.repeat(jnp.exp(draws), dims[dim] // blocks).reshape((-1,) + (1,) * (len(dims) - 1 - dim))
    return gain


def scatter_about(stream_key, dims, scale, limit, cuts=(), held_as=jnp.bfloat16):
    entries = scale * jax.random.normal(stream_key, dims, jnp.float32)
    if cuts:
        entries = entries * level_of(stream_key, dims, cuts, -0.22, 0.18)
    return jnp.clip(entries, -limit, limit).astype(held_as)


def setup_inputs(seed: int = 0) -> dict:
    seeds = jax.random.split(jax.random.key(seed), 17)
    return {
        "features": scatter_about(seeds[0], (TOKENS, D), 1.0, 6.0, ((0, 32),)),
        "crop_index": draw_crop_index(jax.random.fold_in(seeds[16], 71), 0),
        "grid_size": draw_grid_size(jax.random.fold_in(seeds[16], 71), 0),
        "position": draw_position(jax.random.fold_in(seeds[16], 71), 0),
        "cpe_weight": scatter_about(seeds[4], (LAYERS, 9, D), 0.25, 1.5, (), jnp.float32),
        "shared_bias": scatter_about(seeds[5], (LAYERS, 3, D), 0.5, 3.0, (), jnp.float32),
        "norm_gain": jnp.clip(1.0 + 0.18 * jax.random.normal(seeds[6], (LAYERS, 2, D), jnp.float32), 0.1, 1.9),
        "norm_bias": scatter_about(seeds[7], (LAYERS, 2, D), 0.3, 2.0, (), jnp.float32),
        "qkv_weight": scatter_about(seeds[8], (LAYERS, D, 3, D), D ** -0.5, 0.25, ((3, 4),)),
        "head_bias": scatter_about(seeds[9], (LAYERS, 3, D), 0.5, 3.0, ((2, 4),), jnp.float32),
        "crpe_weight": scatter_about(seeds[10], (LAYERS, 49, D), 0.2, 1.2, ((2, 4),), jnp.float32),
        "proj_weight": scatter_about(seeds[11], (LAYERS, D, D), (D // 4) ** -0.5, 0.5, ((1, 4),)),
        "fc1_weight": scatter_about(seeds[12], (LAYERS, D, FF), D ** -0.5, 0.25, ((2, 4),)),
        "fc1_bias": scatter_about(seeds[13], (LAYERS, FF), 0.5, 3.0, ((1, 4),), jnp.float32),
        "fc2_weight": scatter_about(seeds[14], (LAYERS, FF, D), (FF // 2) ** -0.5, 0.1875, ((1, 4),)),
        "out_grad": scatter_about(seeds[15], (TOKENS, D), 1.0, 6.0, ((0, 32),)),
    }


epsilon = 1e-06
highest = lax.Precision.HIGHEST

@jax.custom_vjp
def low(v):
    return lax.optimization_barrier(v.astype(jnp.bfloat16)).astype(jnp.float32)

@jax.custom_vjp
def low_back(v):
    return v

def low_keep(v):
    return (low(v), None)

def low_pass(kept, grad):
    return (grad,)

def back_keep(v):
    return (v, None)

def back_low(kept, grad):
    return (low(grad),)
low.defvjp(low_keep, low_pass)
low_back.defvjp(back_keep, back_low)

def geometry(grid_sizes, positions):
    spatial = positions > 0
    cell_index = jnp.maximum(positions - 1, 0)
    return (spatial, cell_index // grid_sizes, cell_index % grid_sizes, grid_sizes)

def depthwise(source, tap_weights, geo_rows, radius, kernel):
    spatial, row_coord, col_coord, grid_sizes = geo_rows
    accumulated = jnp.zeros_like(source)
    half_width = kernel // 2
    for grid_side in (3, 7):
        max_reach = min(radius, grid_side - 1)
        for delta_row in range(-max_reach, max_reach + 1):
            for delta_col in range(-max_reach, max_reach + 1):
                row_offset = delta_row * grid_side + delta_col
                inside = spatial & (grid_sizes == grid_side)
                inside = inside & (row_coord + delta_row >= 0) & (row_coord + delta_row < grid_side)
                inside = inside & (col_coord + delta_col >= 0) & (col_coord + delta_col < grid_side)
                shifted = jnp.roll(source, -row_offset, axis=0)
                tap_index = (delta_row + half_width) * kernel + delta_col + half_width
                accumulated = accumulated + jnp.where(inside[:, None], shifted, 0.0) * tap_weights[tap_index]
    return accumulated

def window_mask(channel_start, channels):
    head_ids = (channel_start + jnp.arange(channels, dtype=jnp.int32)) // HD
    head_reach = jnp.where(head_ids < 2, 1, jnp.where(head_ids < 5, 2, 3))
    tap_reach = np.array([max(abs(row_tap - 3), abs(col_tap - 3)) for row_tap in range(7) for col_tap in range(7)], dtype=np.int32)
    return (jnp.asarray(tap_reach)[:, None] <= head_reach[None, :]).astype(jnp.float32)

def layer_norm(values, gain_vec, bias_vec):
    center = values - lax.optimization_barrier(jnp.mean(values, axis=-1, keepdims=True))
    spread = lax.optimization_barrier(jnp.mean(center * center, axis=-1, keepdims=True))
    return center * lax.rsqrt(spread + epsilon) * gain_vec + bias_vec

def one_layer(stream, crop_ids, geo_rows, params):
    cpe_weight, shared_bias, norm_gain, norm_bias, qkv_weight, head_bias, crpe_weight, proj_weight, fc1_weight, fc1_bias, fc2_weight = params
    spatial = geo_rows[0]
    conv_pos = depthwise(stream, cpe_weight, geo_rows, 1, 3)
    after_conv = stream + jnp.where(spatial[:, None], conv_pos + shared_bias[0], 0.0)
    normed = low(layer_norm(after_conv, norm_gain[0], norm_bias[0]))
    project = jnp.einsum('rd,dtc->rtc', normed, qkv_weight, precision=highest)
    queries = low(low_back(project[:, 0] + head_bias[0]))
    key_rows = low(low_back(project[:, 1]))
    value_rows = low(low_back(project[:, 2] + head_bias[1]))
    same_crop = (crop_ids[:, None] == crop_ids[None, :]).astype(jnp.float32)
    exponent = jnp.exp(key_rows - lax.optimization_barrier(jnp.max(key_rows, axis=0)))
    denominator = jnp.dot(same_crop, exponent, precision=highest)
    soft_keys = low(low_back(exponent / denominator))
    row_count = stream.shape[0]
    shape_heads = (row_count, HEADS, HD)
    scores = jnp.einsum('rhd,shd->hrs', queries.reshape(shape_heads), soft_keys.reshape(shape_heads), precision=highest)
    mixing = low(low_back(scores * HD ** (-0.5) * same_crop[None]))
    factor = jnp.einsum('hrs,shd->rhd', mixing, value_rows.reshape(shape_heads), precision=highest).reshape(row_count, D)
    crpe_taps = crpe_weight * window_mask(0, D)
    conv_val = depthwise(value_rows, crpe_taps, geo_rows, 3, 7) + head_bias[2]
    relative = jnp.where(spatial[:, None], queries * conv_val, 0.0)
    attended = low(low_back(factor + relative))
    branch = low_back(jnp.dot(attended, proj_weight, precision=highest))
    after_attn = after_conv + branch + shared_bias[1]
    normed_two = low(layer_norm(after_attn, norm_gain[1], norm_bias[1]))
    hidden = low_back(jnp.dot(normed_two, fc1_weight, precision=highest) + fc1_bias)
    active = low(jax.nn.gelu(hidden, approximate=False))
    mlp_out = low_back(jnp.dot(active, fc2_weight, precision=highest))
    return after_attn + mlp_out + shared_bias[2]

def run_layers(stream, crop_ids, grid_sizes, positions, params):
    geo_rows = geometry(grid_sizes, positions)
    for layer_index in range(LAYERS):
        picked = tuple((stacked[layer_index] for stacked in params))
        stream = one_layer(stream, crop_ids, geo_rows, picked)
    return stream

def reference(features, crop_index, grid_size, position, cpe_weight, shared_bias, norm_gain, norm_bias, qkv_weight, head_bias, crpe_weight, proj_weight, fc1_weight, fc1_bias, fc2_weight, out_grad):
    params = tuple((tensor.astype(jnp.float32) for tensor in (cpe_weight, shared_bias, norm_gain, norm_bias, qkv_weight, head_bias, crpe_weight, proj_weight, fc1_weight, fc1_bias, fc2_weight)))
    block_rows = 4 * ROWS_IMG
    groups = TOKENS // block_rows
    inputs = (features.astype(jnp.float32).reshape(groups, block_rows, D), crop_index.reshape(groups, block_rows), grid_size.reshape(groups, block_rows), position.reshape(groups, block_rows), out_grad.astype(jnp.float32).reshape(groups, block_rows, D))

    def step(totals, pieces):
        stream, crops, grids, places, cotangent = pieces

        def forward(weights_in, source):
            return run_layers(source, crops, grids, places, weights_in)
        result, pullback = jax.vjp(forward, params, stream)
        grads, stream_grad = pullback(cotangent)
        return (jax.tree.map(jnp.add, totals, grads), (result.astype(jnp.bfloat16), stream_grad))
    zeros = jax.tree.map(jnp.zeros_like, params)
    totals, (outputs, input_grads) = lax.scan(step, zeros, inputs)
    return (outputs.reshape(TOKENS, D), input_grads.reshape(TOKENS, D), totals[0], totals[1], totals[2], totals[3], totals[4], totals[5], totals[6], totals[7], totals[8], totals[9], totals[10])
```

```python
import functools

import jax
import jax.numpy as jnp
import numpy as np
from jax import lax
from jax.experimental import pallas as pl
from jax.experimental.pallas import tpu as pltpu
from jax.sharding import PartitionSpec as P

HD = 64
LAYERS = 2
ROWS_IMG = 160
CAN = 192
END7 = 112
END3 = 184
LANES = 128
WIDE = 512
BLOCKS = 4
EPSILON = 1e-06
SCALE = HD ** (-0.5)
REACH7 = (1, 2, 3, 3)
REACH3 = (1, 2, 2, 2)
f32 = jnp.float32
bf16 = jnp.bfloat16


def canonical_tables():
    crop = np.full(CAN, 100)
    col = np.full(CAN, -1)
    side = np.zeros(CAN, int)
    for t in range(END7):
        if t % 8 < 7:
            crop[t], col[t], side[t] = t // 56, t % 8, 7
    for t in range(END7, END3):
        u = t - END7
        if t % 4 < 3:
            crop[t], col[t], side[t] = 2 + 2 * (u // 24) + (t % 8) // 4, t % 4, 3
    for t in range(END3, CAN):
        crop[t] = t - END3
    same = (crop[:, None] == crop[None, :]).astype(np.float32)
    moves = np.zeros((7, CAN, CAN), np.float32)
    for b in range(-3, 4):
        for t in range(END3):
            if col[t] >= 0 and 0 <= col[t] + b < side[t]:
                moves[b + 3, t, t + b] = 1
    return same, moves


def tap_table():
    table = np.zeros((BLOCKS, 56, LANES), np.float32)
    for channel in range(WIDE):
        head = channel // HD
        reach = 1 if head < 2 else 2 if head < 5 else 3
        for tap in range(49):
            if max(abs(tap // 7 - 3), abs(tap % 7 - 3)) <= reach:
                table[channel // LANES, tap, channel % LANES] = 1
    return table


def mm(left, right):
    return jnp.dot(left, right, preferred_element_type=f32)


def mm_nt(left, right):
    return lax.dot_general(left, right, (((1,), (1,)), ((), ())), preferred_element_type=f32)


def mm_tn(left, right):
    return lax.dot_general(left, right, (((0,), (0,)), ((), ())), preferred_element_type=f32)


def halves(values):
    high = values.astype(bf16)
    return [high, (values - high.astype(f32)).astype(bf16)]


def lanes_of(block):
    return pl.ds(block * LANES, LANES)


def column_sum(values):
    return jnp.sum(values, axis=0, keepdims=True)


def fill(parts, reach, moves, wide7, wide3):
    for b in range(-reach, reach + 1):
        moved = sum(mm(moves[b + 3], part) for part in parts)
        for grid in range(2):
            wide7[b + 3, grid, 24:80] = moved[grid * 56 : grid * 56 + 56]
        if abs(b) <= 2:
            for pair in range(3):
                first = END7 + pair * 24
                wide3[b + 2, pair, 16:40] = moved[first : first + 24]


def tap_row(a, b, half, flip):
    if flip:
        a, b = -a, -b
    return (a + half) * (2 * half + 1) + b + half


def spread_taps(spread, block, rows):
    for row in range(rows.shape[0]):
        spread[block, row] = jnp.broadcast_to(rows[row : row + 1], (8, LANES))


def convolve(spread, block, reach7, reach3, half, flip, wide7, wide3):
    lanes = lanes_of(block)

    def loop(wide, offset, reach, grids, tall):
        def body(step, acc):
            b = step - reach
            for a in range(-reach, reach + 1):
                weight = spread[block, tap_row(a, b, half, flip)]
                seen = wide[b + offset, :, pl.ds((a + offset) * 8, tall), lanes]
                acc = acc + weight * seen.reshape(-1, 8, LANES)
            return acc

        return lax.fori_loop(0, 2 * reach + 1, body, jnp.zeros((grids * tall // 8, 8, LANES), f32))

    acc7 = loop(wide7, 3, reach7, 2, 56)
    acc3 = loop(wide3, 2, reach3, 3, 24)
    return jnp.concatenate([acc7.reshape(END7, LANES), acc3.reshape(END3 - END7, LANES)], axis=0)


def tap_grads(grad, block, reach7, reach3, half, spread, wide7, wide3):
    lanes = lanes_of(block)
    count = (2 * half + 1) ** 2
    grad7 = grad[:END7].reshape(-1, 8, LANES)
    grad3 = grad[END7:END3].reshape(-1, 8, LANES)
    spread[block, 0:count] = jnp.zeros((count, 8, LANES), f32)

    def loop(wide, offset, reach, part, tall):
        def body(step, carry):
            b = step - reach
            for a in range(-reach, reach + 1):
                seen = wide[b + offset, :, pl.ds((a + offset) * 8, tall), lanes]
                row = tap_row(a, b, half, False)
                spread[block, row] += jnp.sum(part * seen.reshape(-1, 8, LANES), axis=0)
            return carry

        lax.fori_loop(0, 2 * reach + 1, body, 0)

    loop(wide7, 3, reach7, grad7, 56)
    loop(wide3, 2, reach3, grad3, 24)
    return jnp.sum(spread[block, 0:count], axis=1)


def norm_forward(values, gain, bias):
    center = values - jnp.mean(values, axis=-1, keepdims=True)
    spread = jnp.mean(center * center, axis=-1, keepdims=True)
    inverse = lax.rsqrt(spread + EPSILON)
    unit = center * inverse
    return unit, inverse, (unit * gain + bias).astype(bf16)


def norm_backward(incoming, unit, inverse, gain):
    scaled = incoming * gain
    mean_one = jnp.mean(scaled, axis=-1, keepdims=True)
    mean_two = jnp.mean(scaled * unit, axis=-1, keepdims=True)
    return inverse * (scaled - mean_one - unit * mean_two)


def real_rows():
    row = lax.broadcasted_iota(jnp.int32, (CAN, LANES), 0)
    seven = (row < END7) & ((row & 7) != 7)
    three = (row >= END7) & (row < END3) & ((row & 3) != 3)
    return seven | three | (row >= END3)


def head_lanes(head):
    lane = lax.broadcasted_iota(jnp.int32, (CAN, LANES), 1)
    return (lane >= HD) if head else (lane < HD)


def step_kernel(
    tgt_row, tgt_col, feats, ograd, same, moves, tap_mask, wqkv, wproj, wfc1, wfc2, small, shared,
    out, fgrad, gqkv, gproj, gfc1, gfc2, gsmall, gshared,
    streams, unit1, inv1, normed1, queries, softs, exacts, values, convs, attended, unit2, inv2, normed2, active, slope,
    taps, wide7, wide3, work, grads, rel, gatt,
):
    wide7[...] = jnp.zeros_like(wide7)
    wide3[...] = jnp.zeros_like(wide3)
    place = (lax.broadcasted_iota(jnp.int32, (CAN, ROWS_IMG), 0) == tgt_row[0:1, :]).astype(f32).astype(bf16)
    streams[0] = mm(place, feats[...])
    grads[...] = mm(place, ograd[...])
    real = real_rows()
    for layer in range(LAYERS):
        forward(
            layer, real, same, moves, tap_mask, wqkv, wproj, wfc1, wfc2, small, shared, streams, unit1, inv1, normed1,
            queries, softs, exacts, values, convs, attended, unit2, inv2, normed2, active, slope, taps, wide7, wide3, work,
        )
    back = (
        lax.broadcasted_iota(jnp.int32, (ROWS_IMG, CAN), 1) == tgt_col[:, 0:1]
    ).astype(f32).astype(bf16)
    out[...] = mm(back, streams[LAYERS].astype(bf16)).astype(bf16)
    for layer in reversed(range(LAYERS)):
        backward(
            layer, same, moves, tap_mask, wqkv, wproj, wfc1, wfc2, small, shared, streams, unit1, inv1, normed1,
            queries, softs, exacts, values, convs, attended, unit2, inv2, normed2, active, slope, taps, wide7, wide3, work,
            grads, rel, gatt, gqkv, gproj, gfc1, gfc2, gsmall, gshared,
        )
    fgrad[...] = sum(mm(back, part) for part in halves(grads[...]))


def forward(
    layer, real, same, moves, tap_mask, wqkv, wproj, wfc1, wfc2, small, shared, streams, unit1, inv1, normed1,
    queries, softs, exacts, values, convs, attended, unit2, inv2, normed2, active, slope, taps, wide7, wide3, work,
):
    stream = streams[layer]
    fill(halves(stream), 1, moves, wide7, wide3)
    for block in range(BLOCKS):
        lanes = lanes_of(block)
        spread_taps(taps, block, shared[layer, 0:9, lanes])
        conv = convolve(taps, block, 1, 1, 1, False, wide7, wide3)
        work[0:END3, lanes] = streams[layer, 0:END3, lanes] + conv + shared[layer, 9:10, lanes]
        work[END3:CAN, lanes] = streams[layer, END3:CAN, lanes]
    unit, inverse, normed = norm_forward(work[...], shared[layer, 12:13], shared[layer, 14:15])
    unit1[layer] = unit
    inv1[layer] = inverse
    normed1[layer] = normed
    for block in range(BLOCKS):
        lanes = lanes_of(block)
        project = mm(normed, wqkv[block, layer])
        queries[layer, :, lanes] = (project[:, :LANES] + small[block, layer, 49:50]).astype(bf16)
        values[layer, :, lanes] = (project[:, 2 * LANES :] + small[block, layer, 50:51]).astype(bf16)
        keys = project[:, LANES : 2 * LANES].astype(bf16).astype(f32)
        largest = jnp.max(jnp.where(real, keys, -1e30), axis=0, keepdims=True)
        exponent = jnp.exp(jnp.where(real, keys - largest, 0.0))
        exact = exponent / sum(mm(same[...], part) for part in halves(exponent))
        exacts[layer, :, lanes] = exact
        softs[layer, :, lanes] = exact.astype(bf16)
        spread_taps(taps, block, small[block, layer, 0:49] * tap_mask[block, 0:49])
    fill([values[layer]], 3, moves, wide7, wide3)
    for block in range(BLOCKS):
        lanes = lanes_of(block)
        query = queries[layer, :, lanes]
        soft = softs[layer, :, lanes]
        value = values[layer, :, lanes]
        factors = []
        for head in range(2):
            masked = jnp.where(head_lanes(head), query, jnp.zeros_like(query))
            mixing = (mm_nt(masked, soft) * SCALE * same[...].astype(f32)).astype(bf16)
            factors.append(mm(mixing, value))
        factor = jnp.where(head_lanes(0), factors[0], factors[1])
        conv = convolve(taps, block, REACH7[block], REACH3[block], 3, False, wide7, wide3) + small[block, layer, 51:52]
        convs[layer, 0:END3, lanes] = conv
        attended[layer, 0:END3, lanes] = (factor[0:END3] + query[0:END3].astype(f32) * conv).astype(bf16)
        attended[layer, END3:CAN, lanes] = factor[END3:CAN].astype(bf16)
    after = work[...] + mm(attended[layer], wproj[:, layer].reshape(WIDE, WIDE)) + shared[layer, 10:11]
    unit, inverse, normed = norm_forward(after, shared[layer, 13:14], shared[layer, 15:16])
    unit2[layer] = unit
    inv2[layer] = inverse
    normed2[layer] = normed
    work[...] = after + shared[layer, 11:12]

    def feed(block, carry):
        hidden = mm(normed2[layer], wfc1[block, layer]) + jnp.concatenate(
            [small[block, layer, 52 + part : 53 + part] for part in range(4)], axis=1
        )
        chance = 0.5 * (1.0 + lax.erf(hidden * np.float32(0.5**0.5)))
        density = jnp.exp(hidden * hidden * -0.5) * np.float32((2 * np.pi) ** -0.5)
        slope[layer, block] = chance + hidden * density
        act = (hidden * chance).astype(bf16)
        active[layer, block] = act
        work[...] += mm(act, wfc2[block, layer])
        return carry

    lax.fori_loop(0, BLOCKS, feed, 0)
    streams[layer + 1] = work[...]


def backward(
    layer, same, moves, tap_mask, wqkv, wproj, wfc1, wfc2, small, shared, streams, unit1, inv1, normed1,
    queries, softs, exacts, values, convs, attended, unit2, inv2, normed2, active, slope, taps, wide7, wide3, work,
    grads, rel, gatt, gqkv, gproj, gfc1, gfc2, gsmall, gshared,
):
    low = grads[...].astype(bf16)
    gshared[layer, 11:12] = column_sum(grads[...])
    work[...] = jnp.zeros_like(work)

    def feed(block, carry):
        grad_low = grads[...].astype(bf16)
        gfc2[block, layer] = mm_tn(active[layer, block], grad_low).astype(bf16)
        hidden = (mm_nt(grad_low, wfc2[block, layer]) * slope[layer, block]).astype(bf16)
        gfc1[block, layer] = mm_tn(normed2[layer], hidden).astype(bf16)
        sums = column_sum(hidden.astype(f32))
        for part in range(4):
            gsmall[block, layer, 52 + part : 53 + part] = sums[:, part * LANES : (part + 1) * LANES]
        work[...] += mm_nt(hidden, wfc1[block, layer])
        return carry

    lax.fori_loop(0, BLOCKS, feed, 0)
    incoming = work[...]
    unit = unit2[layer]
    gshared[layer, 13:14] = column_sum(incoming * unit)
    gshared[layer, 15:16] = column_sum(incoming)
    grads[...] = grads[...] + norm_backward(incoming, unit, inv2[layer], shared[layer, 13:14])
    branch = grads[...]
    gshared[layer, 10:11] = column_sum(branch)
    branch = branch.astype(bf16)
    gproj[:, layer] = mm_tn(attended[layer], branch).astype(bf16).reshape(BLOCKS, LANES, WIDE)
    gatt[...] = mm_nt(branch, wproj[:, layer].reshape(WIDE, WIDE)).astype(bf16)
    fill([values[layer]], 3, moves, wide7, wide3)
    for block in range(BLOCKS):
        lanes = lanes_of(block)
        product = gatt[0:END3, lanes].astype(f32) * queries[layer, 0:END3, lanes].astype(f32)
        rel[0:END3, lanes] = product.astype(bf16)
        rel[END3:CAN, lanes] = jnp.zeros((CAN - END3, LANES), bf16)
        gsmall[block, layer, 51:52] = column_sum(product)
        sums = tap_grads(product, block, REACH7[block], REACH3[block], 3, taps, wide7, wide3)
        gsmall[block, layer, 0:49] = sums * tap_mask[block, 0:49]
        spread_taps(taps, block, small[block, layer, 0:49] * tap_mask[block, 0:49])
    fill([rel[...]], 3, moves, wide7, wide3)
    work[...] = jnp.zeros_like(work)
    for block in range(BLOCKS):
        lanes = lanes_of(block)
        query = queries[layer, :, lanes]
        soft = softs[layer, :, lanes]
        value = values[layer, :, lanes]
        grad = gatt[:, lanes]
        exact = exacts[layer, :, lanes]
        picked = []
        for head in range(2):
            chosen = head_lanes(head)
            zero = jnp.zeros_like(query)
            query_head = jnp.where(chosen, query, zero)
            grad_head = jnp.where(chosen, grad, zero)
            same_low = same[...]
            mixing_t = (mm_nt(soft, query_head) * SCALE * same_low.astype(f32)).astype(bf16)
            mix = mm_nt(grad_head, value).astype(bf16) * same_low
            mix_t = mm_nt(value, grad_head).astype(bf16) * same_low
            picked.append((mm(mixing_t, grad), SCALE * mm(mix, soft), SCALE * mm(mix_t, query)))
        grad_value, grad_query, grad_soft = (
            jnp.where(head_lanes(0), one, two) for one, two in zip(*picked)
        )
        grad_soft = grad_soft.astype(bf16).astype(f32)
        weighted = grad_soft * exact
        grad_key = weighted - exact * sum(mm(same[...], part) for part in halves(weighted))
        conv = convolve(taps, block, REACH7[block], REACH3[block], 3, True, wide7, wide3)
        grad_value = jnp.concatenate([grad_value[0:END3] + conv, grad_value[END3:CAN]], axis=0).astype(bf16)
        grad_query = jnp.concatenate(
            [grad_query[0:END3] + grad[0:END3].astype(f32) * convs[layer, 0:END3, lanes], grad_query[END3:CAN]], axis=0
        ).astype(bf16)
        gsmall[block, layer, 49:50] = column_sum(grad_query.astype(f32))
        gsmall[block, layer, 50:51] = column_sum(grad_value.astype(f32))
        joined = jnp.concatenate([grad_query, grad_key.astype(bf16), grad_value], axis=1)
        gqkv[block, layer] = mm_tn(normed1[layer], joined).astype(bf16)
        work[...] += mm_nt(joined, wqkv[block, layer])
    incoming = work[...]
    unit = unit1[layer]
    gshared[layer, 12:13] = column_sum(incoming * unit)
    gshared[layer, 14:15] = column_sum(incoming)
    grads[...] = grads[...] + norm_backward(incoming, unit, inv1[layer], shared[layer, 12:13])
    fill(halves(streams[layer]), 1, moves, wide7, wide3)
    for block in range(BLOCKS):
        lanes = lanes_of(block)
        product = grads[0:END3, lanes]
        gshared[layer, 9:10, lanes] = column_sum(product)
        gshared[layer, 0:9, lanes] = tap_grads(product, block, 1, 1, 1, taps, wide7, wide3)
    fill(halves(grads[...]), 1, moves, wide7, wide3)
    for block in range(BLOCKS):
        lanes = lanes_of(block)
        spread_taps(taps, block, shared[layer, 0:9, lanes])
        conv = convolve(taps, block, 1, 1, 1, True, wide7, wide3)
        grads[0:END3, lanes] = grads[0:END3, lanes] + conv


def canonical_targets(crops, sides, places):
    crops = crops % 8
    first = places == 0
    earlier = first[None, :] & (crops[None, :] < crops[:, None])
    seven = jnp.sum((earlier & (sides == 7)[None, :]).astype(jnp.int32), axis=1)
    three = jnp.sum((earlier & (sides == 3)[None, :]).astype(jnp.int32), axis=1)
    cell = jnp.maximum(places - 1, 0)
    row, col = cell // sides, cell % sides
    in_seven = seven * 56 + row * 8 + col
    in_three = END7 + (three // 2) * 24 + row * 8 + (three % 2) * 4 + col
    big = sides == 7
    return jnp.where(first, END3 + jnp.where(big, seven, 2 + three), jnp.where(big, in_seven, in_three))


def shards(
    features, crop_index, grid_size, position, cpe_weight, shared_bias, norm_gain, norm_bias,
    qkv_weight, head_bias, crpe_weight, proj_weight, fc1_weight, fc1_bias, fc2_weight, out_grad,
):
    start = lax.axis_index("mp") * ROWS_IMG
    mine = [lax.dynamic_slice_in_dim(item, start, ROWS_IMG) for item in (crop_index, grid_size, position)]
    target = canonical_targets(*mine)
    tgt_row = jnp.broadcast_to(target[None, :], (8, ROWS_IMG))
    tgt_col = jnp.broadcast_to(target[:, None], (ROWS_IMG, LANES))
    same, moves = canonical_tables()
    small = jnp.concatenate([crpe_weight, head_bias, fc1_bias.reshape(LAYERS, 4, LANES)], axis=1)
    shared = jnp.concatenate([cpe_weight, shared_bias, norm_gain, norm_bias], axis=1)
    gathered = [
        lax.all_gather(item, "mp", axis=0)
        for item in (qkv_weight.reshape(LAYERS, WIDE, 3 * LANES), proj_weight, fc1_weight, fc2_weight, small)
    ]
    vmem = pl.BlockSpec(memory_space=pltpu.VMEM)
    shape = jax.ShapeDtypeStruct
    rows = lambda kind: pltpu.VMEM((LAYERS, CAN, WIDE), kind)
    out, fgrad, gqkv, gproj, gfc1, gfc2, gsmall, gshared = pl.pallas_call(
        step_kernel,
        out_shape=(
            shape((ROWS_IMG, WIDE), bf16),
            shape((ROWS_IMG, WIDE), f32),
            shape((BLOCKS, LAYERS, WIDE, 3 * LANES), bf16),
            shape((BLOCKS, LAYERS, LANES, WIDE), bf16),
            shape((BLOCKS, LAYERS, WIDE, WIDE), bf16),
            shape((BLOCKS, LAYERS, WIDE, WIDE), bf16),
            shape((BLOCKS, LAYERS, 56, LANES), f32),
            shape((LAYERS, 16, WIDE), f32),
        ),
        in_specs=[vmem] * 13,
        out_specs=(vmem,) * 8,
        scratch_shapes=[
            pltpu.VMEM((LAYERS + 1, CAN, WIDE), f32),
            rows(f32),
            pltpu.VMEM((LAYERS, CAN, 1), f32),
            rows(bf16),
            rows(bf16),
            rows(bf16),
            rows(f32),
            rows(bf16),
            rows(f32),
            rows(bf16),
            rows(f32),
            pltpu.VMEM((LAYERS, CAN, 1), f32),
            rows(bf16),
            pltpu.VMEM((LAYERS, BLOCKS, CAN, WIDE), bf16),
            pltpu.VMEM((LAYERS, BLOCKS, CAN, WIDE), f32),
            pltpu.VMEM((BLOCKS, 49, 8, LANES), f32),
            pltpu.VMEM((7, 2, 104, WIDE), f32),
            pltpu.VMEM((5, 3, 56, WIDE), f32),
            pltpu.VMEM((CAN, WIDE), f32),
            pltpu.VMEM((CAN, WIDE), f32),
            pltpu.VMEM((CAN, WIDE), bf16),
            pltpu.VMEM((CAN, WIDE), bf16),
        ],
        compiler_params=pltpu.CompilerParams(vmem_limit_bytes=60 * 2**20),
        name="step",
    )(
        tgt_row, tgt_col, features, out_grad,
        jnp.asarray(same, bf16), jnp.asarray(moves, bf16), jnp.asarray(tap_table()), *gathered, shared,
    )
    reduced = [
        lax.psum(lax.psum_scatter(item, "mp", scatter_dimension=0, tiled=False), "dp").astype(f32)
        for item in (gqkv, gproj, gfc1, gfc2)
    ]
    small_sum = lax.psum(lax.psum_scatter(gsmall, "mp", scatter_dimension=0, tiled=False), "dp")
    shared_sum = lax.psum(gshared, ("dp", "mp"))
    return (
        out,
        fgrad,
        shared_sum[:, 0:9],
        shared_sum[:, 9:12],
        shared_sum[:, 12:14],
        shared_sum[:, 14:16],
        reduced[0].reshape(LAYERS, WIDE, 3, LANES),
        small_sum[:, 49:52],
        small_sum[:, 0:49],
        reduced[1],
        reduced[2],
        small_sum[:, 52:56].reshape(LAYERS, WIDE),
        reduced[3],
    )


def solution(mesh):
    placed = (
        P(("dp", "mp"), None),
        P("dp"),
        P("dp"),
        P("dp"),
        P(),
        P(),
        P(),
        P(),
        P(None, None, None, "mp"),
        P(None, None, "mp"),
        P(None, None, "mp"),
        P(None, "mp", None),
        P(None, None, "mp"),
        P(None, "mp"),
        P(None, "mp", None),
        P(("dp", "mp"), None),
    )
    return jax.shard_map(
        shards,
        mesh=mesh,
        in_specs=placed,
        out_specs=(
            P(("dp", "mp"), None),
            P(("dp", "mp"), None),
            P(),
            P(),
            P(),
            P(),
            P(None, None, None, "mp"),
            P(None, None, "mp"),
            P(None, None, "mp"),
            P(None, "mp", None),
            P(None, None, "mp"),
            P(None, "mp"),
            P(None, "mp", None),
        ),
        check_vma=False,
    )
```

```python
import functools

import jax
import jax.numpy as jnp
import numpy as np
from jax import lax
from jax.experimental import pallas as pl
from jax.experimental.pallas import tpu as pltpu
from jax.sharding import PartitionSpec as P

HD = 64
LAYERS = 2
ROWS_IMG = 160
CAN = 192
END7 = 112
END3 = 184
LANES = 128
WIDE = 512
BLOCKS = 4
EPSILON = 1e-06
SCALE = HD ** (-0.5)
REACH7 = (1, 2, 3, 3)
REACH3 = (1, 2, 2, 2)
MESH = pl.DeviceIdType.MESH
f32 = jnp.float32
bf16 = jnp.bfloat16


def canonical_tables():
    crop = np.full(CAN, 100)
    col = np.full(CAN, -1)
    side = np.zeros(CAN, int)
    for t in range(END7):
        if t % 8 < 7:
            crop[t], col[t], side[t] = t // 56, t % 8, 7
    for t in range(END7, END3):
        u = t - END7
        if t % 4 < 3:
            crop[t], col[t], side[t] = 2 + 2 * (u // 24) + (t % 8) // 4, t % 4, 3
    for t in range(END3, CAN):
        crop[t] = t - END3
    same = (crop[:, None] == crop[None, :]).astype(np.float32)
    moves = np.zeros((7, CAN, CAN), np.float32)
    for b in range(-3, 4):
        for t in range(END3):
            if col[t] >= 0 and 0 <= col[t] + b < side[t]:
                moves[b + 3, t, t + b] = 1
    return same, moves


def tap_table():
    table = np.zeros((BLOCKS, 56, LANES), np.float32)
    for channel in range(WIDE):
        head = channel // HD
        reach = 1 if head < 2 else 2 if head < 5 else 3
        for tap in range(49):
            if max(abs(tap // 7 - 3), abs(tap % 7 - 3)) <= reach:
                table[channel // LANES, tap, channel % LANES] = 1
    return table


def mm(left, right):
    return jnp.dot(left, right, preferred_element_type=f32)


def mm_nt(left, right):
    return lax.dot_general(left, right, (((1,), (1,)), ((), ())), preferred_element_type=f32)


def mm_tn(left, right):
    return lax.dot_general(left, right, (((0,), (0,)), ((), ())), preferred_element_type=f32)


def halves(values):
    high = values.astype(bf16)
    return [high, (values - high.astype(f32)).astype(bf16)]


def lanes_of(block):
    return pl.ds(block * LANES, LANES)


def column_sum(values):
    return jnp.sum(values, axis=0, keepdims=True)


def fill(parts, reach, moves, wide7, wide3):
    for b in range(-reach, reach + 1):
        moved = sum(mm(moves[b + 3], part) for part in parts)
        for grid in range(2):
            wide7[b + 3, grid, 24:80] = moved[grid * 56 : grid * 56 + 56]
        if abs(b) <= 2:
            for pair in range(3):
                first = END7 + pair * 24
                wide3[b + 2, pair, 16:40] = moved[first : first + 24]


def tap_row(a, b, half, flip):
    if flip:
        a, b = -a, -b
    return (a + half) * (2 * half + 1) + b + half


def spread_taps(spread, block, rows):
    for row in range(rows.shape[0]):
        spread[block, row] = jnp.broadcast_to(rows[row : row + 1], (8, LANES))


def convolve(spread, block, reach7, reach3, half, flip, wide7, wide3):
    lanes = lanes_of(block)

    def loop(wide, offset, reach, grids, tall):
        def body(step, acc):
            b = step - reach
            for a in range(-reach, reach + 1):
                weight = spread[block, tap_row(a, b, half, flip)]
                seen = wide[b + offset, :, pl.ds((a + offset) * 8, tall), lanes]
                acc = acc + weight * seen.reshape(-1, 8, LANES)
            return acc

        return lax.fori_loop(0, 2 * reach + 1, body, jnp.zeros((grids * tall // 8, 8, LANES), f32))

    acc7 = loop(wide7, 3, reach7, 2, 56)
    acc3 = loop(wide3, 2, reach3, 3, 24)
    return jnp.concatenate([acc7.reshape(END7, LANES), acc3.reshape(END3 - END7, LANES)], axis=0)


def tap_grads(grad, block, reach7, reach3, half, spread, wide7, wide3):
    lanes = lanes_of(block)
    count = (2 * half + 1) ** 2
    grad7 = grad[:END7].reshape(-1, 8, LANES)
    grad3 = grad[END7:END3].reshape(-1, 8, LANES)
    spread[block, 0:count] = jnp.zeros((count, 8, LANES), f32)

    def loop(wide, offset, reach, part, tall):
        def body(step, carry):
            b = step - reach
            for a in range(-reach, reach + 1):
                seen = wide[b + offset, :, pl.ds((a + offset) * 8, tall), lanes]
                row = tap_row(a, b, half, False)
                spread[block, row] += jnp.sum(part * seen.reshape(-1, 8, LANES), axis=0)
            return carry

        lax.fori_loop(0, 2 * reach + 1, body, 0)

    loop(wide7, 3, reach7, grad7, 56)
    loop(wide3, 2, reach3, grad3, 24)
    return jnp.sum(spread[block, 0:count], axis=1)


def norm_forward(values, gain, bias):
    center = values - jnp.mean(values, axis=-1, keepdims=True)
    spread = jnp.mean(center * center, axis=-1, keepdims=True)
    inverse = lax.rsqrt(spread + EPSILON)
    unit = center * inverse
    return unit, inverse, (unit * gain + bias).astype(bf16)


def norm_backward(incoming, unit, inverse, gain):
    scaled = incoming * gain
    mean_one = jnp.mean(scaled, axis=-1, keepdims=True)
    mean_two = jnp.mean(scaled * unit, axis=-1, keepdims=True)
    return inverse * (scaled - mean_one - unit * mean_two)


def real_rows():
    row = lax.broadcasted_iota(jnp.int32, (CAN, LANES), 0)
    seven = (row < END7) & ((row & 7) != 7)
    three = (row >= END7) & (row < END3) & ((row & 3) != 3)
    return seven | three | (row >= END3)


def head_lanes(head):
    lane = lax.broadcasted_iota(jnp.int32, (CAN, LANES), 1)
    return (lane >= HD) if head else (lane < HD)


def rows_of(ref, start, count):
    return ref.at[pl.ds(pl.multiple_of(start, 8), count)]


def add_rows(target, start, source, first, count):
    step = next(size for size in (64, 48, 32, 24, 16, 8) if count % size == 0)

    def body(index, carry):
        into = pl.ds(pl.multiple_of(start + index * step, 8), step)
        target[into] = target[into] + source[pl.ds(pl.multiple_of(first + index * step, 8), step)]
        return carry

    lax.fori_loop(0, count // step, body, 0)


class Links:
    def __init__(self, many):
        dp, mp = lax.axis_index("dp"), lax.axis_index("mp")
        self.many = many
        self.core, self.side = lax.rem(mp, 2), lax.div(mp, 2)
        self.half, self.quad, self.group = lax.rem(dp, 2), lax.rem(lax.div(dp, 2), 4), lax.div(dp, 8)
        self.block = mp
        self.block_core = self.side * 2 + 1 - self.core
        self.block_side = (1 - self.side) * 2 + self.core
        self.block_far = (1 - self.side) * 2 + 1 - self.core
        self.by_core = (dp, self.block_core)
        self.by_side = (dp, self.block_side)
        self.by_far = (dp, self.block_far)
        self.by_half = (dp + 1 - 2 * self.half, mp)
        self.by_quad = [
            (self.group * 8 + lax.rem(self.quad + step, 4) * 2 + self.half, mp) for step in range(1, 4)
        ]
        self.by_group = [
            (lax.rem(self.group + step, many) * 8 + self.quad * 2 + self.half, mp) for step in range(1, many)
        ]
        self.sent = []

    def meet(self):
        barrier = pltpu.get_barrier_semaphore()
        others = [self.by_core, self.by_side, self.by_far, self.by_half] + self.by_quad + self.by_group
        for other in others:
            pl.semaphore_signal(barrier, inc=1, device_id=other, device_id_type=MESH)
        pl.semaphore_wait(barrier, len(others))

    def send(self, source, target, send_sem, recv_sem, other):
        copy = pltpu.make_async_remote_copy(
            src_ref=source, dst_ref=target, send_sem=send_sem, recv_sem=recv_sem, device_id=other, device_id_type=MESH
        )
        copy.start()
        self.sent.append(copy)

    def arrived(self, target, send_sem, recv_sem):
        pltpu.make_async_remote_copy(
            src_ref=target, dst_ref=target, send_sem=send_sem, recv_sem=recv_sem, device_id=self.by_core,
            device_id_type=MESH,
        ).wait_recv()

    def finish(self):
        for copy in self.sent:
            copy.wait_send()


class Weights:
    def __init__(self, links, local, full, send_sems, recv_sems, own_sem, split=True):
        self.links, self.local, self.full = links, local, full
        self.send_sems, self.recv_sems, self.own_sem, self.split = send_sems, recv_sems, own_sem, split
        self.count = local.shape[0] // 2 if split else local.shape[0]
        self.here = links.half * self.count if split else 0
        self.there = (1 - links.half) * self.count

    def part(self, block, start):
        return rows_of(self.full(block), start, self.count)

    def start(self):
        links = self.links
        part = rows_of(self.local, self.here, self.count)
        links.send(part, self.part(links.block, self.here), self.send_sems.at[0], self.recv_sems.at[0], links.by_side)
        links.send(self.local, self.full(links.block), self.send_sems.at[1], self.recv_sems.at[1], links.by_core)
        self.own = pltpu.make_async_copy(self.local, self.full(links.block), self.own_sem)
        self.own.start()

    def pass_first(self):
        links = self.links
        part = self.part(links.block_side, self.here)
        links.arrived(part, self.send_sems.at[0], self.recv_sems.at[0])
        if self.split:
            links.send(part, part, self.send_sems.at[2], self.recv_sems.at[2], links.by_half)
        links.send(part, part, self.send_sems.at[3], self.recv_sems.at[3], links.by_core)

    def pass_second(self):
        links = self.links
        part = self.part(links.block_side, self.there)
        links.arrived(part, self.send_sems.at[2], self.recv_sems.at[2])
        links.send(part, part, self.send_sems.at[4], self.recv_sems.at[4], links.by_core)

    def wait(self):
        links = self.links
        self.own.wait()
        links.arrived(self.full(links.block_core), self.send_sems.at[1], self.recv_sems.at[1])
        links.arrived(self.part(links.block_far, self.here), self.send_sems.at[3], self.recv_sems.at[3])
        if self.split:
            links.arrived(self.part(links.block_far, self.there), self.send_sems.at[4], self.recv_sems.at[4])


class Gradient:
    def __init__(self, links, full, core_in, side_in, half_in, quad_in, group_in, result, send_sems, recv_sems):
        self.links, self.full, self.result = links, full, result
        self.core_in, self.side_in, self.half_in, self.quad_in, self.group_in = core_in, side_in, half_in, quad_in, group_in
        self.send_sems, self.recv_sems = send_sems, recv_sems
        self.tall = result.shape[0]
        self.half, self.piece = self.tall // 2, self.tall // 8
        self.here, self.there = links.half * self.half, (1 - links.half) * self.half
        self.mine = self.here + links.quad * self.piece

    def CS(self):
        links = self.links
        for place, side in ((0, 1 - links.side), (1, links.side)):
            links.send(
                self.full(side * 2 + 1 - links.core), self.core_in.at[place], self.send_sems.at[place],
                self.recv_sems.at[place], links.by_core,
            )

    def CX(self):
        links = self.links
        links.arrived(self.core_in.at[0], self.send_sems.at[0], self.recv_sems.at[0])
        part = self.full(links.block_side)
        add_rows(part, 0, self.core_in.at[0], 0, self.tall)
        links.send(part, self.side_in, self.send_sems.at[2], self.recv_sems.at[2], links.by_side)

    def CO(self):
        links = self.links
        links.arrived(self.core_in.at[1], self.send_sems.at[1], self.recv_sems.at[1])
        add_rows(self.full(links.block), 0, self.core_in.at[1], 0, self.tall)

    def XA(self):
        links = self.links
        links.arrived(self.side_in, self.send_sems.at[2], self.recv_sems.at[2])
        total = self.full(links.block)
        add_rows(total, self.there, self.side_in, self.there, self.half)
        links.send(
            rows_of(total, self.there, self.half), self.half_in, self.send_sems.at[3], self.recv_sems.at[3], links.by_half
        )
        add_rows(total, self.here, self.side_in, self.here, self.half)

    def YA(self):
        links = self.links
        links.arrived(self.half_in, self.send_sems.at[3], self.recv_sems.at[3])
        total = self.full(links.block)
        add_rows(total, self.here, self.half_in, 0, self.half)
        for step in range(3):
            start = self.here + lax.rem(links.quad + step + 1, 4) * self.piece
            links.send(
                rows_of(total, start, self.piece), self.quad_in.at[step], self.send_sems.at[4 + step],
                self.recv_sems.at[4 + step], links.by_quad[step],
            )

    def ZA(self):
        links = self.links
        mine = pl.ds(pl.multiple_of(self.mine, 8), self.piece)
        total = self.full(links.block)
        for step in range(3):
            links.arrived(self.quad_in.at[step], self.send_sems.at[4 + step], self.recv_sems.at[4 + step])
        value = total[mine].astype(f32)
        for step in range(3):
            value = value + self.quad_in[step].astype(f32)
        if links.many > 1:
            total[mine] = value.astype(total.dtype)
            for step in range(links.many - 1):
                links.send(
                    total.at[mine], self.group_in.at[step], self.send_sems.at[16 + step], self.recv_sems.at[16 + step],
                    links.by_group[step],
                )
            value = total[mine].astype(f32)
            for step in range(links.many - 1):
                links.arrived(self.group_in.at[step], self.send_sems.at[16 + step], self.recv_sems.at[16 + step])
                value = value + self.group_in[step].astype(f32)
        self.result[mine] = value.astype(self.result.dtype)
        for step in range(3):
            links.send(
                self.result.at[mine], self.result.at[mine], self.send_sems.at[7 + step], self.recv_sems.at[7 + step],
                links.by_quad[step],
            )

    def ZF(self):
        links = self.links
        for step in range(3):
            start = self.here + lax.rem(links.quad + 3 - step, 4) * self.piece
            links.arrived(
                rows_of(self.result, start, self.piece), self.send_sems.at[7 + step], self.recv_sems.at[7 + step]
            )
        part = rows_of(self.result, self.here, self.half)
        links.send(part, part, self.send_sems.at[10], self.recv_sems.at[10], links.by_half)

    def FN(self):
        self.links.arrived(
            rows_of(self.result, self.there, self.half), self.send_sems.at[10], self.recv_sems.at[10]
        )


ORDER = (
    (
        "CS.fc2.1",
    ),
    (
        "CS.fc1.1", "CX.fc2.1",
    ),
    (
        "CS.proj.1", "CO.fc2.1", "CX.fc1.1",
    ),
    (
        "CO.fc1.1", "CX.proj.1", "CO.proj.1",
    ),
    (
        "CS.qkv.1",
    ),
    (
        "CX.qkv.1", "CO.qkv.1", "XA.fc2.1",
    ),
    (
        "CS.fc2.0",
    ),
    (
        "CS.fc1.0", "CX.fc2.0",
    ),
    (
        "CS.proj.0", "CO.fc2.0", "CX.fc1.0", "YA.fc2.1",
    ),
    (
        "CO.fc1.0", "CX.proj.0", "CO.proj.0", "XA.fc1.1", "XA.proj.1",
    ),
    (
        "CS.qkv.0", "ZA.fc2.1",
    ),
    (
        "CS.rest.0", "CX.qkv.0", "CO.qkv.0", "YA.fc1.1", "XA.qkv.1", "YA.proj.1",
    ),
    (
        "CX.rest.0", "CO.rest.0", "ZF.fc2.1", "YA.qkv.1", "ZA.fc1.1", "XA.fc2.0",
        "ZA.proj.1", "FN.fc2.1", "ZA.qkv.1", "YA.fc2.0", "ZF.fc1.1", "XA.fc1.0",
        "ZF.proj.1", "XA.proj.0", "ZF.qkv.1", "FN.fc1.1", "ZA.fc2.0", "XA.qkv.0",
        "YA.fc1.0", "XA.rest.0", "FN.proj.1", "YA.proj.0", "ZF.fc2.0", "FN.qkv.1",
        "YA.qkv.0", "ZA.fc1.0", "YA.rest.0", "ZA.proj.0", "ZA.qkv.0", "FN.fc2.0",
        "ZF.fc1.0", "ZA.rest.0", "ZF.proj.0", "ZF.qkv.0", "FN.fc1.0", "ZF.rest.0",
        "FN.proj.0", "FN.qkv.0", "FN.rest.0",
    ),
)
KINDS = ("qkv", "proj", "fc1", "fc2")
REST = 192
FIRST_SHARED = 112


def step_kernel(
    many,
    tgt_row, tgt_col, feats, ograd, same, moves, tap_mask, lqkv, lproj, lfc1, lfc2, lsmall, shared,
    out, fgrad, rqkv, rproj, rfc1, rfc2, rrest, rshared,
    wqkv, wproj, wfc1, wfc2, small, gqkv, gproj, gfc1, gfc2, grest,
    cqkv, cproj, cfc1, cfc2, crest, xqkv, xproj, xfc1, xfc2, xrest, yqkv, yproj, yfc1, yfc2, yrest,
    zqkv, zproj, zfc1, zfc2, zrest, eqkv, eproj, efc1, efc2, erest,
    streams, unit1, inv1, normed1, queries, softs, exacts, values, convs, attended, unit2, inv2, normed2, active, slope,
    taps, wide7, wide3, work, grads, rel, gatt,
    weight_send, weight_recv, weight_own, grad_send, grad_recv, last_send, last_recv,
):
    links = Links(many)
    links.meet()
    weights = {}
    for place, (kind, local, full) in enumerate(
        zip(KINDS, (lqkv, lproj, lfc1, lfc2), (wqkv, wproj, wfc1, wfc2))
    ):
        for layer in range(LAYERS):
            slot = place * LAYERS + layer
            weights[kind, layer] = Weights(
                links, local.at[layer], functools.partial(lambda full, layer, block: full.at[block, layer], full, layer),
                weight_send.at[slot], weight_recv.at[slot], weight_own.at[slot],
            )
    weights["small", 0] = Weights(
        links, lsmall, lambda block: small.at[block], weight_send.at[8], weight_recv.at[8], weight_own.at[8], False
    )
    weights["small", 0].start()
    for layer in range(LAYERS):
        for kind in KINDS:
            weights[kind, layer].start()
    gradients = {}
    for place, (kind, full, core_in, side_in, half_in, quad_in, group_in, result) in enumerate(
        zip(
            KINDS, (gqkv, gproj, gfc1, gfc2), (cqkv, cproj, cfc1, cfc2), (xqkv, xproj, xfc1, xfc2),
            (yqkv, yproj, yfc1, yfc2), (zqkv, zproj, zfc1, zfc2), (eqkv, eproj, efc1, efc2), (rqkv, rproj, rfc1, rfc2),
        )
    ):
        for layer in range(LAYERS):
            slot = place * LAYERS + layer
            gradients[kind, layer] = Gradient(
                links, functools.partial(lambda full, layer, block: full.at[block, layer], full, layer),
                core_in.at[layer], side_in.at[layer], half_in.at[layer], quad_in.at[layer], group_in.at[layer],
                result.at[layer], grad_send.at[slot], grad_recv.at[slot],
            )
    gradients["rest", 0] = Gradient(
        links, lambda block: grest.at[block], crest, xrest, yrest, zrest, erest, rrest, grad_send.at[8], grad_recv.at[8]
    )

    def backward_point(index):
        for item in ORDER[index]:
            what, kind, layer = item.split(".")
            getattr(gradients[kind, int(layer)], what)()

    wide7[...] = jnp.zeros_like(wide7)
    wide3[...] = jnp.zeros_like(wide3)
    grest[...] = jnp.zeros_like(grest)
    place = (lax.broadcasted_iota(jnp.int32, (CAN, ROWS_IMG), 0) == tgt_row[0:1, :]).astype(f32).astype(bf16)
    streams[0] = mm(place, feats[...])
    grads[...] = mm(place, ograd[...])
    real = real_rows()
    for layer in range(LAYERS):
        forward(
            layer, real, same, moves, tap_mask, wqkv, wproj, wfc1, wfc2, small, shared, streams, unit1, inv1, normed1,
            queries, softs, exacts, values, convs, attended, unit2, inv2, normed2, active, slope, taps, wide7, wide3, work,
            functools.partial(forward_point, weights, layer),
        )
    back = (
        lax.broadcasted_iota(jnp.int32, (ROWS_IMG, CAN), 1) == tgt_col[:, 0:1]
    ).astype(f32).astype(bf16)
    out[...] = mm(back, streams[LAYERS].astype(bf16)).astype(bf16)
    for layer in reversed(range(LAYERS)):
        base = 0 if layer == LAYERS - 1 else 6
        backward(
            layer, same, moves, tap_mask, wqkv, wproj, wfc1, wfc2, small, shared, streams, unit1, inv1, normed1,
            queries, softs, exacts, values, convs, attended, unit2, inv2, normed2, active, slope, taps, wide7, wide3, work,
            grads, rel, gatt, gqkv, gproj, gfc1, gfc2, grest, lambda index, base=base: backward_point(base + index),
        )
    fgrad[...] = sum(mm(back, part) for part in halves(grads[...]))
    backward_point(12)
    last = pl.ds(FIRST_SHARED, 32)
    rshared[links.block] = rrest[last]
    for slot, (other, block) in enumerate(
        ((links.by_core, links.block_core), (links.by_side, links.block_side), (links.by_far, links.block_far))
    ):
        links.send(
            rshared.at[links.block], rshared.at[links.block], last_send.at[slot], last_recv.at[slot], other
        )
    for slot, block in enumerate((links.block_core, links.block_side, links.block_far)):
        links.arrived(rshared.at[block], last_send.at[slot], last_recv.at[slot])
    links.finish()


def forward_point(weights, layer, index):
    first = lambda kind, which: weights[kind, which].pass_first()
    second = lambda kind, which: weights[kind, which].pass_second()
    ready = lambda kind, which: weights[kind, which].wait()
    if layer == 0 and index == 0:
        first("small", 0)
        first("qkv", 0)
        first("proj", 0)
        second("qkv", 0)
        second("proj", 0)
        ready("small", 0)
        ready("qkv", 0)
    elif layer == 0 and index == 1:
        first("fc1", 0)
    elif layer == 0 and index == 3:
        first("fc2", 0)
        second("fc1", 0)
        ready("proj", 0)
    elif layer == 0 and index == 4:
        ready("fc1", 0)
    elif layer == 0 and index == 5:
        first("qkv", 1)
        second("fc2", 0)
        first("proj", 1)
        ready("fc2", 0)
    elif layer == 1 and index == 0:
        second("qkv", 1)
        second("proj", 1)
        first("fc1", 1)
        ready("qkv", 1)
    elif layer == 1 and index == 2:
        second("fc1", 1)
        first("fc2", 1)
    elif layer == 1 and index == 3:
        ready("proj", 1)
    elif layer == 1 and index == 4:
        ready("fc1", 1)
    elif layer == 1 and index == 5:
        second("fc2", 1)
        ready("fc2", 1)


def forward(
    layer, real, same, moves, tap_mask, wqkv, wproj, wfc1, wfc2, small, shared, streams, unit1, inv1, normed1,
    queries, softs, exacts, values, convs, attended, unit2, inv2, normed2, active, slope, taps, wide7, wide3, work,
    point,
):
    stream = streams[layer]
    fill(halves(stream), 1, moves, wide7, wide3)
    for block in range(BLOCKS):
        lanes = lanes_of(block)
        spread_taps(taps, block, shared[layer, 0:9, lanes])
        conv = convolve(taps, block, 1, 1, 1, False, wide7, wide3)
        work[0:END3, lanes] = streams[layer, 0:END3, lanes] + conv + shared[layer, 9:10, lanes]
        work[END3:CAN, lanes] = streams[layer, END3:CAN, lanes]
    unit, inverse, normed = norm_forward(work[...], shared[layer, 12:13], shared[layer, 14:15])
    unit1[layer] = unit
    inv1[layer] = inverse
    normed1[layer] = normed
    point(0)
    for block in range(BLOCKS):
        lanes = lanes_of(block)
        project = mm(normed, wqkv[block, layer])
        queries[layer, :, lanes] = (project[:, :LANES] + small[block, layer, 49:50]).astype(bf16)
        values[layer, :, lanes] = (project[:, 2 * LANES :] + small[block, layer, 50:51]).astype(bf16)
        keys = project[:, LANES : 2 * LANES].astype(bf16).astype(f32)
        largest = jnp.max(jnp.where(real, keys, -1e30), axis=0, keepdims=True)
        exponent = jnp.exp(jnp.where(real, keys - largest, 0.0))
        exact = exponent / sum(mm(same[...], part) for part in halves(exponent))
        exacts[layer, :, lanes] = exact
        softs[layer, :, lanes] = exact.astype(bf16)
        spread_taps(taps, block, small[block, layer, 0:49] * tap_mask[block, 0:49])
    point(1)
    fill([values[layer]], 3, moves, wide7, wide3)
    for block in range(BLOCKS):
        if block == 2:
            point(2)
        lanes = lanes_of(block)
        query = queries[layer, :, lanes]
        soft = softs[layer, :, lanes]
        value = values[layer, :, lanes]
        factors = []
        for head in range(2):
            masked = jnp.where(head_lanes(head), query, jnp.zeros_like(query))
            mixing = (mm_nt(masked, soft) * SCALE * same[...].astype(f32)).astype(bf16)
            factors.append(mm(mixing, value))
        factor = jnp.where(head_lanes(0), factors[0], factors[1])
        conv = convolve(taps, block, REACH7[block], REACH3[block], 3, False, wide7, wide3) + small[block, layer, 51:52]
        convs[layer, 0:END3, lanes] = conv
        attended[layer, 0:END3, lanes] = (factor[0:END3] + query[0:END3].astype(f32) * conv).astype(bf16)
        attended[layer, END3:CAN, lanes] = factor[END3:CAN].astype(bf16)
    point(3)
    after = work[...] + mm(attended[layer], wproj[:, layer].reshape(WIDE, WIDE)) + shared[layer, 10:11]
    unit, inverse, normed = norm_forward(after, shared[layer, 13:14], shared[layer, 15:16])
    unit2[layer] = unit
    inv2[layer] = inverse
    normed2[layer] = normed
    work[...] = after + shared[layer, 11:12]
    point(4)

    def feed(block, carry):
        hidden = mm(normed2[layer], wfc1[block, layer]) + jnp.concatenate(
            [small[block, layer, 52 + part : 53 + part] for part in range(4)], axis=1
        )
        chance = 0.5 * (1.0 + lax.erf(hidden * np.float32(0.5**0.5)))
        density = jnp.exp(hidden * hidden * -0.5) * np.float32((2 * np.pi) ** -0.5)
        slope[layer, block] = chance + hidden * density
        active[layer, block] = (hidden * chance).astype(bf16)
        return carry

    lax.fori_loop(0, BLOCKS, feed, 0)
    point(5)

    def collect(block, carry):
        work[...] += mm(active[layer, block], wfc2[block, layer])
        return carry

    lax.fori_loop(0, BLOCKS, collect, 0)
    streams[layer + 1] = work[...]


def backward(
    layer, same, moves, tap_mask, wqkv, wproj, wfc1, wfc2, small, shared, streams, unit1, inv1, normed1,
    queries, softs, exacts, values, convs, attended, unit2, inv2, normed2, active, slope, taps, wide7, wide3, work,
    grads, rel, gatt, gqkv, gproj, gfc1, gfc2, grest, point,
):
    def put_small(block, row, value):
        grest[block, 56 * layer + row : 56 * layer + row + value.shape[0]] = value

    def put_shared(row, value):
        for block in range(BLOCKS):
            first = FIRST_SHARED + 16 * layer + row
            grest[block, first : first + 1] = value[:, block * LANES : (block + 1) * LANES]

    put_shared(11, column_sum(grads[...]))
    work[...] = jnp.zeros_like(work)

    def feed(block, carry):
        grad_low = grads[...].astype(bf16)
        gfc2[block, layer] = mm_tn(active[layer, block], grad_low).astype(bf16)
        hidden = (mm_nt(grad_low, wfc2[block, layer]) * slope[layer, block]).astype(bf16)
        sums = column_sum(hidden.astype(f32))
        for part in range(4):
            row = 56 * layer + 52 + part
            grest[block, row : row + 1] = sums[:, part * LANES : (part + 1) * LANES]
        active[layer, block] = hidden
        return carry

    lax.fori_loop(0, BLOCKS, feed, 0)
    point(0)

    def collect(block, carry):
        hidden = active[layer, block]
        gfc1[block, layer] = mm_tn(normed2[layer], hidden).astype(bf16)
        work[...] += mm_nt(hidden, wfc1[block, layer])
        return carry

    lax.fori_loop(0, BLOCKS, collect, 0)
    point(1)
    incoming = work[...]
    unit = unit2[layer]
    put_shared(13, column_sum(incoming * unit))
    put_shared(15, column_sum(incoming))
    grads[...] = grads[...] + norm_backward(incoming, unit, inv2[layer], shared[layer, 13:14])
    branch = grads[...]
    put_shared(10, column_sum(branch))
    branch = branch.astype(bf16)
    gproj[:, layer] = mm_tn(attended[layer], branch).astype(bf16).reshape(BLOCKS, LANES, WIDE)
    gatt[...] = mm_nt(branch, wproj[:, layer].reshape(WIDE, WIDE)).astype(bf16)
    point(2)
    fill([values[layer]], 3, moves, wide7, wide3)
    for block in range(BLOCKS):
        lanes = lanes_of(block)
        product = gatt[0:END3, lanes].astype(f32) * queries[layer, 0:END3, lanes].astype(f32)
        rel[0:END3, lanes] = product.astype(bf16)
        rel[END3:CAN, lanes] = jnp.zeros((CAN - END3, LANES), bf16)
        put_small(block, 51, column_sum(product))
        sums = tap_grads(product, block, REACH7[block], REACH3[block], 3, taps, wide7, wide3)
        put_small(block, 0, sums * tap_mask[block, 0:49])
        spread_taps(taps, block, small[block, layer, 0:49] * tap_mask[block, 0:49])
    point(3)
    fill([rel[...]], 3, moves, wide7, wide3)
    work[...] = jnp.zeros_like(work)
    for block in range(BLOCKS):
        lanes = lanes_of(block)
        query = queries[layer, :, lanes]
        soft = softs[layer, :, lanes]
        value = values[layer, :, lanes]
        grad = gatt[:, lanes]
        exact = exacts[layer, :, lanes]
        picked = []
        for head in range(2):
            chosen = head_lanes(head)
            zero = jnp.zeros_like(query)
            query_head = jnp.where(chosen, query, zero)
            grad_head = jnp.where(chosen, grad, zero)
            same_low = same[...]
            mixing_t = (mm_nt(soft, query_head) * SCALE * same_low.astype(f32)).astype(bf16)
            mix = mm_nt(grad_head, value).astype(bf16) * same_low
            mix_t = mm_nt(value, grad_head).astype(bf16) * same_low
            picked.append((mm(mixing_t, grad), SCALE * mm(mix, soft), SCALE * mm(mix_t, query)))
        grad_value, grad_query, grad_soft = (
            jnp.where(head_lanes(0), one, two) for one, two in zip(*picked)
        )
        grad_soft = grad_soft.astype(bf16).astype(f32)
        weighted = grad_soft * exact
        grad_key = weighted - exact * sum(mm(same[...], part) for part in halves(weighted))
        conv = convolve(taps, block, REACH7[block], REACH3[block], 3, True, wide7, wide3)
        grad_value = jnp.concatenate([grad_value[0:END3] + conv, grad_value[END3:CAN]], axis=0).astype(bf16)
        grad_query = jnp.concatenate(
            [grad_query[0:END3] + grad[0:END3].astype(f32) * convs[layer, 0:END3, lanes], grad_query[END3:CAN]], axis=0
        ).astype(bf16)
        put_small(block, 49, column_sum(grad_query.astype(f32)))
        put_small(block, 50, column_sum(grad_value.astype(f32)))
        joined = jnp.concatenate([grad_query, grad_key.astype(bf16), grad_value], axis=1)
        gqkv[block, layer] = mm_tn(normed1[layer], joined).astype(bf16)
        work[...] += mm_nt(joined, wqkv[block, layer])
    point(4)
    incoming = work[...]
    unit = unit1[layer]
    put_shared(12, column_sum(incoming * unit))
    put_shared(14, column_sum(incoming))
    grads[...] = grads[...] + norm_backward(incoming, unit, inv1[layer], shared[layer, 12:13])
    fill(halves(streams[layer]), 1, moves, wide7, wide3)
    for block in range(BLOCKS):
        lanes = lanes_of(block)
        product = grads[0:END3, lanes]
        first = FIRST_SHARED + 16 * layer
        grest[block, first + 9 : first + 10] = column_sum(product)
        grest[block, first : first + 9] = tap_grads(product, block, 1, 1, 1, taps, wide7, wide3)
    fill(halves(grads[...]), 1, moves, wide7, wide3)
    for block in range(BLOCKS):
        lanes = lanes_of(block)
        spread_taps(taps, block, shared[layer, 0:9, lanes])
        conv = convolve(taps, block, 1, 1, 1, True, wide7, wide3)
        grads[0:END3, lanes] = grads[0:END3, lanes] + conv
    point(5)


def canonical_targets(crops, sides, places):
    crops = crops % 8
    first = places == 0
    earlier = first[None, :] & (crops[None, :] < crops[:, None])
    seven = jnp.sum((earlier & (sides == 7)[None, :]).astype(jnp.int32), axis=1)
    three = jnp.sum((earlier & (sides == 3)[None, :]).astype(jnp.int32), axis=1)
    cell = jnp.maximum(places - 1, 0)
    row, col = cell // sides, cell % sides
    in_seven = seven * 56 + row * 8 + col
    in_three = END7 + (three // 2) * 24 + row * 8 + (three % 2) * 4 + col
    big = sides == 7
    return jnp.where(first, END3 + jnp.where(big, seven, 2 + three), jnp.where(big, in_seven, in_three))


def shards(
    data, features, crop_index, grid_size, position, cpe_weight, shared_bias, norm_gain, norm_bias,
    qkv_weight, head_bias, crpe_weight, proj_weight, fc1_weight, fc1_bias, fc2_weight, out_grad,
):
    start = lax.axis_index("mp") * ROWS_IMG
    mine = [lax.dynamic_slice_in_dim(item, start, ROWS_IMG) for item in (crop_index, grid_size, position)]
    target = canonical_targets(*mine)
    tgt_row = jnp.broadcast_to(target[None, :], (8, ROWS_IMG))
    tgt_col = jnp.broadcast_to(target[:, None], (ROWS_IMG, LANES))
    same, moves = canonical_tables()
    small = jnp.concatenate([crpe_weight, head_bias, fc1_bias.reshape(LAYERS, 4, LANES)], axis=1)
    shared = jnp.concatenate([cpe_weight, shared_bias, norm_gain, norm_bias], axis=1)
    assert data % 8 == 0 and features.shape[0] == ROWS_IMG
    many = data // 8
    vmem = pl.BlockSpec(memory_space=pltpu.VMEM)
    hbm = pl.BlockSpec(memory_space=pl.ANY)
    shape = jax.ShapeDtypeStruct
    rows = lambda kind: pltpu.VMEM((LAYERS, CAN, WIDE), kind)
    quarters = ((WIDE, 3 * LANES), (LANES, WIDE), (WIDE, WIDE), (WIDE, WIDE))
    received = lambda lead, share: [
        pltpu.VMEM((LAYERS, *lead, tall // share, wide), bf16) for tall, wide in quarters
    ] + [pltpu.VMEM((*lead, REST // share, LANES), f32)]
    copies = 16 + many
    out, fgrad, rqkv, rproj, rfc1, rfc2, rrest, rshared = pl.pallas_call(
        functools.partial(step_kernel, many),
        out_shape=(
            shape((ROWS_IMG, WIDE), bf16),
            shape((ROWS_IMG, WIDE), f32),
            *(shape((LAYERS, *quarter), bf16) for quarter in quarters),
            shape((REST, LANES), f32),
            shape((BLOCKS, 32, LANES), f32),
        ),
        in_specs=[vmem] * 7 + [hbm] * 5 + [vmem],
        out_specs=(vmem,) * 8,
        scratch_shapes=[
            *(pltpu.VMEM((BLOCKS, LAYERS, *quarter), bf16) for quarter in quarters),
            pltpu.VMEM((BLOCKS, LAYERS, 56, LANES), f32),
            *(pltpu.VMEM((BLOCKS, LAYERS, *quarter), bf16) for quarter in quarters),
            pltpu.VMEM((BLOCKS, REST, LANES), f32),
            *received((2,), 1),
            *received((), 1),
            *received((), 2),
            *received((3,), 8),
            *received((max(many - 1, 1),), 8),
            pltpu.VMEM((LAYERS + 1, CAN, WIDE), f32),
            rows(f32),
            pltpu.VMEM((LAYERS, CAN, 1), f32),
            rows(bf16),
            rows(bf16),
            rows(bf16),
            rows(f32),
            rows(bf16),
            rows(f32),
            rows(bf16),
            rows(f32),
            pltpu.VMEM((LAYERS, CAN, 1), f32),
            rows(bf16),
            pltpu.VMEM((LAYERS, BLOCKS, CAN, WIDE), bf16),
            pltpu.VMEM((LAYERS, BLOCKS, CAN, WIDE), f32),
            pltpu.VMEM((BLOCKS, 49, 8, LANES), f32),
            pltpu.VMEM((7, 2, 104, WIDE), f32),
            pltpu.VMEM((5, 3, 56, WIDE), f32),
            pltpu.VMEM((CAN, WIDE), f32),
            pltpu.VMEM((CAN, WIDE), f32),
            pltpu.VMEM((CAN, WIDE), bf16),
            pltpu.VMEM((CAN, WIDE), bf16),
            pltpu.SemaphoreType.DMA((9, 5)),
            pltpu.SemaphoreType.DMA((9, 5)),
            pltpu.SemaphoreType.DMA((9,)),
            pltpu.SemaphoreType.DMA((9, copies)),
            pltpu.SemaphoreType.DMA((9, copies)),
            pltpu.SemaphoreType.DMA((3,)),
            pltpu.SemaphoreType.DMA((3,)),
        ],
        compiler_params=pltpu.CompilerParams(
            vmem_limit_bytes=63 * 2**20, collective_id=0, has_side_effects=True
        ),
        name="step",
    )(
        tgt_row, tgt_col, features, out_grad,
        jnp.asarray(same, bf16), jnp.asarray(moves, bf16), jnp.asarray(tap_table()),
        qkv_weight.reshape(LAYERS, WIDE, 3 * LANES), proj_weight, fc1_weight, fc2_weight, small, shared,
    )
    rest = rrest[:FIRST_SHARED].reshape(LAYERS, 56, LANES)
    both = jnp.transpose(rshared, (1, 0, 2)).reshape(LAYERS, 16, WIDE)
    return (
        out,
        fgrad,
        both[:, 0:9],
        both[:, 9:12],
        both[:, 12:14],
        both[:, 14:16],
        rqkv.astype(f32).reshape(LAYERS, WIDE, 3, LANES),
        rest[:, 49:52],
        rest[:, 0:49],
        rproj.astype(f32),
        rfc1.astype(f32),
        rest[:, 52:56].reshape(LAYERS, WIDE),
        rfc2.astype(f32),
    )


def solution(mesh):
    placed = (
        P(("dp", "mp"), None),
        P("dp"),
        P("dp"),
        P("dp"),
        P(),
        P(),
        P(),
        P(),
        P(None, None, None, "mp"),
        P(None, None, "mp"),
        P(None, None, "mp"),
        P(None, "mp", None),
        P(None, None, "mp"),
        P(None, "mp"),
        P(None, "mp", None),
        P(("dp", "mp"), None),
    )
    return jax.shard_map(
        functools.partial(shards, mesh.shape["dp"]),
        mesh=mesh,
        in_specs=placed,
        out_specs=(
            P(("dp", "mp"), None),
            P(("dp", "mp"), None),
            P(),
            P(),
            P(),
            P(),
            P(None, None, None, "mp"),
            P(None, None, "mp"),
            P(None, None, "mp"),
            P(None, "mp", None),
            P(None, None, "mp"),
            P(None, "mp"),
            P(None, "mp", None),
        ),
        check_vma=False,
    )
```

```python
import functools
import types

import jax
import jax.numpy as jnp
import numpy as np
from jax import lax
from jax.experimental import pallas as pl
from jax.experimental.pallas import tpu as pltpu
from jax.sharding import PartitionSpec as P

HD = 64
LAYERS = 2
ROWS_IMG = 160
CAN = 192
END7 = 112
END3 = 184
LANES = 128
WIDE = 512
BLOCKS = 4
EPSILON = 1e-06
SCALE = HD ** (-0.5)
REACH7 = (1, 2, 3, 3)
REACH3 = (1, 2, 2, 2)
MESH = pl.DeviceIdType.MESH
f32 = jnp.float32
bf16 = jnp.bfloat16


def canonical_tables():
    crop = np.full(CAN, 100)
    col = np.full(CAN, -1)
    side = np.zeros(CAN, int)
    for t in range(END7):
        if t % 8 < 7:
            crop[t], col[t], side[t] = t // 56, t % 8, 7
    for t in range(END7, END3):
        u = t - END7
        if t % 4 < 3:
            crop[t], col[t], side[t] = 2 + 2 * (u // 24) + (t % 8) // 4, t % 4, 3
    for t in range(END3, CAN):
        crop[t] = t - END3
    same = (crop[:, None] == crop[None, :]).astype(np.float32)
    moves = np.zeros((7, CAN, CAN), np.float32)
    for b in range(-3, 4):
        for t in range(END3):
            if col[t] >= 0 and 0 <= col[t] + b < side[t]:
                moves[b + 3, t, t + b] = 1
    return same, moves


def tap_table():
    table = np.zeros((BLOCKS, 56, LANES), np.float32)
    for channel in range(WIDE):
        head = channel // HD
        reach = 1 if head < 2 else 2 if head < 5 else 3
        for tap in range(49):
            if max(abs(tap // 7 - 3), abs(tap % 7 - 3)) <= reach:
                table[channel // LANES, tap, channel % LANES] = 1
    return table


def mm(left, right):
    return jnp.dot(left, right, preferred_element_type=f32)


def mm_nt(left, right):
    return lax.dot_general(left, right, (((1,), (1,)), ((), ())), preferred_element_type=f32)


def mm_tn(left, right):
    return lax.dot_general(left, right, (((0,), (0,)), ((), ())), preferred_element_type=f32)


def side_by_side(parts):
    return jnp.concatenate([parts[index] for index in range(parts.shape[0])], axis=1)


def halves(values):
    high = values.astype(bf16)
    return [high, (values - high.astype(f32)).astype(bf16)]


def lanes_of(block):
    return pl.ds(block * LANES, LANES)


def column_sum(values):
    return jnp.sum(values, axis=0, keepdims=True)


def fill(parts, reach, moves, wide7, wide3):
    for b in range(-reach, reach + 1):
        moved = sum(mm(moves[b + 3], part) for part in parts)
        for grid in range(2):
            wide7[b + 3, grid, 24:80] = moved[grid * 56 : grid * 56 + 56]
        if abs(b) <= 2:
            for pair in range(3):
                first = END7 + pair * 24
                wide3[b + 2, pair, 16:40] = moved[first : first + 24]


def tap_row(a, b, half, flip):
    if flip:
        a, b = -a, -b
    return (a + half) * (2 * half + 1) + b + half


def spread_taps(spread, block, rows):
    for row in range(rows.shape[0]):
        spread[block, row] = jnp.broadcast_to(rows[row : row + 1], (8, LANES))


def convolve(spread, block, reach7, reach3, half, flip, wide7, wide3):
    lanes = lanes_of(block)

    def loop(wide, offset, reach, grids, tall):
        def body(step, acc):
            b = step - reach
            for a in range(-reach, reach + 1):
                weight = spread[block, tap_row(a, b, half, flip)]
                seen = wide[b + offset, :, pl.ds((a + offset) * 8, tall), lanes]
                acc = acc + weight * seen.reshape(-1, 8, LANES)
            return acc

        return lax.fori_loop(0, 2 * reach + 1, body, jnp.zeros((grids * tall // 8, 8, LANES), f32))

    acc7 = loop(wide7, 3, reach7, 2, 56)
    acc3 = loop(wide3, 2, reach3, 3, 24)
    return jnp.concatenate([acc7.reshape(END7, LANES), acc3.reshape(END3 - END7, LANES)], axis=0)


def tap_grads(grad, block, reach7, reach3, half, spread, wide7, wide3):
    lanes = lanes_of(block)
    count = (2 * half + 1) ** 2
    grad7 = grad[:END7].reshape(-1, 8, LANES)
    grad3 = grad[END7:END3].reshape(-1, 8, LANES)
    spread[block, 0:count] = jnp.zeros((count, 8, LANES), f32)

    def loop(wide, offset, reach, part, tall):
        def body(step, carry):
            b = step - reach
            for a in range(-reach, reach + 1):
                seen = wide[b + offset, :, pl.ds((a + offset) * 8, tall), lanes]
                row = tap_row(a, b, half, False)
                spread[block, row] += jnp.sum(part * seen.reshape(-1, 8, LANES), axis=0)
            return carry

        lax.fori_loop(0, 2 * reach + 1, body, 0)

    loop(wide7, 3, reach7, grad7, 56)
    loop(wide3, 2, reach3, grad3, 24)
    return jnp.sum(spread[block, 0:count], axis=1)


def norm_forward(values, gain, bias):
    center = values - jnp.mean(values, axis=-1, keepdims=True)
    spread = jnp.mean(center * center, axis=-1, keepdims=True)
    inverse = lax.rsqrt(spread + EPSILON)
    unit = center * inverse
    return unit, inverse, (unit * gain + bias).astype(bf16)


def norm_backward(incoming, unit, inverse, gain):
    scaled = incoming * gain
    mean_one = jnp.mean(scaled, axis=-1, keepdims=True)
    mean_two = jnp.mean(scaled * unit, axis=-1, keepdims=True)
    return inverse * (scaled - mean_one - unit * mean_two)


def real_rows():
    row = lax.broadcasted_iota(jnp.int32, (CAN, LANES), 0)
    seven = (row < END7) & ((row & 7) != 7)
    three = (row >= END7) & (row < END3) & ((row & 3) != 3)
    return seven | three | (row >= END3)


def head_lanes(head):
    lane = lax.broadcasted_iota(jnp.int32, (CAN, LANES), 1)
    return (lane >= HD) if head else (lane < HD)


def rows_of(ref, start, count):
    rows = pl.ds(pl.multiple_of(start, 8), count)
    return ref.at[rows] if len(ref.shape) == 2 else ref.at[:, rows]


def add_rows(target, start, source, first, count):
    step = next(size for size in (64, 48, 32, 24, 16, 8) if count % size == 0)

    def body(index, carry):
        into = pl.ds(pl.multiple_of(start + index * step, 8), step)
        target[into] = target[into] + source[pl.ds(pl.multiple_of(first + index * step, 8), step)]
        return carry

    lax.fori_loop(0, count // step, body, 0)


class Links:
    def __init__(self, many):
        dp, mp = lax.axis_index("dp"), lax.axis_index("mp")
        self.many = many
        self.core, self.side = lax.rem(mp, 2), lax.div(mp, 2)
        self.half, self.quad, self.group = lax.rem(dp, 2), lax.rem(lax.div(dp, 2), 4), lax.div(dp, 8)
        self.block = mp
        self.block_core = self.side * 2 + 1 - self.core
        self.block_side = (1 - self.side) * 2 + self.core
        self.block_far = (1 - self.side) * 2 + 1 - self.core
        self.by_core = (dp, self.block_core)
        self.by_side = (dp, self.block_side)
        self.by_far = (dp, self.block_far)
        self.by_half = (dp + 1 - 2 * self.half, mp)
        self.by_quad = [
            (self.group * 8 + lax.rem(self.quad + step, 4) * 2 + self.half, mp) for step in range(1, 4)
        ]
        self.by_group = [
            (lax.rem(self.group + step, many) * 8 + self.quad * 2 + self.half, mp) for step in range(1, many)
        ]
        self.pair = lax.rem(self.quad, 2)
        self.by_pair = (self.group * 8 + (self.quad + 1 - 2 * self.pair) * 2 + self.half, mp)
        self.sent = []

    def meet(self):
        barrier = pltpu.get_barrier_semaphore()
        others = [self.by_core, self.by_side, self.by_far, self.by_half] + self.by_quad + self.by_group
        for other in others:
            pl.semaphore_signal(barrier, inc=1, device_id=other, device_id_type=MESH)
        pl.semaphore_wait(barrier, len(others))

    def send(self, source, target, send_sem, recv_sem, other):
        copy = pltpu.make_async_remote_copy(
            src_ref=source, dst_ref=target, send_sem=send_sem, recv_sem=recv_sem, device_id=other, device_id_type=MESH
        )
        copy.start()
        self.sent.append(copy)

    def arrived(self, target, send_sem, recv_sem):
        pltpu.make_async_remote_copy(
            src_ref=target, dst_ref=target, send_sem=send_sem, recv_sem=recv_sem, device_id=self.by_core,
            device_id_type=MESH,
        ).wait_recv()

    def finish(self):
        for copy in self.sent:
            copy.wait_send()


class Weights:
    def __init__(self, links, local, full, send_sems, recv_sems, own_sem):
        self.links, self.local, self.full = links, local, full
        self.send_sems, self.recv_sems, self.own_sem = send_sems, recv_sems, own_sem
        self.count = local.shape[-2] // 4
        self.sub = self.count // 2

    def start_of(self, half, pair):
        return (half * 2 + pair) * self.count

    def places(self):
        links = self.links
        far = self.start_of(1 - links.half, 1 - links.pair)
        return (
            (self.start_of(links.half, links.pair), self.count),
            (self.start_of(1 - links.half, links.pair), self.count),
            (self.start_of(links.half, 1 - links.pair), self.count),
            (far + self.sub, self.sub),
            (far, self.sub),
        )

    def push(self, part, slot, other):
        self.links.send(part, part, self.send_sems.at[slot], self.recv_sems.at[slot], other)

    def take(self, index):
        start, count = self.places()[index]
        part = rows_of(self.full(self.links.block_side), start, count)
        self.links.arrived(part, self.send_sems.at[index], self.recv_sems.at[index])
        self.push(part, 5 + index, self.links.by_core)
        return part

    def start(self):
        links = self.links
        start = self.start_of(links.half, links.pair)
        links.send(
            rows_of(self.local, start, self.count), rows_of(self.full(links.block), start, self.count),
            self.send_sems.at[0], self.recv_sems.at[0], links.by_side,
        )

    def start_near(self):
        links = self.links
        links.send(self.local, self.full(links.block), self.send_sems.at[10], self.recv_sems.at[10], links.by_core)
        self.own = pltpu.make_async_copy(self.local, self.full(links.block), self.own_sem)
        self.own.start()

    def F1(self):
        part = self.take(0)
        self.push(part, 1, self.links.by_half)
        self.push(part, 2, self.links.by_pair)

    def Y1(self):
        part = self.take(1)
        self.push(rows_of(part, 0, self.sub), 4, self.links.by_pair)

    def Z1(self):
        part = self.take(2)
        self.push(rows_of(part, self.sub, self.sub), 3, self.links.by_half)

    def YD(self):
        self.take(3)

    def ZD(self):
        self.take(4)

    def wait(self):
        links = self.links
        self.own.wait()
        links.arrived(self.full(links.block_core), self.send_sems.at[10], self.recv_sems.at[10])
        for index, (start, count) in enumerate(self.places()):
            links.arrived(
                rows_of(self.full(links.block_far), start, count), self.send_sems.at[5 + index], self.recv_sems.at[5 + index]
            )


class Small:
    def __init__(self, links, local, full, send_sems, recv_sems, own_sem):
        self.links, self.local, self.full = links, local, full
        self.send_sems, self.recv_sems, self.own_sem = send_sems, recv_sems, own_sem

    def start(self):
        links = self.links
        for slot, other in enumerate((links.by_side, links.by_core)):
            links.send(self.local, self.full.at[links.block], self.send_sems.at[slot], self.recv_sems.at[slot], other)
        self.own = pltpu.make_async_copy(self.local, self.full.at[links.block], self.own_sem)
        self.own.start()

    def wait(self):
        links = self.links
        part = self.full.at[links.block_side]
        links.arrived(part, self.send_sems.at[0], self.recv_sems.at[0])
        links.send(part, part, self.send_sems.at[2], self.recv_sems.at[2], links.by_core)
        self.own.wait()
        links.arrived(self.full.at[links.block_core], self.send_sems.at[1], self.recv_sems.at[1])
        links.arrived(self.full.at[links.block_far], self.send_sems.at[2], self.recv_sems.at[2])


class Gradient:
    def __init__(self, links, full, core_in, side_in, half_in, quad_in, group_in, result, send_sems, recv_sems):
        self.links, self.full, self.result = links, full, result
        self.core_in, self.side_in, self.half_in, self.quad_in, self.group_in = core_in, side_in, half_in, quad_in, group_in
        self.send_sems, self.recv_sems = send_sems, recv_sems
        self.tall = result.shape[0]
        self.half, self.piece = self.tall // 2, self.tall // 8
        self.here, self.there = links.half * self.half, (1 - links.half) * self.half
        self.mine = self.here + links.quad * self.piece

    def CS(self):
        links = self.links
        for place, side in ((0, 1 - links.side), (1, links.side)):
            links.send(
                self.full(side * 2 + 1 - links.core), self.core_in.at[place], self.send_sems.at[place],
                self.recv_sems.at[place], links.by_core,
            )

    def CX(self):
        links = self.links
        links.arrived(self.core_in.at[0], self.send_sems.at[0], self.recv_sems.at[0])
        part = self.full(links.block_side)
        add_rows(part, 0, self.core_in.at[0], 0, self.tall)
        links.send(part, self.side_in, self.send_sems.at[2], self.recv_sems.at[2], links.by_side)

    def CO(self):
        links = self.links
        links.arrived(self.core_in.at[1], self.send_sems.at[1], self.recv_sems.at[1])
        add_rows(self.full(links.block), 0, self.core_in.at[1], 0, self.tall)

    def XA(self):
        links = self.links
        links.arrived(self.side_in, self.send_sems.at[2], self.recv_sems.at[2])
        total = self.full(links.block)
        add_rows(total, self.there, self.side_in, self.there, self.half)
        links.send(
            rows_of(total, self.there, self.half), self.half_in, self.send_sems.at[3], self.recv_sems.at[3], links.by_half
        )
        add_rows(total, self.here, self.side_in, self.here, self.half)

    def YA(self):
        links = self.links
        links.arrived(self.half_in, self.send_sems.at[3], self.recv_sems.at[3])
        total = self.full(links.block)
        add_rows(total, self.here, self.half_in, 0, self.half)
        for step in range(3):
            start = self.here + lax.rem(links.quad + step + 1, 4) * self.piece
            links.send(
                rows_of(total, start, self.piece), self.quad_in.at[step], self.send_sems.at[4 + step],
                self.recv_sems.at[4 + step], links.by_quad[step],
            )

    def ZA(self):
        links = self.links
        mine = pl.ds(pl.multiple_of(self.mine, 8), self.piece)
        total = self.full(links.block)
        for step in range(3):
            links.arrived(self.quad_in.at[step], self.send_sems.at[4 + step], self.recv_sems.at[4 + step])
        value = total[mine].astype(f32)
        for step in range(3):
            value = value + self.quad_in[step].astype(f32)
        if links.many > 1:
            total[mine] = value.astype(total.dtype)
            for step in range(links.many - 1):
                links.send(
                    total.at[mine], self.group_in.at[step], self.send_sems.at[11 + step], self.recv_sems.at[11 + step],
                    links.by_group[step],
                )
            value = total[mine].astype(f32)
            for step in range(links.many - 1):
                links.arrived(self.group_in.at[step], self.send_sems.at[11 + step], self.recv_sems.at[11 + step])
                value = value + self.group_in[step].astype(f32)
        self.result[mine] = value.astype(self.result.dtype)
        for step in range(3):
            links.send(
                self.result.at[mine], self.result.at[mine], self.send_sems.at[7 + step], self.recv_sems.at[7 + step],
                links.by_quad[step],
            )

    def ZF(self):
        links = self.links
        for step in range(3):
            start = self.here + lax.rem(links.quad + 3 - step, 4) * self.piece
            links.arrived(
                rows_of(self.result, start, self.piece), self.send_sems.at[7 + step], self.recv_sems.at[7 + step]
            )
        part = rows_of(self.result, self.here, self.half)
        links.send(part, part, self.send_sems.at[10], self.recv_sems.at[10], links.by_half)

    def FN(self):
        self.links.arrived(
            rows_of(self.result, self.there, self.half), self.send_sems.at[10], self.recv_sems.at[10]
        )


FORWARD_ORDER = {
    (0, 0): (
        "F1.qkv.0.0", "F1.proj.0.0", "F1.fc1.0.0", "Y1.qkv.0.0", "Z1.qkv.0.0", "Y1.proj.0.0", "Z1.proj.0.0",
        "F1.fc2.0.0", "Y1.fc1.0.0", "Z1.fc1.0.0", "F1.qkv.1.0", "YD.qkv.0.0", "ZD.qkv.0.0",
    ),
    (0, 1): (
        "F1.proj.1.0", "YD.proj.0.0", "ZD.proj.0.0", "F1.fc1.1.0", "Y1.fc2.0.0", "Z1.fc2.0.0",
    ),
    (0, 2): (
        "YD.fc1.0.0", "ZD.fc1.0.0",
    ),
    (0, 3): (
        "F1.fc2.1.0",
    ),
    (0, 4): (
        "Y1.qkv.1.0", "Z1.qkv.1.0",
    ),
    (0, 5): (
        "Y1.proj.1.0", "Z1.proj.1.0",
    ),
    (0, 7): (
        "Y1.fc1.1.0", "Z1.fc1.1.0", "YD.fc2.0.0", "ZD.fc2.0.0",
    ),
    (1, 0): (
        "Y1.fc2.1.0", "Z1.fc2.1.0", "YD.qkv.1.0", "ZD.qkv.1.0", "YD.proj.1.0", "ZD.proj.1.0",
    ),
    (1, 1): (
        "YD.fc1.1.0", "ZD.fc1.1.0", "ZD.fc2.1.0", "YD.fc2.1.0",
    ),
}
BACKWARD_ORDER = {
    (1, 0): (
        "CS.fc2.1.0", "CS.fc2.1.1", "CS.fc2.1.2", "CS.fc2.1.3",
    ),
    (1, 1): (
        "CS.fc1.1.0", "CS.fc1.1.1", "CS.fc1.1.2", "CS.fc1.1.3", "CX.fc2.1.0", "CX.fc2.1.1", "CO.fc2.1.0",
        "CX.fc2.1.2", "CO.fc2.1.1", "CO.fc2.1.2",
    ),
    (1, 2): (
        "CS.proj.1.0", "CX.fc2.1.3", "CX.fc1.1.0", "CX.fc1.1.1", "CO.fc2.1.3", "CO.fc1.1.0", "CO.fc1.1.1",
        "CX.fc1.1.2",
    ),
    (1, 3): (
        "CX.fc1.1.3", "CX.proj.1.0", "XA.fc2.1.0", "CO.fc1.1.2", "CO.fc1.1.3", "CO.proj.1.0",
    ),
    (1, 5): (
        "XA.fc2.1.1",
    ),
    (1, 6): (
        "YA.fc2.1.0",
    ),
    (1, 7): (
        "CS.qkv.1.0", "CS.qkv.1.1", "CS.qkv.1.2", "XA.fc2.1.2",
    ),
    (1, 8): (
        "CX.qkv.1.0", "YA.fc2.1.1", "ZA.fc2.1.0", "XA.fc2.1.3", "CX.qkv.1.1", "CO.qkv.1.0", "CO.qkv.1.1",
    ),
    (0, 0): (
        "CS.fc2.0.0", "CS.fc2.0.1", "CS.fc2.0.2", "CS.fc2.0.3", "CX.qkv.1.2", "XA.fc1.1.0", "YA.fc2.1.2",
        "YA.fc2.1.3", "ZA.fc2.1.1", "CO.qkv.1.2",
    ),
    (0, 1): (
        "CS.fc1.0.0", "CS.fc1.0.1", "CS.fc1.0.2", "CS.fc1.0.3", "CX.fc2.0.0", "CX.fc2.0.1", "CX.fc2.0.2",
        "CX.fc2.0.3", "XA.fc1.1.1", "YA.fc1.1.0", "ZA.fc2.1.2", "ZF.fc2.1.0", "CO.fc2.0.0", "CO.fc2.0.1",
        "CO.fc2.0.2", "CO.fc2.0.3",
    ),
    (0, 2): (
        "CS.proj.0.0", "CX.fc1.0.0", "CX.fc1.0.1", "CX.fc1.0.2", "XA.fc1.1.2", "ZA.fc2.1.3", "CO.fc1.0.0",
        "CX.fc1.0.3", "ZF.fc2.1.1", "CO.fc1.0.1", "YA.fc1.1.1", "CO.fc1.0.2", "CO.fc1.0.3",
    ),
    (0, 3): (
        "CX.proj.0.0", "XA.fc1.1.3", "YA.fc1.1.2", "ZA.fc1.1.0", "ZF.fc2.1.2", "CO.proj.0.0", "FN.fc2.1.0",
    ),
    (0, 4): (
        "XA.proj.1.0", "ZF.fc2.1.3", "FN.fc2.1.1",
    ),
    (0, 5): (
        "YA.fc1.1.3", "ZA.fc1.1.1",
    ),
    (0, 6): (
        "ZA.fc1.1.2",
    ),
    (0, 7): (
        "CS.qkv.0.0", "CS.qkv.0.1", "CS.qkv.0.2", "XA.qkv.1.0", "ZF.fc1.1.0", "YA.proj.1.0", "FN.fc2.1.2",
    ),
    (0, 8): (
        "CX.qkv.0.0", "CX.qkv.0.1", "XA.qkv.1.1", "ZA.fc1.1.3", "ZF.fc1.1.1", "CX.qkv.0.2", "CO.qkv.0.0",
        "CO.qkv.0.1", "CO.qkv.0.2", "YA.qkv.1.0", "FN.fc2.1.3",
    ),
    (0, 9): (
        "CS.rest.0.0", "ZF.fc1.1.2", "XA.qkv.1.2", "FN.fc1.1.0", "ZA.proj.1.0", "CX.rest.0.0", "CO.rest.0.0",
        "YA.qkv.1.1", "ZF.fc1.1.3", "XA.fc2.0.0", "FN.fc1.1.1", "ZA.qkv.1.0", "FN.fc1.1.2", "ZF.proj.1.0",
        "XA.fc2.0.1", "YA.qkv.1.2", "ZA.qkv.1.1", "FN.fc1.1.3", "ZF.qkv.1.0", "XA.fc2.0.2", "YA.fc2.0.0",
        "ZA.qkv.1.2", "FN.proj.1.0", "ZF.qkv.1.1", "XA.fc2.0.3", "YA.fc2.0.1", "ZA.fc2.0.0", "FN.qkv.1.0",
        "ZF.qkv.1.2", "XA.fc1.0.0", "YA.fc2.0.2", "ZA.fc2.0.1", "FN.qkv.1.1", "ZF.fc2.0.0", "XA.fc1.0.1",
        "YA.fc2.0.3", "ZA.fc2.0.2", "FN.qkv.1.2", "ZF.fc2.0.1", "XA.fc1.0.2", "YA.fc1.0.0", "ZA.fc2.0.3",
        "FN.fc2.0.0", "ZF.fc2.0.2", "XA.fc1.0.3", "YA.fc1.0.1", "ZA.fc1.0.0", "FN.fc2.0.1", "ZF.fc2.0.3",
        "XA.proj.0.0", "YA.fc1.0.2", "ZA.fc1.0.1", "FN.fc2.0.2", "ZF.fc1.0.0", "XA.qkv.0.0", "YA.fc1.0.3",
        "ZA.fc1.0.2", "FN.fc2.0.3", "ZF.fc1.0.1", "XA.qkv.0.1", "YA.proj.0.0", "ZA.fc1.0.3", "FN.fc1.0.0",
        "ZF.fc1.0.2", "XA.qkv.0.2", "YA.qkv.0.0", "ZA.proj.0.0", "FN.fc1.0.1", "XA.rest.0.0", "ZF.fc1.0.3",
        "YA.qkv.0.1", "ZA.qkv.0.0", "FN.fc1.0.2", "ZF.proj.0.0", "YA.qkv.0.2", "ZA.qkv.0.1", "YA.rest.0.0",
        "ZF.qkv.0.0", "FN.fc1.0.3", "ZA.qkv.0.2", "FN.proj.0.0", "ZF.qkv.0.1", "FN.qkv.0.0", "ZA.rest.0.0",
        "ZF.qkv.0.2", "FN.qkv.0.1", "ZF.rest.0.0", "FN.qkv.0.2", "FN.rest.0.0",
    ),
}
NEEDED = {0: "qkv", 5: "proj", 6: "fc1", 7: "fc2"}
KINDS = ("qkv", "proj", "fc1", "fc2")
SHAPES = {"qkv": (3, WIDE, LANES), "proj": (LANES, WIDE), "fc1": (WIDE, WIDE), "fc2": (WIDE, WIDE)}
CHUNKS = {"qkv": 3, "proj": 1, "fc1": 4, "fc2": 4}
REST = 192
FIRST_SHARED = 112


def chunk_list():
    names = [(kind, layer, part) for kind in KINDS for layer in range(LAYERS) for part in range(CHUNKS[kind])]
    return names + [("rest", 0, 0)]


def chunk_shape(kind):
    if kind == "rest":
        return REST, LANES, f32
    if kind == "qkv":
        return WIDE, LANES, bf16
    tall, wide = SHAPES[kind]
    return tall // CHUNKS[kind], wide, bf16


def scratch_specs(many):
    rows = lambda kind: pltpu.VMEM((LAYERS, CAN, WIDE), kind)
    specs = {}
    for kind in KINDS:
        specs["w" + kind] = pltpu.VMEM((BLOCKS, LAYERS, *SHAPES[kind]), bf16)
        specs["g" + kind] = pltpu.VMEM((BLOCKS, LAYERS, *SHAPES[kind]), bf16)
    specs["small"] = pltpu.VMEM((BLOCKS, LAYERS, 56, LANES), f32)
    specs["lsmall"] = pltpu.VMEM((LAYERS, 56, LANES), f32)
    specs["grest"] = pltpu.VMEM((BLOCKS, REST, LANES), f32)
    for slot, (kind, layer, part) in enumerate(chunk_list()):
        tall, wide, dtype = chunk_shape(kind)
        specs[f"core{slot}"] = pltpu.VMEM((2, tall, wide), dtype)
        specs[f"side{slot}"] = pltpu.VMEM((tall, wide), dtype)
        specs[f"half{slot}"] = pltpu.VMEM((tall // 2, wide), dtype)
        specs[f"quad{slot}"] = pltpu.VMEM((3, tall // 8, wide), dtype)
        specs[f"group{slot}"] = pltpu.VMEM((max(many - 1, 1), tall // 8, wide), dtype) if many > 1 else None
    for name, dtype in (
        ("unit1", f32), ("normed1", bf16), ("queries", bf16), ("softs", bf16), ("exacts", f32), ("values", bf16),
        ("convs", f32), ("attended", bf16), ("unit2", f32), ("normed2", bf16),
    ):
        specs[name] = rows(dtype)
    specs["streams"] = pltpu.VMEM((LAYERS + 1, CAN, WIDE), f32)
    specs["inv1"] = pltpu.VMEM((LAYERS, CAN, 1), f32)
    specs["inv2"] = pltpu.VMEM((LAYERS, CAN, 1), f32)
    specs["active"] = pltpu.VMEM((LAYERS, BLOCKS, CAN, WIDE), bf16)
    specs["slope"] = pltpu.VMEM((LAYERS, BLOCKS, CAN, WIDE), f32)
    specs["taps"] = pltpu.VMEM((BLOCKS, 49, 8, LANES), f32)
    specs["wide7"] = pltpu.VMEM((7, 2, 104, WIDE), f32)
    specs["wide3"] = pltpu.VMEM((5, 3, 56, WIDE), f32)
    specs["place"] = pltpu.VMEM((CAN, ROWS_IMG), bf16)
    for name, dtype in (("work", f32), ("grads", f32), ("rel", bf16), ("gatt", bf16)):
        specs[name] = pltpu.VMEM((CAN, WIDE), dtype)
    count = len(chunk_list())
    copies = 11 + (many - 1)
    specs["weight_send"] = pltpu.SemaphoreType.DMA((8, 11))
    specs["weight_recv"] = pltpu.SemaphoreType.DMA((8, 11))
    specs["weight_own"] = pltpu.SemaphoreType.DMA((9,))
    specs["small_send"] = pltpu.SemaphoreType.DMA((3,))
    specs["small_recv"] = pltpu.SemaphoreType.DMA((3,))
    specs["grad_send"] = pltpu.SemaphoreType.DMA((count, copies))
    specs["grad_recv"] = pltpu.SemaphoreType.DMA((count, copies))
    specs["last_send"] = pltpu.SemaphoreType.DMA((3,))
    specs["last_recv"] = pltpu.SemaphoreType.DMA((3,))
    return {name: spec for name, spec in specs.items() if spec is not None}


INPUTS = (
    "geometry", "feats", "ograd", "same", "moves", "tap_mask", "lqkv", "lproj", "lfc1", "lfc2",
    "crpe", "head_bias", "fc1_bias", "cpe", "bias", "gain", "shift",
)
OUTPUTS = ("out", "fgrad", "rqkv", "rproj", "rfc1", "rfc2", "rrest", "rshared")


def target_rows(geometry):
    crops, sides, places = geometry[0:1] & 7, geometry[1:2], geometry[2:3]
    first = places == 0
    big = sides == 7
    code = crops + jnp.where(first, jnp.where(big, 8, 16), 0)
    square = (ROWS_IMG, ROWS_IMG)
    diagonal = lax.broadcasted_iota(jnp.int32, square, 0) == lax.broadcasted_iota(jnp.int32, square, 1)
    column = jnp.sum(jnp.where(diagonal, code.astype(f32), 0.0), axis=1, keepdims=True).astype(jnp.int32)
    earlier = (column & 7) < crops
    seven = jnp.sum(jnp.where(earlier & ((column & 8) > 0), 1.0, 0.0), axis=0, keepdims=True).astype(jnp.int32)
    three = jnp.sum(jnp.where(earlier & ((column & 16) > 0), 1.0, 0.0), axis=0, keepdims=True).astype(jnp.int32)
    cell = jnp.maximum(places - 1, 0)
    row = jnp.where(big, (cell * 37) >> 8, (cell * 43) >> 7)
    col = cell - row * sides
    in_seven = seven * 56 + row * 8 + col
    in_three = END7 + (three >> 1) * 24 + row * 8 + (three & 1) * 4 + col
    classes = END3 + jnp.where(big, seven, 2 + three)
    return jnp.where(first, classes, jnp.where(big, in_seven, in_three))


def step_kernel(many, names, *refs):
    r = types.SimpleNamespace(**dict(zip(names, refs)))
    links = Links(many)
    for layer in range(LAYERS):
        r.lsmall[layer, 0:49] = r.crpe[:, layer]
        r.lsmall[layer, 49:52] = r.head_bias[:, layer]
        for part in range(4):
            r.lsmall[layer, 52 + part : 53 + part] = r.fc1_bias[layer : layer + 1, part * LANES : (part + 1) * LANES]
    links.meet()
    small = Small(links, r.lsmall, r.small, r.small_send, r.small_recv, r.weight_own.at[8])
    small.start()
    weights = {}
    for place, kind in enumerate(KINDS):
        local, full = getattr(r, "l" + kind), getattr(r, "w" + kind)
        for layer in range(LAYERS):
            slot = place * LAYERS + layer
            weights[kind, layer] = Weights(
                links, local.at[layer], functools.partial(lambda full, layer, block: full.at[block, layer], full, layer),
                r.weight_send.at[slot], r.weight_recv.at[slot], r.weight_own.at[slot],
            )
    for layer in range(LAYERS):
        for kind in KINDS:
            weights[kind, layer].start()
            weights[kind, layer].start_near()
    gradients = {}
    for slot, (kind, layer, part) in enumerate(chunk_list()):
        tall, wide, dtype = chunk_shape(kind)
        if kind == "rest":
            full = lambda block: r.grest.at[block]
            result = r.rrest
        else:
            rows = part if kind == "qkv" else pl.ds(part * tall, tall)
            whole = getattr(r, "g" + kind)
            full = functools.partial(lambda whole, layer, rows, block: whole.at[block, layer, rows], whole, layer, rows)
            result = getattr(r, "r" + kind).at[layer, rows]
        gradients[kind, layer, part] = Gradient(
            links, full, *(getattr(r, name + str(slot), None) for name in ("core", "side", "half", "quad", "group")), result,
            r.grad_send.at[slot], r.grad_recv.at[slot],
        )

    def forward_point(layer, index):
        for item in FORWARD_ORDER.get((layer, index), ()):
            what, kind, which, part = item.split(".")
            getattr(weights[kind, int(which)], what)()
        if index == 0 and layer == 0:
            small.wait()
        if index in NEEDED:
            weights[NEEDED[index], layer].wait()

    def backward_point(layer, index):
        for item in BACKWARD_ORDER.get((layer, index), ()):
            what, kind, which, part = item.split(".")
            getattr(gradients[kind, int(which), int(part)], what)()

    r.wide7[...] = jnp.zeros_like(r.wide7)
    r.wide3[...] = jnp.zeros_like(r.wide3)
    r.grest[...] = jnp.zeros_like(r.grest)
    target = target_rows(r.geometry[...])
    r.place[...] = (lax.broadcasted_iota(jnp.int32, (CAN, ROWS_IMG), 0) == target).astype(f32).astype(bf16)
    r.streams[0] = mm(r.place[...], r.feats[...])
    r.grads[...] = mm(r.place[...], r.ograd[...])
    for layer in range(LAYERS):
        forward(r, layer, functools.partial(forward_point, layer))
    r.out[...] = mm_tn(r.place[...], r.streams[LAYERS].astype(bf16)).astype(bf16)
    for layer in reversed(range(LAYERS)):
        backward(r, layer, functools.partial(backward_point, layer))
    r.fgrad[...] = sum(mm_tn(r.place[...], part) for part in halves(r.grads[...]))
    backward_point(0, 9)
    r.rshared[links.block] = r.rrest[FIRST_SHARED : FIRST_SHARED + 32]
    mine = r.rshared.at[links.block]
    for slot, other in enumerate((links.by_core, links.by_side, links.by_far)):
        links.send(mine, mine, r.last_send.at[slot], r.last_recv.at[slot], other)
    for slot, block in enumerate((links.block_core, links.block_side, links.block_far)):
        links.arrived(r.rshared.at[block], r.last_send.at[slot], r.last_recv.at[slot])
    links.finish()


def forward(r, layer, point):
    real = real_rows()
    fill(halves(r.streams[layer]), 1, r.moves, r.wide7, r.wide3)
    for block in range(BLOCKS):
        lanes = lanes_of(block)
        spread_taps(r.taps, block, r.cpe[:, layer, lanes])
        conv = convolve(r.taps, block, 1, 1, 1, False, r.wide7, r.wide3)
        r.work[0:END3, lanes] = r.streams[layer, 0:END3, lanes] + conv + r.bias[0, layer : layer + 1, lanes]
        r.work[END3:CAN, lanes] = r.streams[layer, END3:CAN, lanes]
    unit, inverse, normed = norm_forward(r.work[...], r.gain[layer, 0:1], r.shift[layer, 0:1])
    r.unit1[layer] = unit
    r.inv1[layer] = inverse
    r.normed1[layer] = normed
    point(0)
    for block in range(BLOCKS):
        lanes = lanes_of(block)
        project = mm(normed, side_by_side(r.wqkv[block, layer]))
        r.queries[layer, :, lanes] = (project[:, :LANES] + r.small[block, layer, 49:50]).astype(bf16)
        r.values[layer, :, lanes] = (project[:, 2 * LANES :] + r.small[block, layer, 50:51]).astype(bf16)
        keys = project[:, LANES : 2 * LANES].astype(bf16).astype(f32)
        largest = jnp.max(jnp.where(real, keys, -1e30), axis=0, keepdims=True)
        exponent = jnp.exp(jnp.where(real, keys - largest, 0.0))
        exact = exponent / sum(mm(r.same[...], part) for part in halves(exponent))
        r.exacts[layer, :, lanes] = exact
        r.softs[layer, :, lanes] = exact.astype(bf16)
        spread_taps(r.taps, block, r.small[block, layer, 0:49] * r.tap_mask[block, 0:49])
    point(1)
    fill([r.values[layer]], 3, r.moves, r.wide7, r.wide3)
    for block in range(BLOCKS):
        lanes = lanes_of(block)
        query = r.queries[layer, :, lanes]
        soft = r.softs[layer, :, lanes]
        value = r.values[layer, :, lanes]
        factors = []
        for head in range(2):
            masked = jnp.where(head_lanes(head), query, jnp.zeros_like(query))
            mixing = (mm_nt(masked, soft) * SCALE * r.same[...].astype(f32)).astype(bf16)
            factors.append(mm(mixing, value))
        factor = jnp.where(head_lanes(0), factors[0], factors[1])
        conv = convolve(r.taps, block, REACH7[block], REACH3[block], 3, False, r.wide7, r.wide3) + r.small[block, layer, 51:52]
        r.convs[layer, 0:END3, lanes] = conv
        r.attended[layer, 0:END3, lanes] = (factor[0:END3] + query[0:END3].astype(f32) * conv).astype(bf16)
        r.attended[layer, END3:CAN, lanes] = factor[END3:CAN].astype(bf16)
        point(2 + block)
    after = r.work[...] + mm(r.attended[layer], r.wproj[:, layer].reshape(WIDE, WIDE)) + r.bias[1, layer : layer + 1]
    unit, inverse, normed = norm_forward(after, r.gain[layer, 1:2], r.shift[layer, 1:2])
    r.unit2[layer] = unit
    r.inv2[layer] = inverse
    r.normed2[layer] = normed
    r.work[...] = after + r.bias[2, layer : layer + 1]
    point(6)

    def feed(block, carry):
        hidden = mm(r.normed2[layer], r.wfc1[block, layer]) + jnp.concatenate(
            [r.small[block, layer, 52 + part : 53 + part] for part in range(4)], axis=1
        )
        chance = 0.5 * (1.0 + lax.erf(hidden * np.float32(0.5**0.5)))
        density = jnp.exp(hidden * hidden * -0.5) * np.float32((2 * np.pi) ** -0.5)
        r.slope[layer, block] = chance + hidden * density
        r.active[layer, block] = (hidden * chance).astype(bf16)
        return carry

    lax.fori_loop(0, BLOCKS, feed, 0)
    point(7)

    def collect(block, carry):
        r.work[...] += mm(r.active[layer, block], r.wfc2[block, layer])
        return carry

    lax.fori_loop(0, BLOCKS, collect, 0)
    r.streams[layer + 1] = r.work[...]
    point(8)


def backward(r, layer, point):
    def put_small(block, row, value):
        r.grest[block, 56 * layer + row : 56 * layer + row + value.shape[0]] = value

    def put_shared(row, value):
        for block in range(BLOCKS):
            first = FIRST_SHARED + 16 * layer + row
            r.grest[block, first : first + 1] = value[:, block * LANES : (block + 1) * LANES]

    put_shared(11, column_sum(r.grads[...]))
    r.work[...] = jnp.zeros_like(r.work)

    def feed(block, carry):
        grad_low = r.grads[...].astype(bf16)
        r.gfc2[block, layer] = mm_tn(r.active[layer, block], grad_low).astype(bf16)
        hidden = (mm_nt(grad_low, r.wfc2[block, layer]) * r.slope[layer, block]).astype(bf16)
        sums = column_sum(hidden.astype(f32))
        for part in range(4):
            row = 56 * layer + 52 + part
            r.grest[block, row : row + 1] = sums[:, part * LANES : (part + 1) * LANES]
        r.active[layer, block] = hidden
        return carry

    lax.fori_loop(0, BLOCKS, feed, 0)
    point(0)

    def collect(block, carry):
        hidden = r.active[layer, block]
        r.gfc1[block, layer] = mm_tn(r.normed2[layer], hidden).astype(bf16)
        r.work[...] += mm_nt(hidden, r.wfc1[block, layer])
        return carry

    lax.fori_loop(0, BLOCKS, collect, 0)
    point(1)
    incoming = r.work[...]
    unit = r.unit2[layer]
    put_shared(13, column_sum(incoming * unit))
    put_shared(15, column_sum(incoming))
    r.grads[...] = r.grads[...] + norm_backward(incoming, unit, r.inv2[layer], r.gain[layer, 1:2])
    branch = r.grads[...]
    put_shared(10, column_sum(branch))
    branch = branch.astype(bf16)
    r.gproj[:, layer] = mm_tn(r.attended[layer], branch).astype(bf16).reshape(BLOCKS, LANES, WIDE)
    r.gatt[...] = mm_nt(branch, r.wproj[:, layer].reshape(WIDE, WIDE)).astype(bf16)
    point(2)
    fill([r.values[layer]], 3, r.moves, r.wide7, r.wide3)
    for block in range(BLOCKS):
        lanes = lanes_of(block)
        product = r.gatt[0:END3, lanes].astype(f32) * r.queries[layer, 0:END3, lanes].astype(f32)
        r.rel[0:END3, lanes] = product.astype(bf16)
        r.rel[END3:CAN, lanes] = jnp.zeros((CAN - END3, LANES), bf16)
        put_small(block, 51, column_sum(product))
        sums = tap_grads(product, block, REACH7[block], REACH3[block], 3, r.taps, r.wide7, r.wide3)
        put_small(block, 0, sums * r.tap_mask[block, 0:49])
        spread_taps(r.taps, block, r.small[block, layer, 0:49] * r.tap_mask[block, 0:49])
    point(3)
    fill([r.rel[...]], 3, r.moves, r.wide7, r.wide3)
    r.work[...] = jnp.zeros_like(r.work)
    for block in range(BLOCKS):
        lanes = lanes_of(block)
        query = r.queries[layer, :, lanes]
        soft = r.softs[layer, :, lanes]
        value = r.values[layer, :, lanes]
        grad = r.gatt[:, lanes]
        exact = r.exacts[layer, :, lanes]
        picked = []
        for head in range(2):
            chosen = head_lanes(head)
            zero = jnp.zeros_like(query)
            query_head = jnp.where(chosen, query, zero)
            grad_head = jnp.where(chosen, grad, zero)
            same_low = r.same[...]
            mixing_t = (mm_nt(soft, query_head) * SCALE * same_low.astype(f32)).astype(bf16)
            mix = mm_nt(grad_head, value).astype(bf16) * same_low
            mix_t = mm_nt(value, grad_head).astype(bf16) * same_low
            picked.append((mm(mixing_t, grad), SCALE * mm(mix, soft), SCALE * mm(mix_t, query)))
        grad_value, grad_query, grad_soft = (
            jnp.where(head_lanes(0), one, two) for one, two in zip(*picked)
        )
        grad_soft = grad_soft.astype(bf16).astype(f32)
        weighted = grad_soft * exact
        grad_key = weighted - exact * sum(mm(r.same[...], part) for part in halves(weighted))
        conv = convolve(r.taps, block, REACH7[block], REACH3[block], 3, True, r.wide7, r.wide3)
        grad_value = jnp.concatenate([grad_value[0:END3] + conv, grad_value[END3:CAN]], axis=0).astype(bf16)
        grad_query = jnp.concatenate(
            [grad_query[0:END3] + grad[0:END3].astype(f32) * r.convs[layer, 0:END3, lanes], grad_query[END3:CAN]], axis=0
        ).astype(bf16)
        put_small(block, 49, column_sum(grad_query.astype(f32)))
        put_small(block, 50, column_sum(grad_value.astype(f32)))
        joined = jnp.concatenate([grad_query, grad_key.astype(bf16), grad_value], axis=1)
        product = mm_tn(r.normed1[layer], joined).astype(bf16)
        for part in range(3):
            r.gqkv[block, layer, part] = product[:, part * LANES : (part + 1) * LANES]
        r.work[...] += mm_nt(joined, side_by_side(r.wqkv[block, layer]))
        point(4 + block)
    incoming = r.work[...]
    unit = r.unit1[layer]
    put_shared(12, column_sum(incoming * unit))
    put_shared(14, column_sum(incoming))
    r.grads[...] = r.grads[...] + norm_backward(incoming, unit, r.inv1[layer], r.gain[layer, 0:1])
    fill(halves(r.streams[layer]), 1, r.moves, r.wide7, r.wide3)
    for block in range(BLOCKS):
        lanes = lanes_of(block)
        product = r.grads[0:END3, lanes]
        first = FIRST_SHARED + 16 * layer
        r.grest[block, first + 9 : first + 10] = column_sum(product)
        r.grest[block, first : first + 9] = tap_grads(product, block, 1, 1, 1, r.taps, r.wide7, r.wide3)
    fill(halves(r.grads[...]), 1, r.moves, r.wide7, r.wide3)
    for block in range(BLOCKS):
        lanes = lanes_of(block)
        spread_taps(r.taps, block, r.cpe[:, layer, lanes])
        conv = convolve(r.taps, block, 1, 1, 1, True, r.wide7, r.wide3)
        r.grads[0:END3, lanes] = r.grads[0:END3, lanes] + conv
    point(8)


def finish_kernel(
    rqkv, rproj, rfc1, rfc2, rrest, rshared, out_in, fgrad_in,
    out, fgrad, cpe, bias, gain, shift, qkv, head_bias, crpe, proj, fc1, fc1_bias, fc2,
):
    qkv[...] = rqkv[...].astype(f32)
    proj[...] = rproj[...].astype(f32)
    fc1[...] = rfc1[...].astype(f32)
    fc2[...] = rfc2[...].astype(f32)
    out[...] = out_in[...]
    fgrad[...] = fgrad_in[...]

    @pl.when(pl.program_id(0) == 0)
    def small():
        for layer in range(LAYERS):
            for block in range(BLOCKS):
                lanes = lanes_of(block)
                first = layer * 16
                cpe[:, layer, lanes] = rshared[block, first : first + 9]
                bias[:, layer, lanes] = rshared[block, first + 9 : first + 12]
                gain[layer, :, lanes] = rshared[block, first + 12 : first + 14]
                shift[layer, :, lanes] = rshared[block, first + 14 : first + 16]
                fc1_bias[layer : layer + 1, lanes] = rrest[layer * 56 + 52 + block : layer * 56 + 53 + block]
            crpe[:, layer] = rrest[layer * 56 : layer * 56 + 49]
            head_bias[:, layer] = rrest[layer * 56 + 49 : layer * 56 + 52]


def shards(
    data, features, crop_index, grid_size, position, cpe_weight, shared_bias, norm_gain, norm_bias,
    qkv_weight, head_bias, crpe_weight, proj_weight, fc1_weight, fc1_bias, fc2_weight, out_grad,
):
    assert data % 8 == 0 and features.shape[0] == ROWS_IMG
    many = data // 8
    start = lax.axis_index("mp") * ROWS_IMG
    geometry = lax.dynamic_slice(jnp.stack([crop_index, grid_size, position]), (0, start), (3, ROWS_IMG))
    same, moves = canonical_tables()
    swap = lambda item: jnp.transpose(item, (1, 0, 2))
    vmem = pl.BlockSpec(memory_space=pltpu.VMEM)
    hbm = pl.BlockSpec(memory_space=pl.ANY)
    shape = jax.ShapeDtypeStruct
    specs = scratch_specs(many)
    results = pl.pallas_call(
        functools.partial(step_kernel, many, INPUTS + OUTPUTS + tuple(specs)),
        out_shape=(
            shape((ROWS_IMG, WIDE), bf16),
            shape((ROWS_IMG, WIDE), f32),
            *(shape((LAYERS, *SHAPES[kind]), bf16) for kind in KINDS),
            shape((REST, LANES), f32),
            shape((BLOCKS, 32, LANES), f32),
        ),
        in_specs=[hbm if name in ("lqkv", "lproj", "lfc1", "lfc2") else vmem for name in INPUTS],
        out_specs=(vmem,) * len(OUTPUTS),
        scratch_shapes=list(specs.values()),
        compiler_params=pltpu.CompilerParams(
            vmem_limit_bytes=63 * 2**20, collective_id=0, has_side_effects=True
        ),
        name="step",
    )(
        geometry, features, out_grad, jnp.asarray(same, bf16), jnp.asarray(moves, bf16), jnp.asarray(tap_table()),
        jnp.transpose(qkv_weight, (0, 2, 1, 3)), proj_weight, fc1_weight, fc2_weight, swap(crpe_weight), swap(head_bias),
        fc1_bias, swap(cpe_weight), swap(shared_bias), norm_gain, norm_bias,
    )
    out, fgrad, rqkv, rproj, rfc1, rfc2, rrest, rshared = results
    steps = 4
    taken = (rqkv, rproj, rfc1, rfc2, rrest, rshared, out, fgrad)
    swapped = lambda item: (item.shape[1], item.shape[0], item.shape[2])
    given = (
        (out.shape, bf16),
        (fgrad.shape, f32),
        (swapped(cpe_weight), f32),
        (swapped(shared_bias), f32),
        (norm_gain.shape, f32),
        (norm_bias.shape, f32),
        (rqkv.shape, f32),
        (swapped(head_bias), f32),
        (swapped(crpe_weight), f32),
        (rproj.shape, f32),
        (rfc1.shape, f32),
        (fc1_bias.shape, f32),
        (rfc2.shape, f32),
    )
    cut = {out.shape, rqkv.shape, rproj.shape, rfc1.shape}

    def spec(dims):
        split = dims in cut
        block = (*dims[:-2], dims[-2] // steps, dims[-1]) if split else dims
        return pl.BlockSpec(block, lambda step: (*(0 for _ in dims[:-2]), step if split else 0, 0))

    final = list(
        pl.pallas_call(
            finish_kernel,
            grid=(steps,),
            out_shape=tuple(shape(dims, dtype) for dims, dtype in given),
            in_specs=[spec(item.shape) for item in taken],
            out_specs=tuple(spec(dims) for dims, dtype in given),
            compiler_params=pltpu.CompilerParams(vmem_limit_bytes=63 * 2**20),
            name="finish",
        )(*taken)
    )
    for index in (2, 3, 7, 8):
        final[index] = swap(final[index])
    final[6] = jnp.transpose(final[6], (0, 2, 1, 3))
    return tuple(final)


def solution(mesh):
    placed = (
        P(("dp", "mp"), None),
        P("dp"),
        P("dp"),
        P("dp"),
        P(),
        P(),
        P(),
        P(),
        P(None, None, None, "mp"),
        P(None, None, "mp"),
        P(None, None, "mp"),
        P(None, "mp", None),
        P(None, None, "mp"),
        P(None, "mp"),
        P(None, "mp", None),
        P(("dp", "mp"), None),
    )
    return jax.shard_map(
        functools.partial(shards, mesh.shape["dp"]),
        mesh=mesh,
        in_specs=placed,
        out_specs=(
            P(("dp", "mp"), None),
            P(("dp", "mp"), None),
            P(),
            P(),
            P(),
            P(),
            P(None, None, None, "mp"),
            P(None, None, "mp"),
            P(None, None, "mp"),
            P(None, "mp", None),
            P(None, None, "mp"),
            P(None, "mp"),
            P(None, "mp", None),
        ),
        check_vma=False,
    )
```

```python
import functools
import types

import jax
import jax.numpy as jnp
import numpy as np
from jax import lax
from jax.experimental import pallas as pl
from jax.experimental.pallas import tpu as pltpu
from jax.sharding import PartitionSpec as P

HD = 64
LAYERS = 2
ROWS_IMG = 160
CAN = 192
END7 = 112
END3 = 184
LANES = 128
WIDE = 512
BLOCKS = 4
SLOT = (0, 2, 1, 3)
EPSILON = 1e-06
SCALE = HD ** (-0.5)
REACH7 = (1, 2, 3, 3)
REACH3 = (1, 2, 2, 2)
MESH = pl.DeviceIdType.MESH
f32 = jnp.float32
bf16 = jnp.bfloat16


def canonical_tables():
    crop = np.full(CAN, 100)
    col = np.full(CAN, -1)
    side = np.zeros(CAN, int)
    for t in range(END7):
        if t % 8 < 7:
            crop[t], col[t], side[t] = t // 56, t % 8, 7
    for t in range(END7, END3):
        u = t - END7
        if t % 4 < 3:
            crop[t], col[t], side[t] = 2 + 2 * (u // 24) + (t % 8) // 4, t % 4, 3
    for t in range(END3, CAN):
        crop[t] = t - END3
    same = (crop[:, None] == crop[None, :]).astype(np.float32)
    moves = np.zeros((7, CAN, CAN), np.float32)
    for b in range(-3, 4):
        for t in range(END3):
            if col[t] >= 0 and 0 <= col[t] + b < side[t]:
                moves[b + 3, t, t + b] = 1
    return same, moves


def tap_table():
    table = np.zeros((BLOCKS, 56, LANES), np.float32)
    for channel in range(WIDE):
        head = channel // HD
        reach = 1 if head < 2 else 2 if head < 5 else 3
        for tap in range(49):
            if max(abs(tap // 7 - 3), abs(tap % 7 - 3)) <= reach:
                table[channel // LANES, tap, channel % LANES] = 1
    return table


def mm(left, right):
    return jnp.dot(left, right, preferred_element_type=f32)


def mm_nt(left, right):
    return lax.dot_general(left, right, (((1,), (1,)), ((), ())), preferred_element_type=f32)


def mm_tn(left, right):
    return lax.dot_general(left, right, (((0,), (0,)), ((), ())), preferred_element_type=f32)


def side_by_side(parts):
    return jnp.concatenate([parts[index] for index in range(parts.shape[0])], axis=1)


def halves(values):
    high = values.astype(bf16)
    return [high, (values - high.astype(f32)).astype(bf16)]


def lanes_of(block):
    return pl.ds(block * LANES, LANES)


def column_sum(values):
    return jnp.sum(values, axis=0, keepdims=True)


def fill(parts, reach, moves, wide7, wide3):
    for b in range(-reach, reach + 1):
        moved = sum(mm(moves[b + 3], part) for part in parts)
        for grid in range(2):
            wide7[b + 3, grid, 24:80] = moved[grid * 56 : grid * 56 + 56]
        if abs(b) <= 2:
            for pair in range(3):
                first = END7 + pair * 24
                wide3[b + 2, pair, 16:40] = moved[first : first + 24]


def tap_row(a, b, half, flip):
    if flip:
        a, b = -a, -b
    return (a + half) * (2 * half + 1) + b + half


def spread_taps(spread, block, rows):
    for row in range(rows.shape[0]):
        spread[block, row] = jnp.broadcast_to(rows[row : row + 1], (8, LANES))


def convolve(spread, block, reach7, reach3, half, flip, wide7, wide3):
    lanes = lanes_of(block)

    def loop(wide, offset, reach, grids, tall):
        def body(step, acc):
            b = step - reach
            for a in range(-reach, reach + 1):
                weight = spread[block, tap_row(a, b, half, flip)]
                seen = wide[b + offset, :, pl.ds((a + offset) * 8, tall), lanes]
                acc = acc + weight * seen.reshape(-1, 8, LANES)
            return acc

        return lax.fori_loop(0, 2 * reach + 1, body, jnp.zeros((grids * tall // 8, 8, LANES), f32))

    acc7 = loop(wide7, 3, reach7, 2, 56)
    acc3 = loop(wide3, 2, reach3, 3, 24)
    return jnp.concatenate([acc7.reshape(END7, LANES), acc3.reshape(END3 - END7, LANES)], axis=0)


def tap_grads(grad, block, reach7, reach3, half, spread, wide7, wide3):
    lanes = lanes_of(block)
    count = (2 * half + 1) ** 2
    grad7 = grad[:END7].reshape(-1, 8, LANES)
    grad3 = grad[END7:END3].reshape(-1, 8, LANES)
    spread[block, 0:count] = jnp.zeros((count, 8, LANES), f32)

    def loop(wide, offset, reach, part, tall):
        def body(step, carry):
            b = step - reach
            for a in range(-reach, reach + 1):
                seen = wide[b + offset, :, pl.ds((a + offset) * 8, tall), lanes]
                row = tap_row(a, b, half, False)
                spread[block, row] += jnp.sum(part * seen.reshape(-1, 8, LANES), axis=0)
            return carry

        lax.fori_loop(0, 2 * reach + 1, body, 0)

    loop(wide7, 3, reach7, grad7, 56)
    loop(wide3, 2, reach3, grad3, 24)
    return jnp.sum(spread[block, 0:count], axis=1)


def norm_forward(values, gain, bias):
    center = values - jnp.mean(values, axis=-1, keepdims=True)
    spread = jnp.mean(center * center, axis=-1, keepdims=True)
    inverse = lax.rsqrt(spread + EPSILON)
    unit = center * inverse
    return unit, inverse, (unit * gain + bias).astype(bf16)


def norm_backward(incoming, unit, inverse, gain):
    scaled = incoming * gain
    mean_one = jnp.mean(scaled, axis=-1, keepdims=True)
    mean_two = jnp.mean(scaled * unit, axis=-1, keepdims=True)
    return inverse * (scaled - mean_one - unit * mean_two)


def real_rows():
    row = lax.broadcasted_iota(jnp.int32, (CAN, LANES), 0)
    seven = (row < END7) & ((row & 7) != 7)
    three = (row >= END7) & (row < END3) & ((row & 3) != 3)
    return seven | three | (row >= END3)


def head_lanes(head):
    lane = lax.broadcasted_iota(jnp.int32, (CAN, LANES), 1)
    return (lane >= HD) if head else (lane < HD)


def rows_of(ref, start, count):
    rows = pl.ds(pl.multiple_of(start, 8), count)
    return ref.at[rows] if len(ref.shape) == 2 else ref.at[:, rows]


def add_rows(target, start, source, first, count):
    step = next(size for size in (64, 48, 32, 24, 16, 8) if count % size == 0)

    def body(index, carry):
        into = pl.ds(pl.multiple_of(start + index * step, 8), step)
        target[into] = target[into] + source[pl.ds(pl.multiple_of(first + index * step, 8), step)]
        return carry

    lax.fori_loop(0, count // step, body, 0)


class Links:
    def __init__(self, many):
        dp, mp = lax.axis_index("dp"), lax.axis_index("mp")
        self.many = many
        self.core, self.side = lax.rem(mp, 2), lax.div(mp, 2)
        self.half, self.quad, self.group = lax.rem(dp, 2), lax.rem(lax.div(dp, 2), 4), lax.div(dp, 8)
        self.block = self.core * 2 + self.side
        self.block_core = (1 - self.core) * 2 + self.side
        self.block_side = self.core * 2 + 1 - self.side
        self.block_far = (1 - self.core) * 2 + 1 - self.side
        self.by_core = (dp, self.side * 2 + 1 - self.core)
        self.by_side = (dp, (1 - self.side) * 2 + self.core)
        self.by_far = (dp, (1 - self.side) * 2 + 1 - self.core)
        self.by_half = (dp + 1 - 2 * self.half, mp)
        self.by_quad = [
            (self.group * 8 + lax.rem(self.quad + step, 4) * 2 + self.half, mp) for step in range(1, 4)
        ]
        self.rounds = many.bit_length() - 1
        self.by_group = []
        for step in range(self.rounds):
            bit = lax.rem(lax.div(self.group, 1 << step), 2)
            partner = self.group + (1 - 2 * bit) * (1 << step)
            self.by_group.append((partner * 8 + self.quad * 2 + self.half, mp))
        self.pair = lax.rem(self.quad, 2)
        self.by_pair = (self.group * 8 + (self.quad + 1 - 2 * self.pair) * 2 + self.half, mp)
        self.pools = {}

    def meet(self):
        barrier = pltpu.get_barrier_semaphore()
        others = [self.by_core, self.by_side, self.by_far, self.by_half] + self.by_quad + self.by_group
        for other in others:
            pl.semaphore_signal(barrier, inc=1, device_id=other, device_id_type=MESH)
        pl.semaphore_wait(barrier, len(others))

    def pool(self, name, sems):
        self.pools[name] = [sems, [None] * sems.shape[0], 0]

    def take(self, name, waiter):
        sems, waiters, place = self.pools[name]
        if waiters[place] is not None:
            waiters[place]()
        waiters[place] = waiter
        self.pools[name][2] = (place + 1) % len(waiters)
        return sems.at[place]

    def copy(self, source, target, send_sem, recv_sem, other):
        return pltpu.make_async_remote_copy(
            src_ref=source, dst_ref=target, send_sem=send_sem, recv_sem=recv_sem, device_id=other, device_id_type=MESH
        )

    def send(self, name, items, recv_sem, whole=None):
        box = []
        send_sem = self.take(name, lambda: box[0].wait_send())
        copies = [self.copy(source, target, send_sem, recv_sem, other) for source, target, other in items]
        box.append(copies[0] if whole is None else self.copy(whole, whole, send_sem, recv_sem, self.by_core))
        for copy in copies:
            copy.start()

    def arrived(self, target, recv_sem):
        self.copy(target, target, recv_sem, recv_sem, self.by_core).wait_recv()

    def finish(self):
        for sems, waiters, place in self.pools.values():
            for waiter in waiters:
                if waiter is not None:
                    waiter()


class Weights:
    def __init__(self, links, local, full, recv_sems, own_sem, direct):
        self.links, self.local, self.full, self.direct = links, local, full, direct
        self.recv_sems, self.own_sem = recv_sems, own_sem
        self.count = local.shape[-2] // 4
        self.sub = self.count // 2

    def start_of(self, half, pair):
        return (half * 2 + pair) * self.count

    def places(self):
        links = self.links
        far = self.start_of(1 - links.half, 1 - links.pair)
        near = (
            (self.start_of(links.half, links.pair), self.count),
            (self.start_of(1 - links.half, links.pair), self.count),
            (self.start_of(links.half, 1 - links.pair), self.count),
        )
        return near + (((far, self.count),) if self.direct else ((far + self.sub, self.sub), (far, self.sub)))

    def push(self, part, slot, other):
        self.links.send("weights", [(part, part, other)], self.recv_sems.at[slot])

    def take(self, index):
        start, count = self.places()[index]
        part = rows_of(self.full(self.links.block_side), start, count)
        self.links.arrived(part, self.recv_sems.at[index])
        self.push(part, 5, self.links.by_core)
        return part

    def start(self):
        links = self.links
        for index in (0, 3) if self.direct else (0,):
            start, count = self.places()[index]
            target = rows_of(self.full(links.block), start, count)
            links.send("weights", [(rows_of(self.local, start, count), target, links.by_side)], self.recv_sems.at[index])

    def start_near(self):
        links = self.links
        links.send("weights", [(self.local, self.full(links.block), links.by_core)], self.recv_sems.at[5])
        self.own = pltpu.make_async_copy(self.local, self.full(links.block), self.own_sem)
        self.own.start()

    def F1(self):
        part = self.take(0)
        self.push(part, 1, self.links.by_half)
        self.push(part, 2, self.links.by_pair)

    def Y1(self):
        part = self.take(1)
        if not self.direct:
            self.push(rows_of(part, 0, self.sub), 4, self.links.by_pair)

    def Z1(self):
        part = self.take(2)
        if not self.direct:
            self.push(rows_of(part, self.sub, self.sub), 3, self.links.by_half)

    def YD(self):
        self.take(3)

    def ZD(self):
        self.take(4)

    def XD(self):
        self.take(3)

    def wait(self):
        self.own.wait()
        self.links.arrived(self.full(pl.ds((1 - self.links.core) * 2, 2)), self.recv_sems.at[5])


class Small:
    def __init__(self, links, local, full, recv_sems, own_sem):
        self.links, self.local, self.full, self.recv_sems, self.own_sem = links, local, full, recv_sems, own_sem

    def start(self):
        links = self.links
        for slot, other in enumerate((links.by_side, links.by_core)):
            links.send("weights", [(self.local, self.full.at[links.block], other)], self.recv_sems.at[slot])
        self.own = pltpu.make_async_copy(self.local, self.full.at[links.block], self.own_sem)
        self.own.start()

    def wait(self):
        links = self.links
        part = self.full.at[links.block_side]
        links.arrived(part, self.recv_sems.at[0])
        links.send("weights", [(part, part, links.by_core)], self.recv_sems.at[2])
        self.own.wait()
        links.arrived(self.full.at[links.block_core], self.recv_sems.at[1])
        links.arrived(self.full.at[links.block_far], self.recv_sems.at[2])


class Gradient:
    def __init__(self, links, full, core_in, side_in, half_in, quad_in, group_in, result, final, recv_sems):
        self.links, self.full, self.result, self.final = links, full, result, final
        self.core_in, self.side_in, self.half_in, self.quad_in, self.group_in = core_in, side_in, half_in, quad_in, group_in
        self.recv_sems = recv_sems
        self.tall = result.shape[0]
        self.half, self.piece = self.tall // 2, self.tall // 8
        self.here, self.there = links.half * self.half, (1 - links.half) * self.half
        self.mine = self.here + links.quad * self.piece

    def CS(self):
        links = self.links
        source = self.full(pl.ds((1 - links.core) * 2, 2))
        links.send("core", [(source, self.core_in, links.by_core)], self.recv_sems.at[0])

    def CX(self):
        links = self.links
        links.arrived(self.core_in, self.recv_sems.at[0])
        part = self.full(links.block_side)
        add_rows(part, 0, self.core_in.at[1 - links.side], 0, self.tall)
        links.send("side", [(part, self.side_in, links.by_side)], self.recv_sems.at[1])

    def CO(self):
        links = self.links
        add_rows(self.full(links.block), 0, self.core_in.at[links.side], 0, self.tall)

    def XA(self):
        links = self.links
        links.arrived(self.side_in, self.recv_sems.at[1])
        total = self.full(links.block)
        add_rows(total, self.there, self.side_in, self.there, self.half)
        links.send("half", [(rows_of(total, self.there, self.half), self.half_in, links.by_half)], self.recv_sems.at[2])
        add_rows(total, self.here, self.side_in, self.here, self.half)

    def YA(self):
        links = self.links
        links.arrived(self.half_in, self.recv_sems.at[2])
        total = self.full(links.block)
        add_rows(total, self.here, self.half_in, 0, self.half)
        items = []
        for step in range(3):
            start = self.here + lax.rem(links.quad + step + 1, 4) * self.piece
            items.append((rows_of(total, start, self.piece), self.quad_in.at[step], links.by_quad[step]))
        links.send("quad", items, self.recv_sems.at[3], self.quad_in)

    def ZA(self):
        links = self.links
        mine = pl.ds(pl.multiple_of(self.mine, 8), self.piece)
        total = self.full(links.block)
        links.arrived(self.quad_in, self.recv_sems.at[3])
        value = total[mine].astype(f32)
        for step in range(3):
            value = value + self.quad_in[step].astype(f32)
        if links.many > 1:
            for step in range(links.rounds):
                total[mine] = value.astype(total.dtype)
                copy = links.copy(
                    total.at[mine], self.group_in.at[step], links.group_send.at[step], self.recv_sems.at[6 + step],
                    links.by_group[step],
                )
                copy.start()
                copy.wait()
                value = total[mine].astype(f32) + self.group_in[step].astype(f32)
        part = self.result.at[mine]
        part[...] = value.astype(self.result.dtype)
        links.send("spread", [(part, part, other) for other in links.by_quad], self.recv_sems.at[4], self.quad_in)

    def ZF(self):
        links = self.links
        links.arrived(self.quad_in, self.recv_sems.at[4])
        part = rows_of(self.result, self.here, self.half)
        links.send("share", [(part, part, links.by_half)], self.recv_sems.at[5])

    def FN(self):
        self.links.arrived(rows_of(self.result, self.there, self.half), self.recv_sems.at[5])
        self.final()


ORDER = {
    (0, 0, 0): (
        0, 100, 200, 1000, 2000, 1100, 2100, 300, 10, 1200, 2200, 110, 3000, 4000,
    ),
    (0, 0, 1): (210, 1300, 2300, 3100, 4100,),
    (0, 0, 2): (310, 1010, 2010,),
    (0, 0, 3): (3200, 4200,),
    (0, 0, 4): (1110, 2110,),
    (0, 0, 7): (1210, 2210, 3300, 4300,),
    (0, 1, 0): (1310, 2310, 3010, 4010, 3110, 4110,),
    (0, 1, 1): (3210, 4210, 4310, 3310,),
    (1, 1, 0): (6310,),
    (1, 1, 1): (6311,),
    (1, 1, 2): (6312,),
    (1, 1, 3): (6313,),
    (1, 1, 4): (7310, 7311, 8310, 8311,),
    (1, 1, 5): (7312, 8312, 7313, 6210, 8313,),
    (1, 1, 6): (6211,),
    (1, 1, 7): (6212,),
    (1, 1, 8): (6213,),
    (1, 1, 9): (7210, 7211, 7212, 7213, 9310, 8210, 8211, 8212, 8213, 6110,),
    (1, 1, 10): (7110, 9311, 10310, 8110,),
    (1, 1, 11): (9312,),
    (1, 1, 13): (9313, 10311, 11310,),
    (1, 1, 14): (10312, 6010, 6011, 6012, 9210,),
    (1, 1, 15): (10313, 7010, 11311, 8010, 7011, 9211, 12310, 7012, 8011, 8012, 10210,),
    (1, 0, 0): (11312, 6300,),
    (1, 0, 1): (6301,),
    (1, 0, 2): (9212, 11313, 6302,),
    (1, 0, 3): (10211, 6303,),
    (1, 0, 4): (
        7300, 7301, 9213, 7302, 11210, 12311, 8300, 8301, 8302, 7303, 10212, 8303, 12312, 13310,
    ),
    (1, 0, 5): (6200,),
    (1, 0, 6): (9110, 6201, 12313,),
    (1, 0, 7): (6202, 10213,),
    (1, 0, 8): (11211, 7200, 6203, 8200,),
    (1, 0, 9): (
        7201, 7202, 7203, 9010, 11212, 12210, 10110, 8201, 8202, 9011, 11213, 8203, 13311, 13312, 6100,
    ),
    (1, 0, 10): (7100, 9012, 10010, 12211, 12212, 8100, 13313, 13210,),
    (1, 0, 11): (11110, 9300, 10011, 12213,),
    (1, 0, 12): (10012, 11010,),
    (1, 0, 13): (9301, 12110, 13211,),
    (1, 0, 14): (11011, 13212, 6000, 6001, 6002, 9302,),
    (1, 0, 15): (10300, 11012, 12010, 13213,),
    (1, 0, 16): (6400,),
    (2, 0, 0): (
        9303, 10301, 12011, 13110, 7400, 7000, 7001, 7002, 9200, 10302, 11300, 8000, 8001, 8002, 8400, 12012, 13010, 9201,
        11301, 10303, 11302, 13011, 9202, 12300, 10200, 12301, 13012, 9203, 11303, 10201, 12302, 10202, 9100, 11200, 13300, 12303,
        13301, 9400, 11201, 10203, 11202, 13302, 9000, 12200, 10100, 12201, 13303, 9001, 10400, 11203, 10000, 12202, 9002, 13200,
        11100, 11400, 13201, 12203, 10001, 11000, 13202, 12100, 10002, 12400, 13203, 11001, 13100, 12000, 13400, 11002, 12001, 13000,
        12002, 13001, 13002,
    ),
}
NEEDED = {0: "qkv", 5: "proj", 6: "fc1", 7: "fc2"}
DIRECT = ()
KINDS = ("qkv", "proj", "fc1", "fc2")
SHAPES = {"qkv": (3, WIDE, LANES), "proj": (LANES, WIDE), "fc1": (WIDE, WIDE), "fc2": (WIDE, WIDE)}
GRADS = SHAPES | {"fc1": (4, WIDE, LANES)}
CHUNKS = {"qkv": 3, "proj": 1, "fc1": 4, "fc2": 4}
REST = 192
FIRST_SHARED = 112


def chunk_list():
    names = [(kind, layer, part) for kind in KINDS for layer in range(LAYERS) for part in range(CHUNKS[kind])]
    return names + [("rest", 0, 0)]


def chunk_shape(kind):
    if kind == "rest":
        return REST, LANES, f32
    if kind in ("qkv", "fc1"):
        return WIDE, LANES, bf16
    tall, wide = SHAPES[kind]
    return tall // CHUNKS[kind], wide, bf16


POOLS = (
    ("weights", 80), ("core", 8), ("side", 16), ("half", 16), ("quad", 16), ("spread", 16), ("share", 16), ("last", 3),
)


def scratch_specs(many, loaded):
    rows = lambda kind: pltpu.VMEM((LAYERS, CAN, WIDE), kind)
    specs = {}
    for kind in KINDS:
        specs["w" + kind] = pltpu.VMEM((BLOCKS, LAYERS, *SHAPES[kind]), bf16)
        specs["g" + kind] = pltpu.VMEM((BLOCKS, LAYERS, *GRADS[kind]), bf16)
    specs["small"] = pltpu.VMEM((BLOCKS, LAYERS, 56, LANES), f32)
    specs["lsmall"] = pltpu.VMEM((LAYERS, 56, LANES), f32)
    specs["grest"] = pltpu.VMEM((BLOCKS, REST, LANES), f32)
    for slot, (kind, layer, part) in enumerate(chunk_list()):
        tall, wide, dtype = chunk_shape(kind)
        specs[f"core{slot}"] = pltpu.VMEM((2, tall, wide), dtype)
        specs[f"side{slot}"] = pltpu.VMEM((tall, wide), dtype)
        specs[f"half{slot}"] = pltpu.VMEM((tall // 2, wide), dtype)
        specs[f"quad{slot}"] = pltpu.VMEM((3, tall // 8, wide), dtype)
        specs[f"group{slot}"] = pltpu.VMEM((many.bit_length() - 1, tall // 8, wide), dtype) if many > 1 else None
    for name, dtype in (
        ("unit1", f32), ("normed1", bf16), ("queries", bf16), ("softs", bf16), ("exacts", f32), ("values", bf16),
        ("convs", f32), ("attended", bf16), ("unit2", f32), ("normed2", bf16),
    ):
        specs[name] = rows(dtype)
    specs["streams"] = pltpu.VMEM((LAYERS + 1, CAN, WIDE), f32)
    specs["inv1"] = pltpu.VMEM((LAYERS, CAN, 1), f32)
    specs["inv2"] = pltpu.VMEM((LAYERS, CAN, 1), f32)
    specs["active"] = pltpu.VMEM((LAYERS, BLOCKS, CAN, WIDE), bf16)
    specs["slope"] = pltpu.VMEM((LAYERS, BLOCKS, CAN, WIDE), f32)
    specs["taps"] = pltpu.VMEM((BLOCKS, 49, 8, LANES), f32)
    specs["wide7"] = pltpu.VMEM((7, 2, 104, WIDE), f32)
    specs["wide3"] = pltpu.VMEM((5, 3, 56, WIDE), f32)
    specs["place"] = pltpu.VMEM((CAN, ROWS_IMG), bf16)
    for name, dtype in (("work", f32), ("grads", f32), ("rel", bf16), ("gatt", bf16)):
        specs[name] = pltpu.VMEM((CAN, WIDE), dtype)
    specs["low"] = pltpu.VMEM((CAN, WIDE), bf16)
    specs["hidden"] = pltpu.VMEM((BLOCKS, CAN, WIDE), bf16)
    specs["out"] = pltpu.VMEM((ROWS_IMG, WIDE), bf16)
    specs["fgrad"] = pltpu.VMEM((ROWS_IMG, WIDE), f32)
    for kind in KINDS:
        specs["r" + kind] = pltpu.VMEM((LAYERS, *GRADS[kind]), bf16)
    specs["rrest"] = pltpu.VMEM((REST, LANES), f32)
    specs["rshared"] = pltpu.VMEM((BLOCKS, 32, LANES), f32)
    for name, item in loaded.items():
        specs[name] = pltpu.VMEM(item.shape, item.dtype)
    specs["load_sems"] = pltpu.SemaphoreType.DMA((len(loaded),))
    specs["store_sems"] = pltpu.SemaphoreType.DMA((3,))
    count = len(chunk_list())
    specs["final_sems"] = pltpu.SemaphoreType.DMA((9,))
    specs["weight_recv"] = pltpu.SemaphoreType.DMA((8, 6))
    specs["weight_own"] = pltpu.SemaphoreType.DMA((9,))
    specs["small_recv"] = pltpu.SemaphoreType.DMA((3,))
    specs["grad_recv"] = pltpu.SemaphoreType.DMA((count, 5 + many.bit_length()))
    if many > 1:
        specs["group_send"] = pltpu.SemaphoreType.DMA((many.bit_length() - 1,))
    specs["last_recv"] = pltpu.SemaphoreType.DMA((3,))
    for name, size in POOLS:
        specs["send_" + name] = pltpu.SemaphoreType.DMA((size,))
    return {name: spec for name, spec in specs.items() if spec is not None}


INPUTS = (
    "geometry", "crpe", "head_bias", "fc1_bias", "feats", "ograd", "same", "moves", "tap_mask", "cpe", "bias", "gain", "shift",
)
SHARDS = ("lqkv", "lproj", "lfc1", "lfc2")
OUTPUTS = ("out", "fgrad", "rqkv", "rproj", "rfc1", "rfc2", "rrest", "rshared")
STEPS = (
    Weights.F1, Weights.Y1, Weights.Z1, Weights.YD, Weights.ZD, Weights.XD,
    Gradient.CS, Gradient.CX, Gradient.CO, Gradient.XA, Gradient.YA, Gradient.ZA, Gradient.ZF, Gradient.FN,
)


def target_rows(geometry):
    crops, sides, places = geometry[0:1] & 7, geometry[1:2], geometry[2:3]
    first = places == 0
    big = sides == 7
    code = crops + jnp.where(first, jnp.where(big, 8, 16), 0)
    square = (ROWS_IMG, ROWS_IMG)
    diagonal = lax.broadcasted_iota(jnp.int32, square, 0) == lax.broadcasted_iota(jnp.int32, square, 1)
    column = jnp.sum(jnp.where(diagonal, code.astype(f32), 0.0), axis=1, keepdims=True).astype(jnp.int32)
    earlier = (column & 7) < crops
    seven = jnp.sum(jnp.where(earlier & ((column & 8) > 0), 1.0, 0.0), axis=0, keepdims=True).astype(jnp.int32)
    three = jnp.sum(jnp.where(earlier & ((column & 16) > 0), 1.0, 0.0), axis=0, keepdims=True).astype(jnp.int32)
    cell = jnp.maximum(places - 1, 0)
    row = jnp.where(big, (cell * 37) >> 8, (cell * 43) >> 7)
    col = cell - row * sides
    in_seven = seven * 56 + row * 8 + col
    in_three = END7 + (three >> 1) * 24 + row * 8 + (three & 1) * 4 + col
    classes = END3 + jnp.where(big, seven, 2 + three)
    return jnp.where(first, classes, jnp.where(big, in_seven, in_three))


def step_kernel(many, names, *refs):
    outside = INPUTS + SHARDS + OUTPUTS
    hbm = types.SimpleNamespace(**dict(zip(outside, refs)))
    r = types.SimpleNamespace(**dict(zip(names, refs[len(outside) :])))
    links = Links(many)
    links.group_send = getattr(r, "group_send", None)
    for name, size in POOLS:
        links.pool(name, getattr(r, "send_" + name))
    loads = [
        pltpu.make_async_copy(getattr(hbm, name), getattr(r, name), r.load_sems.at[slot]) for slot, name in enumerate(INPUTS)
    ]
    for load in loads:
        load.start()
    links.meet()
    weights = {}
    for place, kind in enumerate(KINDS):
        local, full = getattr(hbm, "l" + kind), getattr(r, "w" + kind)
        for layer in range(LAYERS):
            slot = place * LAYERS + layer
            weights[kind, layer] = Weights(
                links, local.at[layer], functools.partial(lambda full, layer, block: full.at[block, layer], full, layer),
                r.weight_recv.at[slot], r.weight_own.at[slot], (kind, layer) in DIRECT,
            )
    for layer in range(LAYERS):
        for kind in KINDS:
            weights[kind, layer].start()
            weights[kind, layer].start_near()
    for load in loads[:4]:
        load.wait()
    for layer in range(LAYERS):
        r.lsmall[layer, 0:49] = r.crpe[:, layer]
        r.lsmall[layer, 49:52] = r.head_bias[:, layer]
        for part in range(4):
            r.lsmall[layer, 52 + part : 53 + part] = r.fc1_bias[layer : layer + 1, part * LANES : (part + 1) * LANES]
    small = Small(links, r.lsmall, r.small, r.small_recv, r.weight_own.at[8])
    small.start()
    for load in loads[4:]:
        load.wait()
    gradients = {}
    left = {kind: [CHUNKS[kind]] * LAYERS for kind in KINDS}
    finals = []

    def write(kind, layer):
        if kind != "rest":
            left[kind][layer] -= 1
            if left[kind][layer]:
                return
        source, target = (
            (r.rrest, hbm.rrest) if kind == "rest" else (getattr(space, "r" + kind).at[layer] for space in (r, hbm))
        )
        finals.append(pltpu.make_async_copy(source, target, r.final_sems.at[len(finals)]))
        finals[-1].start()

    for slot, (kind, layer, part) in enumerate(chunk_list()):
        tall, wide, dtype = chunk_shape(kind)
        if kind == "rest":
            full = lambda block: r.grest.at[block]
            result = r.rrest
        else:
            rows = part if kind in ("qkv", "fc1") else pl.ds(part * tall, tall)
            whole = getattr(r, "g" + kind)
            full = functools.partial(lambda whole, layer, rows, block: whole.at[block, layer, rows], whole, layer, rows)
            result = getattr(r, "r" + kind).at[layer, rows]
        gradients[kind, layer, part] = Gradient(
            links, full, *(getattr(r, name + str(slot), None) for name in ("core", "side", "half", "quad", "group")), result,
            functools.partial(write, kind, layer), r.grad_recv.at[slot],
        )

    def point(which, layer, place):
        for code in ORDER.get((which, layer, place), ()):
            step, kind, of_layer, part = code // 1000, code // 100 % 10, code // 10 % 10, code % 10
            kind = (KINDS + ("rest",))[kind]
            STEPS[step](weights[kind, of_layer] if step < 6 else gradients[kind, of_layer, part])

    def forward_point(layer, place):
        point(0, layer, place)
        if layer == 0 and place == 0:
            small.wait()
        if place == 7 and layer == LAYERS - 1:
            fc2_gradients(r, layer, functools.partial(point, 1, layer))
        if place in NEEDED:
            weights[NEEDED[place], layer].wait()

    r.wide7[...] = jnp.zeros_like(r.wide7)
    r.wide3[...] = jnp.zeros_like(r.wide3)
    r.grest[...] = jnp.zeros_like(r.grest)
    target = target_rows(r.geometry[...])
    r.place[...] = (lax.broadcasted_iota(jnp.int32, (CAN, ROWS_IMG), 0) == target).astype(f32).astype(bf16)
    r.streams[0] = mm(r.place[...], r.feats[...])
    r.grads[...] = mm(r.place[...], r.ograd[...])
    for layer in range(LAYERS):
        forward(r, layer, functools.partial(forward_point, layer))
    for layer in reversed(range(LAYERS)):
        if layer < LAYERS - 1:
            fc2_gradients(r, layer, functools.partial(point, 1, layer))
        backward(r, layer, functools.partial(point, 1, layer))
    point(1, 0, 16)
    feed_forward_sum(r, LAYERS - 1)
    r.out[...] = mm_tn(r.place[...], r.work[...].astype(bf16)).astype(bf16)
    r.fgrad[...] = sum(mm_tn(r.place[...], part) for part in halves(r.grads[...]))
    stores = [
        pltpu.make_async_copy(getattr(r, name), getattr(hbm, name), r.store_sems.at[slot])
        for slot, name in enumerate(("out", "fgrad", "rshared"))
    ]
    stores[0].start()
    stores[1].start()
    point(2, 0, 0)
    r.rshared[links.block] = r.rrest[FIRST_SHARED : FIRST_SHARED + 32]
    mine = r.rshared.at[links.block]
    for slot, other in enumerate((links.by_core, links.by_side, links.by_far)):
        links.send("last", [(mine, mine, other)], r.last_recv.at[slot])
    for slot, block in enumerate((links.block_core, links.block_side, links.block_far)):
        links.arrived(r.rshared.at[block], r.last_recv.at[slot])
    stores[2].start()
    for store in stores:
        store.wait()
    for final in finals:
        final.wait()
    links.finish()


def proj_matrix(r, layer):
    return jnp.concatenate([r.wproj[SLOT[block], layer] for block in range(BLOCKS)], axis=0)


def forward(r, layer, point):
    real = real_rows()
    fill(halves(r.streams[layer]), 1, r.moves, r.wide7, r.wide3)
    for block in range(BLOCKS):
        lanes = lanes_of(block)
        spread_taps(r.taps, block, r.cpe[:, layer, lanes])
        conv = convolve(r.taps, block, 1, 1, 1, False, r.wide7, r.wide3)
        r.work[0:END3, lanes] = r.streams[layer, 0:END3, lanes] + conv + r.bias[0, layer : layer + 1, lanes]
        r.work[END3:CAN, lanes] = r.streams[layer, END3:CAN, lanes]
    unit, inverse, normed = norm_forward(r.work[...], r.gain[layer, 0:1], r.shift[layer, 0:1])
    r.unit1[layer] = unit
    r.inv1[layer] = inverse
    r.normed1[layer] = normed
    point(0)
    for block in range(BLOCKS):
        lanes = lanes_of(block)
        project = mm(normed, side_by_side(r.wqkv[SLOT[block], layer]))
        r.queries[layer, :, lanes] = (project[:, :LANES] + r.small[SLOT[block], layer, 49:50]).astype(bf16)
        r.values[layer, :, lanes] = (project[:, 2 * LANES :] + r.small[SLOT[block], layer, 50:51]).astype(bf16)
        keys = project[:, LANES : 2 * LANES].astype(bf16).astype(f32)
        largest = jnp.max(jnp.where(real, keys, -1e30), axis=0, keepdims=True)
        exponent = jnp.exp(jnp.where(real, keys - largest, 0.0))
        exact = exponent / sum(mm(r.same[...], part) for part in halves(exponent))
        r.exacts[layer, :, lanes] = exact
        r.softs[layer, :, lanes] = exact.astype(bf16)
        spread_taps(r.taps, block, r.small[SLOT[block], layer, 0:49] * r.tap_mask[block, 0:49])
    point(1)
    fill([r.values[layer]], 3, r.moves, r.wide7, r.wide3)
    for block in range(BLOCKS):
        lanes = lanes_of(block)
        query = r.queries[layer, :, lanes]
        soft = r.softs[layer, :, lanes]
        value = r.values[layer, :, lanes]
        factors = []
        for head in range(2):
            masked = jnp.where(head_lanes(head), query, jnp.zeros_like(query))
            mixing = (mm_nt(masked, soft) * SCALE * r.same[...].astype(f32)).astype(bf16)
            factors.append(mm(mixing, value))
        factor = jnp.where(head_lanes(0), factors[0], factors[1])
        conv = convolve(r.taps, block, REACH7[block], REACH3[block], 3, False, r.wide7, r.wide3) + r.small[SLOT[block], layer, 51:52]
        r.convs[layer, 0:END3, lanes] = conv
        r.attended[layer, 0:END3, lanes] = (factor[0:END3] + query[0:END3].astype(f32) * conv).astype(bf16)
        r.attended[layer, END3:CAN, lanes] = factor[END3:CAN].astype(bf16)
        point(2 + block)
    after = r.work[...] + mm(r.attended[layer], proj_matrix(r, layer)) + r.bias[1, layer : layer + 1]
    unit, inverse, normed = norm_forward(after, r.gain[layer, 1:2], r.shift[layer, 1:2])
    r.unit2[layer] = unit
    r.inv2[layer] = inverse
    r.normed2[layer] = normed
    r.work[...] = after + r.bias[2, layer : layer + 1]
    point(6)

    def feed(block, carry):
        hidden = mm(r.normed2[layer], r.wfc1[block, layer]) + jnp.concatenate(
            [r.small[block, layer, 52 + part : 53 + part] for part in range(4)], axis=1
        )
        chance = 0.5 * (1.0 + lax.erf(hidden * np.float32(0.5**0.5)))
        density = jnp.exp(hidden * hidden * -0.5) * np.float32((2 * np.pi) ** -0.5)
        r.slope[layer, block] = chance + hidden * density
        r.active[layer, block] = (hidden * chance).astype(bf16)
        return carry

    lax.fori_loop(0, BLOCKS, feed, 0)
    point(7)

    if layer < LAYERS - 1:
        feed_forward_sum(r, layer)
        r.streams[layer + 1] = r.work[...]
    else:
        r.streams[LAYERS] = r.work[...]


def feed_forward_sum(r, layer):
    if layer == LAYERS - 1:
        r.work[...] = r.streams[LAYERS]

    def collect(block, carry):
        r.work[...] += mm(r.active[layer, block], r.wfc2[block, layer])
        return carry

    lax.fori_loop(0, BLOCKS, collect, 0)


def put_shared(r, layer, row, value):
    for block in range(BLOCKS):
        first = FIRST_SHARED + 16 * layer + row
        r.grest[SLOT[block], first : first + 1] = value[:, block * LANES : (block + 1) * LANES]


def fc2_gradients(r, layer, point):
    put_shared(r, layer, 11, column_sum(r.grads[...]))
    r.low[...] = r.grads[...].astype(bf16)
    for part in range(4):
        rows = lanes_of(part)
        joined = jnp.concatenate([r.active[layer, block, :, rows] for block in range(BLOCKS)], axis=1)
        product = mm_tn(joined, r.low[...]).astype(bf16)
        for block in range(BLOCKS):
            r.gfc2[block, layer, rows] = product[block * LANES : (block + 1) * LANES]
        point(part)


def backward(r, layer, point):
    def put_small(block, row, value):
        r.grest[block, 56 * layer + row : 56 * layer + row + value.shape[0]] = value

    r.work[...] = jnp.zeros_like(r.work)

    def feed(block, carry):
        hidden = (mm_nt(r.low[...], r.wfc2[block, layer]) * r.slope[layer, block]).astype(bf16)
        sums = column_sum(hidden.astype(f32))
        for part in range(4):
            row = 56 * layer + 52 + part
            r.grest[block, row : row + 1] = sums[:, part * LANES : (part + 1) * LANES]
        r.hidden[block] = hidden
        return carry

    lax.fori_loop(0, BLOCKS, feed, 0)
    point(4)
    for part in range(4):
        joined = jnp.concatenate([r.hidden[block, :, lanes_of(part)] for block in range(BLOCKS)], axis=1)
        product = mm_tn(r.normed2[layer], joined).astype(bf16)
        for block in range(BLOCKS):
            r.gfc1[block, layer, part] = product[:, block * LANES : (block + 1) * LANES]
        point(5 + part)

    def collect(block, carry):
        r.work[...] += mm_nt(r.hidden[block], r.wfc1[block, layer])
        return carry

    lax.fori_loop(0, BLOCKS, collect, 0)
    incoming = r.work[...]
    unit = r.unit2[layer]
    put_shared(r, layer, 13, column_sum(incoming * unit))
    put_shared(r, layer, 15, column_sum(incoming))
    r.grads[...] = r.grads[...] + norm_backward(incoming, unit, r.inv2[layer], r.gain[layer, 1:2])
    branch = r.grads[...]
    put_shared(r, layer, 10, column_sum(branch))
    branch = branch.astype(bf16)
    product = mm_tn(r.attended[layer], branch).astype(bf16)
    for block in range(BLOCKS):
        r.gproj[SLOT[block], layer] = product[block * LANES : (block + 1) * LANES]
    r.gatt[...] = mm_nt(branch, proj_matrix(r, layer)).astype(bf16)
    point(9)
    fill([r.values[layer]], 3, r.moves, r.wide7, r.wide3)
    for block in range(BLOCKS):
        lanes = lanes_of(block)
        product = r.gatt[0:END3, lanes].astype(f32) * r.queries[layer, 0:END3, lanes].astype(f32)
        r.rel[0:END3, lanes] = product.astype(bf16)
        r.rel[END3:CAN, lanes] = jnp.zeros((CAN - END3, LANES), bf16)
        put_small(SLOT[block], 51, column_sum(product))
        sums = tap_grads(product, block, REACH7[block], REACH3[block], 3, r.taps, r.wide7, r.wide3)
        put_small(SLOT[block], 0, sums * r.tap_mask[block, 0:49])
        spread_taps(r.taps, block, r.small[SLOT[block], layer, 0:49] * r.tap_mask[block, 0:49])
    point(10)
    fill([r.rel[...]], 3, r.moves, r.wide7, r.wide3)
    r.work[...] = jnp.zeros_like(r.work)
    for block in range(BLOCKS):
        lanes = lanes_of(block)
        query = r.queries[layer, :, lanes]
        soft = r.softs[layer, :, lanes]
        value = r.values[layer, :, lanes]
        grad = r.gatt[:, lanes]
        exact = r.exacts[layer, :, lanes]
        picked = []
        for head in range(2):
            chosen = head_lanes(head)
            zero = jnp.zeros_like(query)
            query_head = jnp.where(chosen, query, zero)
            grad_head = jnp.where(chosen, grad, zero)
            same_low = r.same[...]
            mixing_t = (mm_nt(soft, query_head) * SCALE * same_low.astype(f32)).astype(bf16)
            mix = mm_nt(grad_head, value).astype(bf16) * same_low
            mix_t = mm_nt(value, grad_head).astype(bf16) * same_low
            picked.append((mm(mixing_t, grad), SCALE * mm(mix, soft), SCALE * mm(mix_t, query)))
        grad_value, grad_query, grad_soft = (
            jnp.where(head_lanes(0), one, two) for one, two in zip(*picked)
        )
        grad_soft = grad_soft.astype(bf16).astype(f32)
        weighted = grad_soft * exact
        grad_key = weighted - exact * sum(mm(r.same[...], part) for part in halves(weighted))
        conv = convolve(r.taps, block, REACH7[block], REACH3[block], 3, True, r.wide7, r.wide3)
        grad_value = jnp.concatenate([grad_value[0:END3] + conv, grad_value[END3:CAN]], axis=0).astype(bf16)
        grad_query = jnp.concatenate(
            [grad_query[0:END3] + grad[0:END3].astype(f32) * r.convs[layer, 0:END3, lanes], grad_query[END3:CAN]], axis=0
        ).astype(bf16)
        put_small(SLOT[block], 49, column_sum(grad_query.astype(f32)))
        put_small(SLOT[block], 50, column_sum(grad_value.astype(f32)))
        joined = jnp.concatenate([grad_query, grad_key.astype(bf16), grad_value], axis=1)
        product = mm_tn(r.normed1[layer], joined).astype(bf16)
        for part in range(3):
            r.gqkv[SLOT[block], layer, part] = product[:, part * LANES : (part + 1) * LANES]
        r.work[...] += mm_nt(joined, side_by_side(r.wqkv[SLOT[block], layer]))
        point(11 + block)
    incoming = r.work[...]
    unit = r.unit1[layer]
    put_shared(r, layer, 12, column_sum(incoming * unit))
    put_shared(r, layer, 14, column_sum(incoming))
    r.grads[...] = r.grads[...] + norm_backward(incoming, unit, r.inv1[layer], r.gain[layer, 0:1])
    fill(halves(r.streams[layer]), 1, r.moves, r.wide7, r.wide3)
    for block in range(BLOCKS):
        lanes = lanes_of(block)
        product = r.grads[0:END3, lanes]
        first = FIRST_SHARED + 16 * layer
        r.grest[SLOT[block], first + 9 : first + 10] = column_sum(product)
        r.grest[SLOT[block], first : first + 9] = tap_grads(product, block, 1, 1, 1, r.taps, r.wide7, r.wide3)
    fill(halves(r.grads[...]), 1, r.moves, r.wide7, r.wide3)
    for block in range(BLOCKS):
        lanes = lanes_of(block)
        spread_taps(r.taps, block, r.cpe[:, layer, lanes])
        conv = convolve(r.taps, block, 1, 1, 1, True, r.wide7, r.wide3)
        r.grads[0:END3, lanes] = r.grads[0:END3, lanes] + conv
    point(15)


def widen(target, source):
    cut = len(source.shape) > len(target.shape)
    tall, wide = source.shape[-2:]
    outer = source.shape[:-2]
    for lead in np.ndindex(*outer):
        into = (lead[0], slice(None), pl.ds(lead[1] * wide, wide)) if cut else (*lead, slice(None), slice(None))
        view, seen = target.at[into], source.at[lead]

        def body(index, carry):
            rows = pl.ds(pl.multiple_of(index * 128, 128), 128)
            view[rows] = seen[rows].astype(f32)
            return carry

        lax.fori_loop(0, tall // 128, body, 0)


def finish_kernel(count, *refs):
    taken, given = refs[:8], refs[8 : 8 + count]
    inside, made, load_sems, store_sems = refs[8 + count : 16 + count], refs[16 + count : -2], refs[-2], refs[-1]
    loads = [pltpu.make_async_copy(source, target, load_sems.at[slot]) for slot, (source, target) in enumerate(zip(taken, inside))]
    order = (3, 2, 0, 1, 4, 5, 6, 7)
    for slot in order:
        loads[slot].start()
    stores = [
        pltpu.make_async_copy(source, target, store_sems.at[slot])
        for slot, (source, target) in enumerate(zip(tuple(inside[6:]) + tuple(made), given))
    ]
    cpe, bias, gain, shift, qkv, head_bias, crpe, proj, fc1, fc1_bias, fc2 = made
    for source, slot in ((3, 10), (2, 8), (0, 4), (1, 7)):
        loads[source].wait()
        widen(made[slot], inside[source])
        stores[2 + slot].start()
    for slot in (6, 7):
        loads[slot].wait()
        stores[slot - 6].start()
    loads[4].wait()
    loads[5].wait()
    rrest, rshared = inside[4:6]
    for layer in range(LAYERS):
        for block in range(BLOCKS):
            lanes = lanes_of(block)
            first = layer * 16
            cpe[:, layer, lanes] = rshared[SLOT[block], first : first + 9]
            bias[:, layer, lanes] = rshared[SLOT[block], first + 9 : first + 12]
            gain[layer, :, lanes] = rshared[SLOT[block], first + 12 : first + 14]
            shift[layer, :, lanes] = rshared[SLOT[block], first + 14 : first + 16]
            fc1_bias[layer : layer + 1, lanes] = rrest[layer * 56 + 52 + block : layer * 56 + 53 + block]
        crpe[:, layer] = rrest[layer * 56 : layer * 56 + 49]
        head_bias[:, layer] = rrest[layer * 56 + 49 : layer * 56 + 52]
    for slot in (0, 1, 2, 3, 5, 6, 9):
        stores[2 + slot].start()
    for copy in stores:
        copy.wait()


def shards(
    data, features, crop_index, grid_size, position, cpe_weight, shared_bias, norm_gain, norm_bias,
    qkv_weight, head_bias, crpe_weight, proj_weight, fc1_weight, fc1_bias, fc2_weight, out_grad,
):
    many = data // 8
    assert data == 8 * many and many & (many - 1) == 0 and features.shape[0] == ROWS_IMG
    start = lax.axis_index("mp") * ROWS_IMG
    geometry = lax.dynamic_slice(jnp.stack([crop_index, grid_size, position]), (0, start), (3, ROWS_IMG))
    same, moves = canonical_tables()
    swap = lambda item: jnp.transpose(item, (1, 0, 2))
    hbm = pl.BlockSpec(memory_space=pl.ANY)
    shape = jax.ShapeDtypeStruct
    loaded = dict(
        zip(
            INPUTS,
            (
                geometry, swap(crpe_weight), swap(head_bias), fc1_bias, features, out_grad, jnp.asarray(same, bf16),
                jnp.asarray(moves, bf16), jnp.asarray(tap_table()), swap(cpe_weight), swap(shared_bias), norm_gain, norm_bias,
            ),
        )
    )
    specs = scratch_specs(many, loaded)
    results = pl.pallas_call(
        functools.partial(step_kernel, many, tuple(specs)),
        out_shape=(
            shape((ROWS_IMG, WIDE), bf16),
            shape((ROWS_IMG, WIDE), f32),
            *(shape((LAYERS, *GRADS[kind]), bf16) for kind in KINDS),
            shape((REST, LANES), f32),
            shape((BLOCKS, 32, LANES), f32),
        ),
        in_specs=[hbm] * len(INPUTS + SHARDS),
        out_specs=(hbm,) * len(OUTPUTS),
        scratch_shapes=list(specs.values()),
        compiler_params=pltpu.CompilerParams(
            vmem_limit_bytes=63 * 2**20, collective_id=0, has_side_effects=True
        ),
        name="step",
    )(
        *loaded.values(), jnp.transpose(qkv_weight, (0, 2, 1, 3)), proj_weight, fc1_weight, fc2_weight
    )
    out, fgrad, rqkv, rproj, rfc1, rfc2, rrest, rshared = results
    taken = (rqkv, rproj, rfc1, rfc2, rrest, rshared, out, fgrad)
    swapped = lambda item: (item.shape[1], item.shape[0], item.shape[2])
    given = [
        shape(dims, f32)
        for dims in (
            fgrad.shape, swapped(cpe_weight), swapped(shared_bias), norm_gain.shape, norm_bias.shape, rqkv.shape,
            swapped(head_bias), swapped(crpe_weight), rproj.shape, fc1_weight.shape, fc1_bias.shape, rfc2.shape,
        )
    ]
    given = [shape(out.shape, bf16)] + given
    final = list(
        pl.pallas_call(
            functools.partial(finish_kernel, len(given)),
            out_shape=given,
            in_specs=[hbm] * len(taken),
            out_specs=[hbm] * len(given),
            scratch_shapes=[pltpu.VMEM(item.shape, item.dtype) for item in list(taken) + given[2:]]
            + [pltpu.SemaphoreType.DMA((len(taken),)), pltpu.SemaphoreType.DMA((len(given),))],
            compiler_params=pltpu.CompilerParams(vmem_limit_bytes=63 * 2**20),
            name="finish",
        )(*taken)
    )
    for index in (2, 3, 7, 8):
        final[index] = swap(final[index])
    final[6] = jnp.transpose(final[6], (0, 2, 1, 3))
    return tuple(final)


def solution(mesh):
    placed = (
        P(("dp", "mp"), None),
        P("dp"),
        P("dp"),
        P("dp"),
        P(),
        P(),
        P(),
        P(),
        P(None, None, None, "mp"),
        P(None, None, "mp"),
        P(None, None, "mp"),
        P(None, "mp", None),
        P(None, None, "mp"),
        P(None, "mp"),
        P(None, "mp", None),
        P(("dp", "mp"), None),
    )
    return jax.shard_map(
        functools.partial(shards, mesh.shape["dp"]),
        mesh=mesh,
        in_specs=placed,
        out_specs=(
            P(("dp", "mp"), None),
            P(("dp", "mp"), None),
            P(),
            P(),
            P(),
            P(),
            P(None, None, None, "mp"),
            P(None, None, "mp"),
            P(None, None, "mp"),
            P(None, "mp", None),
            P(None, None, "mp"),
            P(None, "mp"),
            P(None, "mp", None),
        ),
        check_vma=False,
    )
```

```python
import functools
import types

import jax
import jax.numpy as jnp
import numpy as np
from jax import lax
from jax.experimental import pallas as pl
from jax.experimental.pallas import tpu as pltpu
from jax.sharding import PartitionSpec as P

HD = 64
LAYERS = 2
ROWS_IMG = 160
CAN = 192
END7 = 112
END3 = 184
LANES = 128
WIDE = 512
BLOCKS = 4
SLOT = (0, 2, 1, 3)
EPSILON = 1e-06
SCALE = HD ** (-0.5)
REACH7 = (1, 2, 3, 3)
REACH3 = (1, 2, 2, 2)
MESH = pl.DeviceIdType.MESH
f32 = jnp.float32
bf16 = jnp.bfloat16


def canonical_tables():
    crop = np.full(CAN, 100)
    col = np.full(CAN, -1)
    side = np.zeros(CAN, int)
    for t in range(END7):
        if t % 8 < 7:
            crop[t], col[t], side[t] = t // 56, t % 8, 7
    for t in range(END7, END3):
        u = t - END7
        if t % 4 < 3:
            crop[t], col[t], side[t] = 2 + 2 * (u // 24) + (t % 8) // 4, t % 4, 3
    for t in range(END3, CAN):
        crop[t] = t - END3
    same = (crop[:, None] == crop[None, :]).astype(np.float32)
    moves = np.zeros((7, CAN, CAN), np.float32)
    for b in range(-3, 4):
        for t in range(END3):
            if col[t] >= 0 and 0 <= col[t] + b < side[t]:
                moves[b + 3, t, t + b] = 1
    return same, moves


def tap_table():
    table = np.zeros((BLOCKS, 56, LANES), np.float32)
    for channel in range(WIDE):
        head = channel // HD
        reach = 1 if head < 2 else 2 if head < 5 else 3
        for tap in range(49):
            if max(abs(tap // 7 - 3), abs(tap % 7 - 3)) <= reach:
                table[channel // LANES, tap, channel % LANES] = 1
    return table


def mm(left, right):
    return jnp.dot(left, right, preferred_element_type=f32)


def mm_nt(left, right):
    return lax.dot_general(left, right, (((1,), (1,)), ((), ())), preferred_element_type=f32)


def mm_tn(left, right):
    return lax.dot_general(left, right, (((0,), (0,)), ((), ())), preferred_element_type=f32)


def side_by_side(parts):
    return jnp.concatenate([parts[index] for index in range(parts.shape[0])], axis=1)


def halves(values):
    high = values.astype(bf16)
    return [high, (values - high.astype(f32)).astype(bf16)]


def lanes_of(block):
    return pl.ds(block * LANES, LANES)


def column_sum(values):
    return jnp.sum(values, axis=0, keepdims=True)


def fill(parts, reach, moves, wide7, wide3):
    for b in range(-reach, reach + 1):
        moved = sum(mm(moves[b + 3], part) for part in parts)
        for grid in range(2):
            wide7[b + 3, grid] = moved[grid * 56 : grid * 56 + 56]
        if abs(b) <= 2:
            for pair in range(3):
                first = END7 + pair * 24
                wide3[b + 2, pair] = moved[first : first + 24]


def tap_row(a, b, half, flip):
    if flip:
        a, b = -a, -b
    return (a + half) * (2 * half + 1) + b + half


def spread_taps(spread, block, rows):
    for row in range(rows.shape[0]):
        spread[block, row] = jnp.broadcast_to(rows[row : row + 1], (8, LANES))


def grid_rows(wide, place, side, lanes):
    return [wide[place, :, row * 8 : row * 8 + 8, lanes] for row in range(side)]


def convolve(spread, block, reach7, reach3, half, flip, wide7, wide3):
    lanes = lanes_of(block)

    def loop(wide, offset, reach, grids, side):
        def body(step, sums):
            b = step - reach
            rows = grid_rows(wide, b + offset, side, lanes)
            sums = list(sums)
            for a in range(-reach, reach + 1):
                weight = spread[block, tap_row(a, b, half, flip)]
                for row in range(max(0, -a), min(side, side - a)):
                    sums[row] = sums[row] + weight * rows[row + a]
            return tuple(sums)

        start = tuple(jnp.zeros((grids, 8, LANES), f32) for _ in range(side))
        sums = lax.fori_loop(0, 2 * reach + 1, body, start)
        return [sums[row][grid] for grid in range(grids) for row in range(side)]

    return jnp.concatenate(loop(wide7, 3, reach7, 2, 7) + loop(wide3, 2, reach3, 3, 3), axis=0)


def tap_grads(grad, block, reach7, reach3, half, spread, wide7, wide3):
    lanes = lanes_of(block)
    count = (2 * half + 1) ** 2
    spread[block, 0:count] = jnp.zeros((count, 8, LANES), f32)

    def loop(wide, offset, reach, part, side):
        def body(step, carry):
            b = step - reach
            rows = grid_rows(wide, b + offset, side, lanes)
            for a in range(-reach, reach + 1):
                total = sum(part[:, row * 8 : row * 8 + 8] * rows[row + a] for row in range(max(0, -a), min(side, side - a)))
                spread[block, tap_row(a, b, half, False)] += jnp.sum(total, axis=0)
            return carry

        lax.fori_loop(0, 2 * reach + 1, body, 0)

    loop(wide7, 3, reach7, grad[:END7].reshape(2, 56, LANES), 7)
    loop(wide3, 2, reach3, grad[END7:END3].reshape(3, 24, LANES), 3)
    return jnp.sum(spread[block, 0:count], axis=1)


def norm_forward(values, gain, bias):
    center = values - jnp.mean(values, axis=-1, keepdims=True)
    spread = jnp.mean(center * center, axis=-1, keepdims=True)
    inverse = lax.rsqrt(spread + EPSILON)
    unit = center * inverse
    return unit, inverse, (unit * gain + bias).astype(bf16)


def norm_backward(incoming, unit, inverse, gain):
    scaled = incoming * gain
    mean_one = jnp.mean(scaled, axis=-1, keepdims=True)
    mean_two = jnp.mean(scaled * unit, axis=-1, keepdims=True)
    return inverse * (scaled - mean_one - unit * mean_two)


def real_rows():
    row = lax.broadcasted_iota(jnp.int32, (CAN, LANES), 0)
    seven = (row < END7) & ((row & 7) != 7)
    three = (row >= END7) & (row < END3) & ((row & 3) != 3)
    return seven | three | (row >= END3)


def head_lanes(head):
    lane = lax.broadcasted_iota(jnp.int32, (CAN, LANES), 1)
    return (lane >= HD) if head else (lane < HD)


def rows_of(ref, start, count):
    rows = pl.ds(pl.multiple_of(start, 8), count)
    return ref.at[rows] if len(ref.shape) == 2 else ref.at[:, rows]


def add_rows(target, start, source, first, count):
    step = next(size for size in (64, 48, 32, 24, 16, 8) if count % size == 0)

    def body(index, carry):
        into = pl.ds(pl.multiple_of(start + index * step, 8), step)
        target[into] = target[into] + source[pl.ds(pl.multiple_of(first + index * step, 8), step)]
        return carry

    lax.fori_loop(0, count // step, body, 0)


class Links:
    def __init__(self, many):
        dp, mp = lax.axis_index("dp"), lax.axis_index("mp")
        self.many = many
        self.core, self.side = lax.rem(mp, 2), lax.div(mp, 2)
        self.half, self.quad, self.group = lax.rem(dp, 2), lax.rem(lax.div(dp, 2), 4), lax.div(dp, 8)
        self.block = self.core * 2 + self.side
        self.block_core = (1 - self.core) * 2 + self.side
        self.block_side = self.core * 2 + 1 - self.side
        self.block_far = (1 - self.core) * 2 + 1 - self.side
        self.by_core = (dp, self.side * 2 + 1 - self.core)
        self.by_side = (dp, (1 - self.side) * 2 + self.core)
        self.by_far = (dp, (1 - self.side) * 2 + 1 - self.core)
        self.by_half = (dp + 1 - 2 * self.half, mp)
        self.by_quad = [
            (self.group * 8 + lax.rem(self.quad + step, 4) * 2 + self.half, mp) for step in range(1, 4)
        ]
        self.rounds = many.bit_length() - 1
        self.by_group = []
        for step in range(self.rounds):
            bit = lax.rem(lax.div(self.group, 1 << step), 2)
            partner = self.group + (1 - 2 * bit) * (1 << step)
            self.by_group.append((partner * 8 + self.quad * 2 + self.half, mp))
        self.pair = lax.rem(self.quad, 2)
        self.by_pair = (self.group * 8 + (self.quad + 1 - 2 * self.pair) * 2 + self.half, mp)
        self.pools = {}

    def meet(self):
        barrier = pltpu.get_barrier_semaphore()
        others = [self.by_core, self.by_side, self.by_far, self.by_half] + self.by_quad + self.by_group
        for other in others:
            pl.semaphore_signal(barrier, inc=1, device_id=other, device_id_type=MESH)
        pl.semaphore_wait(barrier, len(others))

    def pool(self, name, sems):
        self.pools[name] = [sems, [None] * sems.shape[0], 0]

    def take(self, name, waiter):
        sems, waiters, place = self.pools[name]
        if waiters[place] is not None:
            waiters[place]()
        waiters[place] = waiter
        self.pools[name][2] = (place + 1) % len(waiters)
        return sems.at[place]

    def copy(self, source, target, send_sem, recv_sem, other):
        return pltpu.make_async_remote_copy(
            src_ref=source, dst_ref=target, send_sem=send_sem, recv_sem=recv_sem, device_id=other, device_id_type=MESH
        )

    def send(self, name, items, recv_sem, whole=None):
        box = []
        send_sem = self.take(name, lambda: box[0].wait_send())
        copies = [self.copy(source, target, send_sem, recv_sem, other) for source, target, other in items]
        box.append(copies[0] if whole is None else self.copy(whole, whole, send_sem, recv_sem, self.by_core))
        for copy in copies:
            copy.start()

    def arrived(self, target, recv_sem):
        self.copy(target, target, recv_sem, recv_sem, self.by_core).wait_recv()

    def finish(self):
        for sems, waiters, place in self.pools.values():
            for waiter in waiters:
                if waiter is not None:
                    waiter()


class Weights:
    def __init__(self, links, local, full, recv_sems, own_sem, direct):
        self.links, self.local, self.full, self.direct = links, local, full, direct
        self.recv_sems, self.own_sem = recv_sems, own_sem
        self.count = local.shape[-2] // 4
        self.sub = self.count // 2

    def start_of(self, half, pair):
        return (half * 2 + pair) * self.count

    def places(self):
        links = self.links
        far = self.start_of(1 - links.half, 1 - links.pair)
        near = (
            (self.start_of(links.half, links.pair), self.count),
            (self.start_of(1 - links.half, links.pair), self.count),
            (self.start_of(links.half, 1 - links.pair), self.count),
        )
        return near + (((far, self.count),) if self.direct else ((far + self.sub, self.sub), (far, self.sub)))

    def push(self, part, slot, other):
        self.links.send("weights", [(part, part, other)], self.recv_sems.at[slot])

    def take(self, index):
        start, count = self.places()[index]
        part = rows_of(self.full(self.links.block_side), start, count)
        self.links.arrived(part, self.recv_sems.at[index])
        self.push(part, 5, self.links.by_core)
        return part

    def start(self):
        links = self.links
        for index in (0, 3) if self.direct else (0,):
            start, count = self.places()[index]
            target = rows_of(self.full(links.block), start, count)
            links.send("weights", [(rows_of(self.local, start, count), target, links.by_side)], self.recv_sems.at[index])

    def start_near(self):
        links = self.links
        links.send("weights", [(self.local, self.full(links.block), links.by_core)], self.recv_sems.at[5])
        self.own = pltpu.make_async_copy(self.local, self.full(links.block), self.own_sem)
        self.own.start()

    def F1(self):
        part = self.take(0)
        self.push(part, 1, self.links.by_half)
        self.push(part, 2, self.links.by_pair)

    def Y1(self):
        part = self.take(1)
        if not self.direct:
            self.push(rows_of(part, 0, self.sub), 4, self.links.by_pair)

    def Z1(self):
        part = self.take(2)
        if not self.direct:
            self.push(rows_of(part, self.sub, self.sub), 3, self.links.by_half)

    def YD(self):
        self.take(3)

    def ZD(self):
        self.take(4)

    def XD(self):
        self.take(3)

    def wait(self):
        self.own.wait()
        self.links.arrived(self.full(pl.ds((1 - self.links.core) * 2, 2)), self.recv_sems.at[5])


class Small:
    def __init__(self, links, local, full, recv_sems, own_sem):
        self.links, self.local, self.full, self.recv_sems, self.own_sem = links, local, full, recv_sems, own_sem

    def start(self):
        links = self.links
        for slot, other in enumerate((links.by_side, links.by_core)):
            links.send("weights", [(self.local, self.full.at[links.block], other)], self.recv_sems.at[slot])
        self.own = pltpu.make_async_copy(self.local, self.full.at[links.block], self.own_sem)
        self.own.start()

    def wait(self):
        links = self.links
        part = self.full.at[links.block_side]
        links.arrived(part, self.recv_sems.at[0])
        links.send("weights", [(part, part, links.by_core)], self.recv_sems.at[2])
        self.own.wait()
        links.arrived(self.full.at[links.block_core], self.recv_sems.at[1])
        links.arrived(self.full.at[links.block_far], self.recv_sems.at[2])


class Gradient:
    def __init__(self, links, full, core_in, side_in, half_in, quad_in, group_in, result, final, recv_sems):
        self.links, self.full, self.result, self.final = links, full, result, final
        self.core_in, self.side_in, self.half_in, self.quad_in, self.group_in = core_in, side_in, half_in, quad_in, group_in
        self.recv_sems = recv_sems
        self.tall = result.shape[0]
        self.half, self.piece = self.tall // 2, self.tall // 8
        self.here, self.there = links.half * self.half, (1 - links.half) * self.half
        self.mine = self.here + links.quad * self.piece

    def CS(self):
        links = self.links
        source = self.full(pl.ds((1 - links.core) * 2, 2))
        links.send("core", [(source, self.core_in, links.by_core)], self.recv_sems.at[0])

    def CX(self):
        links = self.links
        links.arrived(self.core_in, self.recv_sems.at[0])
        part = self.full(links.block_side)
        add_rows(part, 0, self.core_in.at[1 - links.side], 0, self.tall)
        links.send("side", [(part, self.side_in, links.by_side)], self.recv_sems.at[1])

    def CO(self):
        links = self.links
        add_rows(self.full(links.block), 0, self.core_in.at[links.side], 0, self.tall)

    def XA(self):
        links = self.links
        links.arrived(self.side_in, self.recv_sems.at[1])
        total = self.full(links.block)
        add_rows(total, self.there, self.side_in, self.there, self.half)
        links.send("half", [(rows_of(total, self.there, self.half), self.half_in, links.by_half)], self.recv_sems.at[2])
        add_rows(total, self.here, self.side_in, self.here, self.half)

    def YA(self):
        links = self.links
        links.arrived(self.half_in, self.recv_sems.at[2])
        total = self.full(links.block)
        add_rows(total, self.here, self.half_in, 0, self.half)
        items = []
        for step in range(3):
            start = self.here + lax.rem(links.quad + step + 1, 4) * self.piece
            items.append((rows_of(total, start, self.piece), self.quad_in.at[step], links.by_quad[step]))
        links.send("quad", items, self.recv_sems.at[3], self.quad_in)

    def ZA(self):
        links = self.links
        mine = pl.ds(pl.multiple_of(self.mine, 8), self.piece)
        total = self.full(links.block)
        links.arrived(self.quad_in, self.recv_sems.at[3])
        value = total[mine].astype(f32)
        for step in range(3):
            value = value + self.quad_in[step].astype(f32)
        if links.many > 1:
            for step in range(links.rounds):
                total[mine] = value.astype(total.dtype)
                copy = links.copy(
                    total.at[mine], self.group_in.at[step], links.group_send.at[step], self.recv_sems.at[6 + step],
                    links.by_group[step],
                )
                copy.start()
                copy.wait()
                value = total[mine].astype(f32) + self.group_in[step].astype(f32)
        part = self.result.at[mine]
        part[...] = value.astype(self.result.dtype)
        links.send("spread", [(part, part, other) for other in links.by_quad], self.recv_sems.at[4], self.quad_in)

    def ZF(self):
        links = self.links
        links.arrived(self.quad_in, self.recv_sems.at[4])
        part = rows_of(self.result, self.here, self.half)
        links.send("share", [(part, part, links.by_half)], self.recv_sems.at[5])

    def FN(self):
        self.links.arrived(rows_of(self.result, self.there, self.half), self.recv_sems.at[5])
        self.final()


ORDER = {
    (0, 0, 0): (
        0, 100, 200, 1000, 2000, 1100, 2100, 300, 10, 1200, 2200, 110, 3000, 4000,
    ),
    (0, 0, 1): (210, 1300, 2300, 3100, 4100,),
    (0, 0, 4): (310, 1010, 2010,),
    (0, 0, 6): (3200, 4200,),
    (0, 0, 7): (1110, 2110, 1210, 2210, 3300, 4300,),
    (0, 1, 0): (1310, 2310, 3010, 4010, 3110, 4110,),
    (0, 1, 1): (3210, 4210, 4310, 3310,),
    (1, 1, 0): (6310,),
    (1, 1, 1): (6311,),
    (1, 1, 2): (6312,),
    (1, 1, 3): (6313,),
    (1, 1, 5): (7310, 8310, 6210, 7311,),
    (1, 1, 6): (7312, 8311, 8312, 6211,),
    (1, 1, 7): (7313, 8313, 6212,),
    (1, 1, 8): (6213,),
    (1, 1, 9): (7210, 7211, 8210, 7212, 8211, 8212, 6110,),
    (1, 1, 10): (7213, 9310, 8213,),
    (1, 1, 11): (7110, 9311, 8110,),
    (1, 1, 14): (9312, 10310, 6010, 6011, 6012, 10311,),
    (1, 1, 15): (9313,),
    (1, 0, 0): (6300, 7010,),
    (1, 0, 1): (7011, 8010, 10312, 11310, 7012, 8011, 8012, 6301,),
    (1, 0, 2): (9210, 6302, 7300, 11311, 8300,),
    (1, 0, 3): (10313, 6303,),
    (1, 0, 4): (7301, 11312, 7302, 9211, 8301, 8302,),
    (1, 0, 5): (6200,),
    (1, 0, 6): (7303, 10210, 12310, 8303, 6201,),
    (1, 0, 7): (12311, 6202, 9212,),
    (1, 0, 8): (6203, 7200,),
    (1, 0, 9): (
        7201, 7202, 10211, 9213, 7203, 11313, 12312, 8200, 8201, 8202, 8203, 11210, 13310, 13311, 6100,
    ),
    (1, 0, 10): (9110, 10212, 11211, 7100,),
    (1, 0, 11): (10213, 12313, 8100,),
    (1, 0, 12): (9010, 12210, 13312,),
    (1, 0, 13): (10110, 11212,),
    (1, 0, 14): (9011, 12211, 13313, 6000, 6001, 6002, 6003, 6004, 6005,),
    (1, 0, 15): (9012, 10010, 11213, 11110, 13210,),
    (1, 0, 16): (6400,),
    (2, 0, 0): (
        10011, 12212, 9300, 7400, 7000, 7001, 7002, 7003, 7004, 7005, 11010, 8000, 8001, 8002, 8003, 8004, 8005, 8400,
        13211, 10012, 12213, 9301, 13212, 12110, 10300, 11011, 9302, 13213, 12010, 10301, 11012, 9303, 13110, 11300, 10302, 12011,
        9200, 13010, 11301, 10303, 12012, 9201, 13011, 12300, 10200, 11302, 9202, 13012, 12301, 10201, 11303, 9203, 13300, 11200,
        10202, 12302, 9100, 13301, 11201, 10203, 9400, 12303, 13302, 9000, 12200, 10100, 9001, 11202, 10400, 9002, 12201, 13303,
        9003, 10000, 11203, 9004, 13200, 11100, 10001, 9005, 10002, 12202, 11400, 13201, 11000, 10003, 10004, 12203, 10005, 12100,
        13202, 11001, 11002, 13203, 12400, 12000, 13100, 11003, 11004, 11005, 13400, 12001, 13000, 12002, 12003, 12004, 12005, 13001,
        13002, 13003, 13004, 13005,
    ),
}
NEEDED = {0: "qkv", 5: "proj", 6: "fc1", 7: "fc2"}
DIRECT = ()
KINDS = ("qkv", "proj", "fc1", "fc2")
SHAPES = {"qkv": (3, WIDE, LANES), "proj": (LANES, WIDE), "fc1": (WIDE, WIDE), "fc2": (WIDE, WIDE)}
GRADS = SHAPES | {"fc1": (4, WIDE, LANES)}
CHUNKS = {"qkv": (6, 3), "proj": (1, 1), "fc1": (4, 4), "fc2": (4, 4)}
REST = 192
FIRST_SHARED = 112


def chunk_list():
    names = [(kind, layer, part) for kind in KINDS for layer in range(LAYERS) for part in range(CHUNKS[kind][layer])]
    return names + [("rest", 0, 0)]


def chunk_shape(kind, layer):
    if kind == "rest":
        return REST, LANES, f32
    *outer, tall, wide = GRADS[kind]
    return tall * int(np.prod(outer)) // CHUNKS[kind][layer], wide, bf16


def chunk_place(kind, layer, part):
    tall = chunk_shape(kind, layer)[0]
    if len(GRADS[kind]) == 2:
        return (pl.ds(part * tall, tall),)
    cuts = GRADS[kind][1] // tall
    return part // cuts, pl.ds(part % cuts * tall, tall)


POOLS = (
    ("weights", 80), ("core", 8), ("side", 16), ("half", 16), ("quad", 16), ("spread", 16), ("share", 16), ("last", 3),
)


def scratch_specs(many, loaded):
    rows = lambda kind: pltpu.VMEM((LAYERS, CAN, WIDE), kind)
    specs = {}
    for kind in KINDS:
        specs["w" + kind] = pltpu.VMEM((BLOCKS, LAYERS, *SHAPES[kind]), bf16)
        specs["g" + kind] = pltpu.VMEM((BLOCKS, LAYERS, *GRADS[kind]), bf16)
    specs["small"] = pltpu.VMEM((BLOCKS, LAYERS, 56, LANES), f32)
    specs["lsmall"] = pltpu.VMEM((LAYERS, 56, LANES), f32)
    specs["grest"] = pltpu.VMEM((BLOCKS, REST, LANES), f32)
    for slot, (kind, layer, part) in enumerate(chunk_list()):
        tall, wide, dtype = chunk_shape(kind, layer)
        specs[f"core{slot}"] = pltpu.VMEM((2, tall, wide), dtype)
        specs[f"side{slot}"] = pltpu.VMEM((tall, wide), dtype)
        specs[f"half{slot}"] = pltpu.VMEM((tall // 2, wide), dtype)
        specs[f"quad{slot}"] = pltpu.VMEM((3, tall // 8, wide), dtype)
        specs[f"group{slot}"] = pltpu.VMEM((many.bit_length() - 1, tall // 8, wide), dtype) if many > 1 else None
    for name, dtype in (
        ("unit1", f32), ("normed1", bf16), ("queries", bf16), ("softs", bf16), ("exacts", f32), ("values", bf16),
        ("convs", f32), ("attended", bf16), ("unit2", f32), ("normed2", bf16),
    ):
        specs[name] = rows(dtype)
    specs["streams"] = pltpu.VMEM((LAYERS + 1, CAN, WIDE), f32)
    specs["inv1"] = pltpu.VMEM((LAYERS, CAN, 1), f32)
    specs["inv2"] = pltpu.VMEM((LAYERS, CAN, 1), f32)
    specs["active"] = pltpu.VMEM((LAYERS, BLOCKS, CAN, WIDE), bf16)
    specs["slope"] = pltpu.VMEM((LAYERS, BLOCKS, CAN, WIDE), f32)
    specs["taps"] = pltpu.VMEM((BLOCKS, 49, 8, LANES), f32)
    specs["wide7"] = pltpu.VMEM((7, 2, 56, WIDE), f32)
    specs["wide3"] = pltpu.VMEM((5, 3, 24, WIDE), f32)
    specs["place"] = pltpu.VMEM((CAN, ROWS_IMG), bf16)
    for name, dtype in (("work", f32), ("grads", f32), ("rel", bf16), ("gatt", bf16)):
        specs[name] = pltpu.VMEM((CAN, WIDE), dtype)
    specs["low"] = pltpu.VMEM((CAN, WIDE), bf16)
    specs["hidden"] = pltpu.VMEM((BLOCKS, CAN, WIDE), bf16)
    specs["out"] = pltpu.VMEM((ROWS_IMG, WIDE), bf16)
    specs["fgrad"] = pltpu.VMEM((ROWS_IMG, WIDE), f32)
    for kind in KINDS:
        specs["r" + kind] = pltpu.VMEM((LAYERS, *GRADS[kind]), bf16)
    specs["rrest"] = pltpu.VMEM((REST, LANES), f32)
    specs["rshared"] = pltpu.VMEM((BLOCKS, 32, LANES), f32)
    for name, item in loaded.items():
        specs[name] = pltpu.VMEM(item.shape, item.dtype)
    specs["load_sems"] = pltpu.SemaphoreType.DMA((len(loaded),))
    specs["store_sems"] = pltpu.SemaphoreType.DMA((3,))
    count = len(chunk_list())
    specs["final_sems"] = pltpu.SemaphoreType.DMA((9,))
    specs["weight_recv"] = pltpu.SemaphoreType.DMA((8, 6))
    specs["weight_own"] = pltpu.SemaphoreType.DMA((9,))
    specs["small_recv"] = pltpu.SemaphoreType.DMA((3,))
    specs["grad_recv"] = pltpu.SemaphoreType.DMA((count, 5 + many.bit_length()))
    if many > 1:
        specs["group_send"] = pltpu.SemaphoreType.DMA((many.bit_length() - 1,))
    specs["last_recv"] = pltpu.SemaphoreType.DMA((3,))
    for name, size in POOLS:
        specs["send_" + name] = pltpu.SemaphoreType.DMA((size,))
    return {name: spec for name, spec in specs.items() if spec is not None}


INPUTS = (
    "geometry", "crpe", "head_bias", "fc1_bias", "feats", "ograd", "same", "moves", "tap_mask", "cpe", "bias", "gain", "shift",
)
SHARDS = ("lqkv", "lproj", "lfc1", "lfc2")
OUTPUTS = ("out", "fgrad", "rqkv", "rproj", "rfc1", "rfc2", "rrest", "rshared")
STEPS = (
    Weights.F1, Weights.Y1, Weights.Z1, Weights.YD, Weights.ZD, Weights.XD,
    Gradient.CS, Gradient.CX, Gradient.CO, Gradient.XA, Gradient.YA, Gradient.ZA, Gradient.ZF, Gradient.FN,
)


def target_rows(geometry):
    packed = geometry[0:1]
    crops, sides, places = packed & 7, (packed >> 3) & 7, packed >> 6
    first = places == 0
    big = sides == 7
    code = crops + jnp.where(first, jnp.where(big, 8, 16), 0)
    square = (ROWS_IMG, ROWS_IMG)
    diagonal = lax.broadcasted_iota(jnp.int32, square, 0) == lax.broadcasted_iota(jnp.int32, square, 1)
    column = jnp.sum(jnp.where(diagonal, code.astype(f32), 0.0), axis=1, keepdims=True).astype(jnp.int32)
    earlier = (column & 7) < crops
    seven = jnp.sum(jnp.where(earlier & ((column & 8) > 0), 1.0, 0.0), axis=0, keepdims=True).astype(jnp.int32)
    three = jnp.sum(jnp.where(earlier & ((column & 16) > 0), 1.0, 0.0), axis=0, keepdims=True).astype(jnp.int32)
    cell = jnp.maximum(places - 1, 0)
    row = jnp.where(big, (cell * 37) >> 8, (cell * 43) >> 7)
    col = cell - row * sides
    in_seven = seven * 56 + row * 8 + col
    in_three = END7 + (three >> 1) * 24 + row * 8 + (three & 1) * 4 + col
    classes = END3 + jnp.where(big, seven, 2 + three)
    return jnp.where(first, classes, jnp.where(big, in_seven, in_three))


def step_kernel(many, names, *refs):
    outside = INPUTS + SHARDS + OUTPUTS
    hbm = types.SimpleNamespace(**dict(zip(outside, refs)))
    r = types.SimpleNamespace(**dict(zip(names, refs[len(outside) :])))
    links = Links(many)
    links.group_send = getattr(r, "group_send", None)
    for name, size in POOLS:
        links.pool(name, getattr(r, "send_" + name))
    loads = [
        pltpu.make_async_copy(getattr(hbm, name), getattr(r, name), r.load_sems.at[slot]) for slot, name in enumerate(INPUTS)
    ]
    for load in loads:
        load.start()
    links.meet()
    weights = {}
    for place, kind in enumerate(KINDS):
        local, full = getattr(hbm, "l" + kind), getattr(r, "w" + kind)
        for layer in range(LAYERS):
            slot = place * LAYERS + layer
            weights[kind, layer] = Weights(
                links, local.at[layer], functools.partial(lambda full, layer, block: full.at[block, layer], full, layer),
                r.weight_recv.at[slot], r.weight_own.at[slot], (kind, layer) in DIRECT,
            )
    for layer in range(LAYERS):
        for kind in KINDS:
            weights[kind, layer].start()
            weights[kind, layer].start_near()
    for load in loads[:4]:
        load.wait()
    for layer in range(LAYERS):
        r.lsmall[layer, 0:49] = r.crpe[:, layer]
        r.lsmall[layer, 49:52] = r.head_bias[:, layer]
        for part in range(4):
            r.lsmall[layer, 52 + part : 53 + part] = r.fc1_bias[layer : layer + 1, part * LANES : (part + 1) * LANES]
    small = Small(links, r.lsmall, r.small, r.small_recv, r.weight_own.at[8])
    small.start()
    for load in loads[4:]:
        load.wait()
    gradients = {}
    left = {kind: list(CHUNKS[kind]) for kind in KINDS}
    finals = []

    def write(kind, layer):
        if kind != "rest":
            left[kind][layer] -= 1
            if left[kind][layer]:
                return
        source, target = (
            (r.rrest, hbm.rrest) if kind == "rest" else (getattr(space, "r" + kind).at[layer] for space in (r, hbm))
        )
        finals.append(pltpu.make_async_copy(source, target, r.final_sems.at[len(finals)]))
        finals[-1].start()
        if kind != "rest":
            return
        mine = r.rshared.at[links.block]
        mine[...] = r.rrest[FIRST_SHARED : FIRST_SHARED + 32]
        for slot, other in enumerate((links.by_core, links.by_side, links.by_far)):
            links.send("last", [(mine, mine, other)], r.last_recv.at[slot])

    for slot, (kind, layer, part) in enumerate(chunk_list()):
        if kind == "rest":
            full = lambda block: r.grest.at[block]
            result = r.rrest
        else:
            place = (layer, *chunk_place(kind, layer, part))
            full = functools.partial(lambda whole, place, block: whole.at[(block, *place)], getattr(r, "g" + kind), place)
            result = getattr(r, "r" + kind).at[place]
        gradients[kind, layer, part] = Gradient(
            links, full, *(getattr(r, name + str(slot), None) for name in ("core", "side", "half", "quad", "group")), result,
            functools.partial(write, kind, layer), r.grad_recv.at[slot],
        )

    def point(which, layer, place):
        for code in ORDER.get((which, layer, place), ()):
            step, kind, of_layer, part = code // 1000, code // 100 % 10, code // 10 % 10, code % 10
            kind = (KINDS + ("rest",))[kind]
            STEPS[step](weights[kind, of_layer] if step < 6 else gradients[kind, of_layer, part])

    def forward_point(layer, place):
        point(0, layer, place)
        if layer == 0 and place == 0:
            small.wait()
        if place == 7 and layer == LAYERS - 1:
            fc2_gradients(r, layer, functools.partial(point, 1, layer))
        if place in NEEDED:
            weights[NEEDED[place], layer].wait()

    r.grest[...] = jnp.zeros_like(r.grest)
    target = target_rows(r.geometry[...])
    r.place[...] = (lax.broadcasted_iota(jnp.int32, (CAN, ROWS_IMG), 0) == target).astype(f32).astype(bf16)
    r.streams[0] = mm(r.place[...], r.feats[...])
    r.grads[...] = mm(r.place[...], r.ograd[...])
    for layer in range(LAYERS):
        forward(r, layer, functools.partial(forward_point, layer))
    for layer in reversed(range(LAYERS)):
        if layer < LAYERS - 1:
            fc2_gradients(r, layer, functools.partial(point, 1, layer))
        backward(r, layer, functools.partial(point, 1, layer))
    point(1, 0, 16)
    feed_forward_sum(r, LAYERS - 1)
    r.out[...] = mm_tn(r.place[...], r.work[...].astype(bf16)).astype(bf16)
    r.fgrad[...] = sum(mm_tn(r.place[...], part) for part in halves(r.grads[...]))
    stores = [
        pltpu.make_async_copy(getattr(r, name), getattr(hbm, name), r.store_sems.at[slot])
        for slot, name in enumerate(("out", "fgrad", "rshared"))
    ]
    stores[0].start()
    stores[1].start()
    point(2, 0, 0)
    for slot, block in enumerate((links.block_core, links.block_side, links.block_far)):
        links.arrived(r.rshared.at[block], r.last_recv.at[slot])
    stores[2].start()
    for store in stores:
        store.wait()
    for final in finals:
        final.wait()
    links.finish()


def proj_matrix(r, layer):
    return jnp.concatenate([r.wproj[SLOT[block], layer] for block in range(BLOCKS)], axis=0)


def forward(r, layer, point):
    real = real_rows()
    fill(halves(r.streams[layer]), 1, r.moves, r.wide7, r.wide3)
    for block in range(BLOCKS):
        lanes = lanes_of(block)
        spread_taps(r.taps, block, r.cpe[:, layer, lanes])
        conv = convolve(r.taps, block, 1, 1, 1, False, r.wide7, r.wide3)
        r.work[0:END3, lanes] = r.streams[layer, 0:END3, lanes] + conv + r.bias[0, layer : layer + 1, lanes]
        r.work[END3:CAN, lanes] = r.streams[layer, END3:CAN, lanes]
    unit, inverse, normed = norm_forward(r.work[...], r.gain[layer, 0:1], r.shift[layer, 0:1])
    r.unit1[layer] = unit
    r.inv1[layer] = inverse
    r.normed1[layer] = normed
    point(0)
    for block in range(BLOCKS):
        lanes = lanes_of(block)
        project = mm(normed, side_by_side(r.wqkv[SLOT[block], layer]))
        r.queries[layer, :, lanes] = (project[:, :LANES] + r.small[SLOT[block], layer, 49:50]).astype(bf16)
        r.values[layer, :, lanes] = (project[:, 2 * LANES :] + r.small[SLOT[block], layer, 50:51]).astype(bf16)
        keys = project[:, LANES : 2 * LANES].astype(bf16).astype(f32)
        largest = jnp.max(jnp.where(real, keys, -1e30), axis=0, keepdims=True)
        exponent = jnp.exp(jnp.where(real, keys - largest, 0.0))
        exact = exponent / sum(mm(r.same[...], part) for part in halves(exponent))
        r.exacts[layer, :, lanes] = exact
        r.softs[layer, :, lanes] = exact.astype(bf16)
        spread_taps(r.taps, block, r.small[SLOT[block], layer, 0:49] * r.tap_mask[block, 0:49])
    point(1)
    fill([r.values[layer]], 3, r.moves, r.wide7, r.wide3)
    for block in range(BLOCKS):
        lanes = lanes_of(block)
        query = r.queries[layer, :, lanes]
        soft = r.softs[layer, :, lanes]
        value = r.values[layer, :, lanes]
        factors = []
        for head in range(2):
            masked = jnp.where(head_lanes(head), query, jnp.zeros_like(query))
            mixing = (mm_nt(masked, soft) * SCALE * r.same[...].astype(f32)).astype(bf16)
            factors.append(mm(mixing, value))
        factor = jnp.where(head_lanes(0), factors[0], factors[1])
        conv = convolve(r.taps, block, REACH7[block], REACH3[block], 3, False, r.wide7, r.wide3) + r.small[SLOT[block], layer, 51:52]
        r.convs[layer, 0:END3, lanes] = conv
        r.attended[layer, 0:END3, lanes] = (factor[0:END3] + query[0:END3].astype(f32) * conv).astype(bf16)
        r.attended[layer, END3:CAN, lanes] = factor[END3:CAN].astype(bf16)
        point(2 + block)
    after = r.work[...] + mm(r.attended[layer], proj_matrix(r, layer)) + r.bias[1, layer : layer + 1]
    unit, inverse, normed = norm_forward(after, r.gain[layer, 1:2], r.shift[layer, 1:2])
    r.unit2[layer] = unit
    r.inv2[layer] = inverse
    r.normed2[layer] = normed
    r.work[...] = after + r.bias[2, layer : layer + 1]
    point(6)

    def feed(block, carry):
        hidden = mm(r.normed2[layer], r.wfc1[block, layer]) + jnp.concatenate(
            [r.small[block, layer, 52 + part : 53 + part] for part in range(4)], axis=1
        )
        chance = 0.5 * (1.0 + lax.erf(hidden * np.float32(0.5**0.5)))
        density = jnp.exp(hidden * hidden * -0.5) * np.float32((2 * np.pi) ** -0.5)
        r.slope[layer, block] = chance + hidden * density
        r.active[layer, block] = (hidden * chance).astype(bf16)
        return carry

    lax.fori_loop(0, BLOCKS, feed, 0)
    point(7)

    if layer < LAYERS - 1:
        feed_forward_sum(r, layer)
        r.streams[layer + 1] = r.work[...]
    else:
        r.streams[LAYERS] = r.work[...]


def feed_forward_sum(r, layer):
    if layer == LAYERS - 1:
        r.work[...] = r.streams[LAYERS]

    def collect(block, carry):
        r.work[...] += mm(r.active[layer, block], r.wfc2[block, layer])
        return carry

    lax.fori_loop(0, BLOCKS, collect, 0)


def put_shared(r, layer, row, value):
    for block in range(BLOCKS):
        first = FIRST_SHARED + 16 * layer + row
        r.grest[SLOT[block], first : first + 1] = value[:, block * LANES : (block + 1) * LANES]


def fc2_gradients(r, layer, point):
    put_shared(r, layer, 11, column_sum(r.grads[...]))
    r.low[...] = r.grads[...].astype(bf16)
    for part in range(4):
        rows = lanes_of(part)
        joined = jnp.concatenate([r.active[layer, block, :, rows] for block in range(BLOCKS)], axis=1)
        product = mm_tn(joined, r.low[...]).astype(bf16)
        for block in range(BLOCKS):
            r.gfc2[block, layer, rows] = product[block * LANES : (block + 1) * LANES]
        point(part)


def backward(r, layer, point):
    def put_small(block, row, value):
        r.grest[block, 56 * layer + row : 56 * layer + row + value.shape[0]] = value

    r.work[...] = jnp.zeros_like(r.work)

    def feed(block, carry):
        hidden = (mm_nt(r.low[...], r.wfc2[block, layer]) * r.slope[layer, block]).astype(bf16)
        sums = column_sum(hidden.astype(f32))
        for part in range(4):
            row = 56 * layer + 52 + part
            r.grest[block, row : row + 1] = sums[:, part * LANES : (part + 1) * LANES]
        r.hidden[block] = hidden
        return carry

    lax.fori_loop(0, BLOCKS, feed, 0)
    point(4)
    for part in range(4):
        joined = jnp.concatenate([r.hidden[block, :, lanes_of(part)] for block in range(BLOCKS)], axis=1)
        product = mm_tn(r.normed2[layer], joined).astype(bf16)
        for block in range(BLOCKS):
            r.gfc1[block, layer, part] = product[:, block * LANES : (block + 1) * LANES]
        point(5 + part)

    def collect(block, carry):
        r.work[...] += mm_nt(r.hidden[block], r.wfc1[block, layer])
        return carry

    lax.fori_loop(0, BLOCKS, collect, 0)
    incoming = r.work[...]
    unit = r.unit2[layer]
    put_shared(r, layer, 13, column_sum(incoming * unit))
    put_shared(r, layer, 15, column_sum(incoming))
    r.grads[...] = r.grads[...] + norm_backward(incoming, unit, r.inv2[layer], r.gain[layer, 1:2])
    branch = r.grads[...]
    put_shared(r, layer, 10, column_sum(branch))
    branch = branch.astype(bf16)
    product = mm_tn(r.attended[layer], branch).astype(bf16)
    for block in range(BLOCKS):
        r.gproj[SLOT[block], layer] = product[block * LANES : (block + 1) * LANES]
    r.gatt[...] = mm_nt(branch, proj_matrix(r, layer)).astype(bf16)
    point(9)
    fill([r.values[layer]], 3, r.moves, r.wide7, r.wide3)
    for block in range(BLOCKS):
        lanes = lanes_of(block)
        product = r.gatt[0:END3, lanes].astype(f32) * r.queries[layer, 0:END3, lanes].astype(f32)
        r.rel[0:END3, lanes] = product.astype(bf16)
        r.rel[END3:CAN, lanes] = jnp.zeros((CAN - END3, LANES), bf16)
        put_small(SLOT[block], 51, column_sum(product))
        sums = tap_grads(product, block, REACH7[block], REACH3[block], 3, r.taps, r.wide7, r.wide3)
        put_small(SLOT[block], 0, sums * r.tap_mask[block, 0:49])
        spread_taps(r.taps, block, r.small[SLOT[block], layer, 0:49] * r.tap_mask[block, 0:49])
    point(10)
    fill([r.rel[...]], 3, r.moves, r.wide7, r.wide3)
    r.work[...] = jnp.zeros_like(r.work)
    for block in range(BLOCKS):
        lanes = lanes_of(block)
        query = r.queries[layer, :, lanes]
        soft = r.softs[layer, :, lanes]
        value = r.values[layer, :, lanes]
        grad = r.gatt[:, lanes]
        exact = r.exacts[layer, :, lanes]
        picked = []
        for head in range(2):
            chosen = head_lanes(head)
            zero = jnp.zeros_like(query)
            query_head = jnp.where(chosen, query, zero)
            grad_head = jnp.where(chosen, grad, zero)
            same_low = r.same[...]
            mixing_t = (mm_nt(soft, query_head) * SCALE * same_low.astype(f32)).astype(bf16)
            mix = mm_nt(grad_head, value).astype(bf16) * same_low
            mix_t = mm_nt(value, grad_head).astype(bf16) * same_low
            picked.append((mm(mixing_t, grad), SCALE * mm(mix, soft), SCALE * mm(mix_t, query)))
        grad_value, grad_query, grad_soft = (
            jnp.where(head_lanes(0), one, two) for one, two in zip(*picked)
        )
        grad_soft = grad_soft.astype(bf16).astype(f32)
        weighted = grad_soft * exact
        grad_key = weighted - exact * sum(mm(r.same[...], part) for part in halves(weighted))
        conv = convolve(r.taps, block, REACH7[block], REACH3[block], 3, True, r.wide7, r.wide3)
        grad_value = jnp.concatenate([grad_value[0:END3] + conv, grad_value[END3:CAN]], axis=0).astype(bf16)
        grad_query = jnp.concatenate(
            [grad_query[0:END3] + grad[0:END3].astype(f32) * r.convs[layer, 0:END3, lanes], grad_query[END3:CAN]], axis=0
        ).astype(bf16)
        put_small(SLOT[block], 49, column_sum(grad_query.astype(f32)))
        put_small(SLOT[block], 50, column_sum(grad_value.astype(f32)))
        joined = jnp.concatenate([grad_query, grad_key.astype(bf16), grad_value], axis=1)
        product = mm_tn(r.normed1[layer], joined).astype(bf16)
        for part in range(3):
            r.gqkv[SLOT[block], layer, part] = product[:, part * LANES : (part + 1) * LANES]
        r.work[...] += mm_nt(joined, side_by_side(r.wqkv[SLOT[block], layer]))
        point(11 + block)
    incoming = r.work[...]
    unit = r.unit1[layer]
    put_shared(r, layer, 12, column_sum(incoming * unit))
    put_shared(r, layer, 14, column_sum(incoming))
    r.grads[...] = r.grads[...] + norm_backward(incoming, unit, r.inv1[layer], r.gain[layer, 0:1])
    fill(halves(r.streams[layer]), 1, r.moves, r.wide7, r.wide3)
    for block in range(BLOCKS):
        lanes = lanes_of(block)
        product = r.grads[0:END3, lanes]
        first = FIRST_SHARED + 16 * layer
        r.grest[SLOT[block], first + 9 : first + 10] = column_sum(product)
        r.grest[SLOT[block], first : first + 9] = tap_grads(product, block, 1, 1, 1, r.taps, r.wide7, r.wide3)
    fill(halves(r.grads[...]), 1, r.moves, r.wide7, r.wide3)
    for block in range(BLOCKS):
        lanes = lanes_of(block)
        spread_taps(r.taps, block, r.cpe[:, layer, lanes])
        conv = convolve(r.taps, block, 1, 1, 1, True, r.wide7, r.wide3)
        r.grads[0:END3, lanes] = r.grads[0:END3, lanes] + conv
    point(15)


def widen(target, source, layer):
    cut = len(source.shape) > len(target.shape)
    tall, wide = source.shape[-2:]
    for lead in np.ndindex(*source.shape[1:-2]):
        into = (slice(None), pl.ds(lead[0] * wide, wide)) if cut else (*lead, slice(None), slice(None))
        view, seen = target.at[(layer, *into)], source.at[(layer, *lead)]

        def body(index, carry):
            rows = pl.ds(pl.multiple_of(index * 128, 128), 128)
            view[rows] = seen[rows].astype(f32)
            return carry

        lax.fori_loop(0, tall // 128, body, 0)


def finish_kernel(count, *refs):
    taken, given = refs[:8], refs[8 : 8 + count]
    inside, made, load_sems, store_sems = refs[8 + count : 16 + count], refs[16 + count : -2], refs[-2], refs[-1]
    large = [(source, slot, layer) for source, slot in ((3, 10), (2, 8), (0, 4), (1, 7)) for layer in range(LAYERS)]
    large_loads = [
        pltpu.make_async_copy(taken[source].at[layer], inside[source].at[layer], load_sems.at[place])
        for place, (source, slot, layer) in enumerate(large)
    ]
    loads = {
        slot: pltpu.make_async_copy(taken[slot], inside[slot], load_sems.at[4 + slot]) for slot in range(4, 8)
    }
    for load in large_loads + list(loads.values()):
        load.start()
    stores = {
        slot: pltpu.make_async_copy(source, target, store_sems.at[slot])
        for slot, (source, target) in enumerate(zip(tuple(inside[6:]) + tuple(made), given))
        if slot - 2 not in (4, 7, 8, 10)
    }
    cpe, bias, gain, shift, qkv, head_bias, crpe, proj, fc1, fc1_bias, fc2 = made
    large_stores = []
    for place, (source, slot, layer) in enumerate(large):
        large_loads[place].wait()
        widen(made[slot], inside[source], layer)
        sem = store_sems.at[len(given) + place]
        large_stores.append(pltpu.make_async_copy(made[slot].at[layer], given[2 + slot].at[layer], sem))
        large_stores[-1].start()
    for slot in (6, 7):
        loads[slot].wait()
        stores[slot - 6].start()
    loads[4].wait()
    loads[5].wait()
    rrest, rshared = inside[4:6]
    for layer in range(LAYERS):
        for block in range(BLOCKS):
            lanes = lanes_of(block)
            first = layer * 16
            cpe[:, layer, lanes] = rshared[SLOT[block], first : first + 9]
            bias[:, layer, lanes] = rshared[SLOT[block], first + 9 : first + 12]
            gain[layer, :, lanes] = rshared[SLOT[block], first + 12 : first + 14]
            shift[layer, :, lanes] = rshared[SLOT[block], first + 14 : first + 16]
            fc1_bias[layer : layer + 1, lanes] = rrest[layer * 56 + 52 + block : layer * 56 + 53 + block]
        crpe[:, layer] = rrest[layer * 56 : layer * 56 + 49]
        head_bias[:, layer] = rrest[layer * 56 + 49 : layer * 56 + 52]
    for slot in (0, 1, 2, 3, 5, 6, 9):
        stores[2 + slot].start()
    for copy in large_stores + list(stores.values()):
        copy.wait()


def shards(
    data, features, crop_index, grid_size, position, cpe_weight, shared_bias, norm_gain, norm_bias,
    qkv_weight, head_bias, crpe_weight, proj_weight, fc1_weight, fc1_bias, fc2_weight, out_grad,
):
    many = data // 8
    assert data == 8 * many and many & (many - 1) == 0 and features.shape[0] == ROWS_IMG
    start = lax.axis_index("mp") * ROWS_IMG
    mine = [lax.dynamic_slice_in_dim(item, start, ROWS_IMG) for item in (crop_index, grid_size, position)]
    packed = (mine[0] & 7) + 8 * mine[1] + 64 * mine[2]
    geometry = jnp.broadcast_to(packed[None], (8, ROWS_IMG))
    same, moves = canonical_tables()
    swap = lambda item: jnp.transpose(item, (1, 0, 2))
    hbm = pl.BlockSpec(memory_space=pl.ANY)
    shape = jax.ShapeDtypeStruct
    loaded = dict(
        zip(
            INPUTS,
            (
                geometry, swap(crpe_weight), swap(head_bias), fc1_bias, features, out_grad, jnp.asarray(same, bf16),
                jnp.asarray(moves, bf16), jnp.asarray(tap_table()), swap(cpe_weight), swap(shared_bias), norm_gain, norm_bias,
            ),
        )
    )
    specs = scratch_specs(many, loaded)
    results = pl.pallas_call(
        functools.partial(step_kernel, many, tuple(specs)),
        out_shape=(
            shape((ROWS_IMG, WIDE), bf16),
            shape((ROWS_IMG, WIDE), f32),
            *(shape((LAYERS, *GRADS[kind]), bf16) for kind in KINDS),
            shape((REST, LANES), f32),
            shape((BLOCKS, 32, LANES), f32),
        ),
        in_specs=[hbm] * len(INPUTS + SHARDS),
        out_specs=(hbm,) * len(OUTPUTS),
        scratch_shapes=list(specs.values()),
        compiler_params=pltpu.CompilerParams(
            vmem_limit_bytes=63 * 2**20, collective_id=0, has_side_effects=True
        ),
        name="step",
    )(
        *loaded.values(), jnp.transpose(qkv_weight, (0, 2, 1, 3)), proj_weight, fc1_weight, fc2_weight
    )
    out, fgrad, rqkv, rproj, rfc1, rfc2, rrest, rshared = results
    taken = (rqkv, rproj, rfc1, rfc2, rrest, rshared, out, fgrad)
    swapped = lambda item: (item.shape[1], item.shape[0], item.shape[2])
    given = [
        shape(dims, f32)
        for dims in (
            fgrad.shape, swapped(cpe_weight), swapped(shared_bias), norm_gain.shape, norm_bias.shape, rqkv.shape,
            swapped(head_bias), swapped(crpe_weight), rproj.shape, fc1_weight.shape, fc1_bias.shape, rfc2.shape,
        )
    ]
    given = [shape(out.shape, bf16)] + given
    final = list(
        pl.pallas_call(
            functools.partial(finish_kernel, len(given)),
            out_shape=given,
            in_specs=[hbm] * len(taken),
            out_specs=[hbm] * len(given),
            scratch_shapes=[pltpu.VMEM(item.shape, item.dtype) for item in list(taken) + given[2:]]
            + [pltpu.SemaphoreType.DMA((12,)), pltpu.SemaphoreType.DMA((len(given) + 8,))],
            compiler_params=pltpu.CompilerParams(vmem_limit_bytes=63 * 2**20),
            name="finish",
        )(*taken)
    )
    for index in (2, 3, 7, 8):
        final[index] = swap(final[index])
    final[6] = jnp.transpose(final[6], (0, 2, 1, 3))
    return tuple(final)


def solution(mesh):
    placed = (
        P(("dp", "mp"), None),
        P("dp"),
        P("dp"),
        P("dp"),
        P(),
        P(),
        P(),
        P(),
        P(None, None, None, "mp"),
        P(None, None, "mp"),
        P(None, None, "mp"),
        P(None, "mp", None),
        P(None, None, "mp"),
        P(None, "mp"),
        P(None, "mp", None),
        P(("dp", "mp"), None),
    )
    return jax.shard_map(
        functools.partial(shards, mesh.shape["dp"]),
        mesh=mesh,
        in_specs=placed,
        out_specs=(
            P(("dp", "mp"), None),
            P(("dp", "mp"), None),
            P(),
            P(),
            P(),
            P(),
            P(None, None, None, "mp"),
            P(None, None, "mp"),
            P(None, None, "mp"),
            P(None, "mp", None),
            P(None, None, "mp"),
            P(None, "mp"),
            P(None, "mp", None),
        ),
        check_vma=False,
    )
```

```python
import functools
import types

import jax
import jax.numpy as jnp
import numpy as np
from jax import lax
from jax.experimental import pallas as pl
from jax.experimental.pallas import tpu as pltpu
from jax.sharding import PartitionSpec as P

HD = 64
LAYERS = 2
ROWS_IMG = 160
CAN = 192
END7 = 112
END3 = 184
LANES = 128
WIDE = 512
BLOCKS = 4
SLOT = (0, 2, 1, 3)
EPSILON = 1e-06
SCALE = HD ** (-0.5)
REACH7 = (1, 2, 3, 3)
REACH3 = (1, 2, 2, 2)
MESH = pl.DeviceIdType.MESH
f32 = jnp.float32
bf16 = jnp.bfloat16


def canonical_tables():
    crop = np.full(CAN, 100)
    col = np.full(CAN, -1)
    side = np.zeros(CAN, int)
    for t in range(END7):
        if t % 8 < 7:
            crop[t], col[t], side[t] = t // 56, t % 8, 7
    for t in range(END7, END3):
        u = t - END7
        if t % 4 < 3:
            crop[t], col[t], side[t] = 2 + 2 * (u // 24) + (t % 8) // 4, t % 4, 3
    for t in range(END3, CAN):
        crop[t] = t - END3
    same = (crop[:, None] == crop[None, :]).astype(np.float32)
    moves = np.zeros((7, CAN, CAN), np.float32)
    for b in range(-3, 4):
        for t in range(END3):
            if col[t] >= 0 and 0 <= col[t] + b < side[t]:
                moves[b + 3, t, t + b] = 1
    return same, moves


def tap_table():
    table = np.zeros((BLOCKS, 56, LANES), np.float32)
    for channel in range(WIDE):
        head = channel // HD
        reach = 1 if head < 2 else 2 if head < 5 else 3
        for tap in range(49):
            if max(abs(tap // 7 - 3), abs(tap % 7 - 3)) <= reach:
                table[channel // LANES, tap, channel % LANES] = 1
    return table


def mm(left, right):
    return jnp.dot(left, right, preferred_element_type=f32)


def mm_nt(left, right):
    return lax.dot_general(left, right, (((1,), (1,)), ((), ())), preferred_element_type=f32)


def mm_tn(left, right):
    return lax.dot_general(left, right, (((0,), (0,)), ((), ())), preferred_element_type=f32)


def side_by_side(parts):
    return jnp.concatenate([parts[index] for index in range(parts.shape[0])], axis=1)


def stream_parts(r, layer):
    return [r.streams[0].astype(bf16)] if layer == 0 else halves(r.streams[layer])


def halves(values):
    high = values.astype(bf16)
    return [high, (values - high.astype(f32)).astype(bf16)]


def lanes_of(block):
    return pl.ds(block * LANES, LANES)


def column_sum(values):
    return jnp.sum(values, axis=0, keepdims=True)


def fill(parts, reach, moves, wide7, wide3):
    for b in range(-reach, reach + 1):
        moved = sum(mm(moves[b + 3], part) if b else part.astype(f32) for part in parts)
        for grid in range(2):
            wide7[b + 3, grid] = moved[grid * 56 : grid * 56 + 56]
        if abs(b) <= 2:
            for pair in range(3):
                first = END7 + pair * 24
                wide3[b + 2, pair] = moved[first : first + 24]


def tap_row(a, b, half, flip):
    if flip:
        a, b = -a, -b
    return (a + half) * (2 * half + 1) + b + half


def spread_taps(spread, block, rows):
    for row in range(rows.shape[0]):
        spread[block, row] = jnp.broadcast_to(rows[row : row + 1], (8, LANES))


def grid_rows(wide, place, side, lanes):
    return [wide[place, :, row * 8 : row * 8 + 8, lanes] for row in range(side)]


def convolve(spread, block, reach7, reach3, half, flip, wide7, wide3):
    lanes = lanes_of(block)

    def loop(wide, offset, reach, grids, side):
        def body(step, sums):
            b = step - reach
            rows = grid_rows(wide, b + offset, side, lanes)
            sums = list(sums)
            for a in range(-reach, reach + 1):
                weight = spread[block, tap_row(a, b, half, flip)]
                for row in range(max(0, -a), min(side, side - a)):
                    sums[row] = sums[row] + weight * rows[row + a]
            return tuple(sums)

        start = tuple(jnp.zeros((grids, 8, LANES), f32) for _ in range(side))
        sums = lax.fori_loop(0, 2 * reach + 1, body, start)
        return [sums[row][grid] for grid in range(grids) for row in range(side)]

    return jnp.concatenate(loop(wide7, 3, reach7, 2, 7) + loop(wide3, 2, reach3, 3, 3), axis=0)


def tap_grads(grad, block, reach7, reach3, half, spread, wide7, wide3):
    lanes = lanes_of(block)
    count = (2 * half + 1) ** 2
    spread[block, 0:count] = jnp.zeros((count, 8, LANES), f32)

    def loop(wide, offset, reach, part, side):
        def body(step, carry):
            b = step - reach
            rows = grid_rows(wide, b + offset, side, lanes)
            for a in range(-reach, reach + 1):
                total = sum(part[:, row * 8 : row * 8 + 8] * rows[row + a] for row in range(max(0, -a), min(side, side - a)))
                spread[block, tap_row(a, b, half, False)] += jnp.sum(total, axis=0)
            return carry

        lax.fori_loop(0, 2 * reach + 1, body, 0)

    loop(wide7, 3, reach7, grad[:END7].reshape(2, 56, LANES), 7)
    loop(wide3, 2, reach3, grad[END7:END3].reshape(3, 24, LANES), 3)
    return jnp.sum(spread[block, 0:count], axis=1)


def norm_forward(values, gain, bias):
    center = values - jnp.mean(values, axis=-1, keepdims=True)
    spread = jnp.mean(center * center, axis=-1, keepdims=True)
    inverse = lax.rsqrt(spread + EPSILON)
    unit = center * inverse
    return unit, inverse, (unit * gain + bias).astype(bf16)


def norm_backward(incoming, unit, inverse, gain):
    scaled = incoming * gain
    mean_one = jnp.mean(scaled, axis=-1, keepdims=True)
    mean_two = jnp.mean(scaled * unit, axis=-1, keepdims=True)
    return inverse * (scaled - mean_one - unit * mean_two)


def real_rows():
    row = lax.broadcasted_iota(jnp.int32, (CAN, LANES), 0)
    seven = (row < END7) & ((row & 7) != 7)
    three = (row >= END7) & (row < END3) & ((row & 3) != 3)
    return seven | three | (row >= END3)


def head_lanes(head):
    lane = lax.broadcasted_iota(jnp.int32, (CAN, LANES), 1)
    return (lane >= HD) if head else (lane < HD)


def rows_of(ref, start, count):
    rows = pl.ds(pl.multiple_of(start, 8), count)
    return ref.at[rows] if len(ref.shape) == 2 else ref.at[:, rows]


def add_rows(target, start, source, first, count):
    step = next(size for size in (64, 48, 32, 24, 16, 8) if count % size == 0)

    def body(index, carry):
        into = pl.ds(pl.multiple_of(start + index * step, 8), step)
        target[into] = target[into] + source[pl.ds(pl.multiple_of(first + index * step, 8), step)]
        return carry

    lax.fori_loop(0, count // step, body, 0)


class Links:
    def __init__(self, many):
        dp, mp = lax.axis_index("dp"), lax.axis_index("mp")
        self.many = many
        self.core, self.side = lax.rem(mp, 2), lax.div(mp, 2)
        self.half, self.quad, self.group = lax.rem(dp, 2), lax.rem(lax.div(dp, 2), 4), lax.div(dp, 8)
        self.block = self.core * 2 + self.side
        self.block_core = (1 - self.core) * 2 + self.side
        self.block_side = self.core * 2 + 1 - self.side
        self.block_far = (1 - self.core) * 2 + 1 - self.side
        self.by_core = (dp, self.side * 2 + 1 - self.core)
        self.by_side = (dp, (1 - self.side) * 2 + self.core)
        self.by_far = (dp, (1 - self.side) * 2 + 1 - self.core)
        self.by_half = (dp + 1 - 2 * self.half, mp)
        self.by_quad = [
            (self.group * 8 + lax.rem(self.quad + step, 4) * 2 + self.half, mp) for step in range(1, 4)
        ]
        self.rounds = many.bit_length() - 1
        self.by_group = []
        for step in range(self.rounds):
            bit = lax.rem(lax.div(self.group, 1 << step), 2)
            partner = self.group + (1 - 2 * bit) * (1 << step)
            self.by_group.append((partner * 8 + self.quad * 2 + self.half, mp))
        self.pair = lax.rem(self.quad, 2)
        self.by_pair = (self.group * 8 + (self.quad + 1 - 2 * self.pair) * 2 + self.half, mp)
        self.pools = {}

    def meet(self):
        barrier = pltpu.get_barrier_semaphore()
        others = [self.by_core, self.by_side, self.by_far, self.by_half] + self.by_quad + self.by_group
        for other in others:
            pl.semaphore_signal(barrier, inc=1, device_id=other, device_id_type=MESH)
        pl.semaphore_wait(barrier, len(others))

    def pool(self, name, sems):
        self.pools[name] = [sems, [None] * sems.shape[0], 0]

    def take(self, name, waiter):
        sems, waiters, place = self.pools[name]
        if waiters[place] is not None:
            waiters[place]()
        waiters[place] = waiter
        self.pools[name][2] = (place + 1) % len(waiters)
        return sems.at[place]

    def copy(self, source, target, send_sem, recv_sem, other):
        return pltpu.make_async_remote_copy(
            src_ref=source, dst_ref=target, send_sem=send_sem, recv_sem=recv_sem, device_id=other, device_id_type=MESH
        )

    def send(self, name, items, recv_sem, whole=None):
        box = []
        send_sem = self.take(name, lambda: box[0].wait_send())
        copies = [self.copy(source, target, send_sem, recv_sem, other) for source, target, other in items]
        box.append(copies[0] if whole is None else self.copy(whole, whole, send_sem, recv_sem, self.by_core))
        for copy in copies:
            copy.start()

    def arrived(self, target, recv_sem):
        self.copy(target, target, recv_sem, recv_sem, self.by_core).wait_recv()

    def finish(self):
        for sems, waiters, place in self.pools.values():
            for waiter in waiters:
                if waiter is not None:
                    waiter()


class Weights:
    def __init__(self, links, local, full, recv_sems, own_sem, direct):
        self.links, self.local, self.full, self.direct = links, local, full, direct
        self.recv_sems, self.own_sem = recv_sems, own_sem
        self.count = local.shape[-2] // 4
        self.sub = self.count // 2

    def start_of(self, half, pair):
        return (half * 2 + pair) * self.count

    def places(self):
        links = self.links
        far = self.start_of(1 - links.half, 1 - links.pair)
        near = (
            (self.start_of(links.half, links.pair), self.count),
            (self.start_of(1 - links.half, links.pair), self.count),
            (self.start_of(links.half, 1 - links.pair), self.count),
        )
        return near + (((far, self.count),) if self.direct else ((far + self.sub, self.sub), (far, self.sub)))

    def push(self, part, slot, other):
        self.links.send("weights", [(part, part, other)], self.recv_sems.at[slot])

    def take(self, index):
        start, count = self.places()[index]
        part = rows_of(self.full(self.links.block_side), start, count)
        self.links.arrived(part, self.recv_sems.at[index])
        self.push(part, 5, self.links.by_core)
        return part

    def start(self):
        links = self.links
        for index in (0, 3) if self.direct else (0,):
            start, count = self.places()[index]
            target = rows_of(self.full(links.block), start, count)
            links.send("weights", [(rows_of(self.local, start, count), target, links.by_side)], self.recv_sems.at[index])

    def start_near(self):
        links = self.links
        links.send("weights", [(self.local, self.full(links.block), links.by_core)], self.recv_sems.at[5])
        self.own = pltpu.make_async_copy(self.local, self.full(links.block), self.own_sem)
        self.own.start()

    def F1(self):
        part = self.take(0)
        self.push(part, 1, self.links.by_half)
        self.push(part, 2, self.links.by_pair)

    def Y1(self):
        part = self.take(1)
        if not self.direct:
            self.push(rows_of(part, 0, self.sub), 4, self.links.by_pair)

    def Z1(self):
        part = self.take(2)
        if not self.direct:
            self.push(rows_of(part, self.sub, self.sub), 3, self.links.by_half)

    def YD(self):
        self.take(3)

    def ZD(self):
        self.take(4)

    def XD(self):
        self.take(3)

    def wait(self):
        self.own.wait()
        self.links.arrived(self.full(pl.ds((1 - self.links.core) * 2, 2)), self.recv_sems.at[5])


class Small:
    def __init__(self, links, local, full, recv_sems, own_sem):
        self.links, self.local, self.full, self.recv_sems, self.own_sem = links, local, full, recv_sems, own_sem

    def start(self):
        links = self.links
        for slot, other in enumerate((links.by_side, links.by_core)):
            links.send("weights", [(self.local, self.full.at[links.block], other)], self.recv_sems.at[slot])
        self.own = pltpu.make_async_copy(self.local, self.full.at[links.block], self.own_sem)
        self.own.start()

    def wait(self):
        links = self.links
        part = self.full.at[links.block_side]
        links.arrived(part, self.recv_sems.at[0])
        links.send("weights", [(part, part, links.by_core)], self.recv_sems.at[2])
        self.own.wait()
        links.arrived(self.full.at[links.block_core], self.recv_sems.at[1])
        links.arrived(self.full.at[links.block_far], self.recv_sems.at[2])


class Gradient:
    def __init__(self, links, full, core_in, side_in, half_in, quad_in, group_in, result, final, recv_sems):
        self.links, self.full, self.result, self.final = links, full, result, final
        self.core_in, self.side_in, self.half_in, self.quad_in, self.group_in = core_in, side_in, half_in, quad_in, group_in
        self.recv_sems = recv_sems
        self.tall = result.shape[0]
        self.half, self.piece = self.tall // 2, self.tall // 8
        self.here, self.there = links.half * self.half, (1 - links.half) * self.half
        self.mine = self.here + links.quad * self.piece

    def CS(self):
        links = self.links
        source = self.full(pl.ds((1 - links.core) * 2, 2))
        links.send("core", [(source, self.core_in, links.by_core)], self.recv_sems.at[0])

    def CX(self):
        links = self.links
        links.arrived(self.core_in, self.recv_sems.at[0])
        part = self.full(links.block_side)
        add_rows(part, 0, self.core_in.at[1 - links.side], 0, self.tall)
        links.send("side", [(part, self.side_in, links.by_side)], self.recv_sems.at[1])

    def CO(self):
        links = self.links
        add_rows(self.full(links.block), 0, self.core_in.at[links.side], 0, self.tall)

    def XA(self):
        links = self.links
        links.arrived(self.side_in, self.recv_sems.at[1])
        total = self.full(links.block)
        add_rows(total, self.there, self.side_in, self.there, self.half)
        links.send("half", [(rows_of(total, self.there, self.half), self.half_in, links.by_half)], self.recv_sems.at[2])
        add_rows(total, self.here, self.side_in, self.here, self.half)

    def YA(self):
        links = self.links
        links.arrived(self.half_in, self.recv_sems.at[2])
        total = self.full(links.block)
        add_rows(total, self.here, self.half_in, 0, self.half)
        items = []
        for step in range(3):
            start = self.here + lax.rem(links.quad + step + 1, 4) * self.piece
            items.append((rows_of(total, start, self.piece), self.quad_in.at[step], links.by_quad[step]))
        links.send("quad", items, self.recv_sems.at[3], self.quad_in)

    def ZA(self):
        links = self.links
        mine = pl.ds(pl.multiple_of(self.mine, 8), self.piece)
        total = self.full(links.block)
        links.arrived(self.quad_in, self.recv_sems.at[3])
        value = total[mine].astype(f32)
        for step in range(3):
            value = value + self.quad_in[step].astype(f32)
        if links.many > 1:
            for step in range(links.rounds):
                total[mine] = value.astype(total.dtype)
                copy = links.copy(
                    total.at[mine], self.group_in.at[step], links.group_send.at[step], self.recv_sems.at[6 + step],
                    links.by_group[step],
                )
                copy.start()
                copy.wait()
                value = total[mine].astype(f32) + self.group_in[step].astype(f32)
        part = self.result.at[mine]
        part[...] = value.astype(self.result.dtype)
        links.send("spread", [(part, part, other) for other in links.by_quad], self.recv_sems.at[4], self.quad_in)

    def ZF(self):
        links = self.links
        links.arrived(self.quad_in, self.recv_sems.at[4])
        part = rows_of(self.result, self.here, self.half)
        links.send("share", [(part, part, links.by_half)], self.recv_sems.at[5])

    def FN(self):
        self.links.arrived(rows_of(self.result, self.there, self.half), self.recv_sems.at[5])
        self.final()


ORDER = {
    (0, 0, 0): (
        0, 100, 200, 2000, 1000, 2100, 1100, 300, 10, 110, 2200, 1200, 4000, 4100, 3000,
    ),
    (0, 0, 1): (210, 2300, 1300, 3100,),
    (0, 0, 2): (310,),
    (0, 0, 3): (2010,),
    (0, 0, 4): (1010, 2110,),
    (0, 0, 5): (1110,),
    (0, 0, 6): (4200, 3200,),
    (0, 0, 7): (2210, 1210, 4300, 3300,),
    (0, 1, 0): (2310, 1310, 4010, 4110, 3010,),
    (0, 1, 1): (3110, 4210, 3210,),
    (0, 1, 2): (4310, 3310,),
    (1, 1, 0): (6310,),
    (1, 1, 1): (6311,),
    (1, 1, 2): (6312,),
    (1, 1, 3): (6313,),
    (1, 1, 5): (7310, 8310, 6210, 7311,),
    (1, 1, 6): (7312, 8311, 8312, 6211,),
    (1, 1, 7): (7313, 8313, 6212,),
    (1, 1, 8): (6213,),
    (1, 1, 9): (7210, 7211, 8210, 7212, 8211, 8212, 6110,),
    (1, 1, 10): (7213, 9310, 8213,),
    (1, 1, 11): (7110, 9311, 8110,),
    (1, 1, 14): (9312, 6010, 6011, 6012,),
    (1, 1, 15): (10310, 9313, 10311,),
    (1, 0, 0): (7010, 8010, 6300, 7011,),
    (1, 0, 1): (8011, 7012, 6301, 8012,),
    (1, 0, 2): (6302,),
    (1, 0, 3): (9210, 10312, 6303, 7300,),
    (1, 0, 4): (7301, 8300, 8301,),
    (1, 0, 5): (7302, 10313, 9211, 8302, 7303, 6200, 11310, 8303,),
    (1, 0, 6): (6201,),
    (1, 0, 7): (6202,),
    (1, 0, 8): (11311, 10210, 6203,),
    (1, 0, 9): (
        7200, 7201, 7202, 9212, 11312, 10211, 7203, 8200, 8201, 9213, 8202, 8203, 6100,
    ),
    (1, 0, 10): (11313, 12310,),
    (1, 0, 11): (7100, 9110, 12311, 10212, 8100,),
    (1, 0, 12): (11210, 9010, 10213,),
    (1, 0, 13): (12312,),
    (1, 0, 14): (11211, 13310, 6000, 6001, 6002, 6003, 6004, 6005, 9011, 10110, 12313,),
    (1, 0, 15): (11212, 13311,),
    (1, 0, 16): (6400,),
    (2, 0, 0): (
        9012, 10010, 12210, 13312, 7400, 7000, 7001, 7002, 7003, 7004, 7005, 9300, 11213, 8000, 8001, 8002, 10011, 12211,
        8003, 8004, 8005, 8400, 13313, 11110, 9301, 10012, 12212, 13210, 11010, 9302, 10300, 12213, 13211, 11011, 9303, 10301,
        12110, 13212, 11012, 9200, 10302, 12010, 13213, 11300, 9201, 10303, 12011, 13110, 11301, 9202, 10200, 12012, 13010, 11302,
        9203, 10201, 12300, 13011, 11303, 9100, 10202, 12301, 13012, 9400, 11200, 10203, 9000, 12302, 13300, 9001, 11201, 10100,
        9002, 12303, 13301, 9003, 11202, 10400, 9004, 12200, 10000, 9005, 11203, 13302, 10001, 12201, 10002, 11100, 13303, 10003,
        12202, 10004, 11400, 13200, 11000, 10005, 12203, 13201, 11001, 11002, 13202, 12100, 11003, 11004, 13203, 12400, 12000, 11005,
        12001, 13100, 12002, 12003, 12004, 13400, 13000, 13001, 12005, 13002, 13003, 13004, 13005,
    ),
}
NEEDED = {0: "qkv", 5: "proj", 6: "fc1", 7: "fc2"}
DIRECT = ()
KINDS = ("qkv", "proj", "fc1", "fc2")
SHAPES = {"qkv": (3, WIDE, LANES), "proj": (LANES, WIDE), "fc1": (WIDE, WIDE), "fc2": (WIDE, WIDE)}
GRADS = SHAPES | {"fc1": (4, WIDE, LANES)}
CHUNKS = {"qkv": (6, 3), "proj": (1, 1), "fc1": (4, 4), "fc2": (4, 4)}
REST = 192
FIRST_SHARED = 112


def chunk_list():
    names = [(kind, layer, part) for kind in KINDS for layer in range(LAYERS) for part in range(CHUNKS[kind][layer])]
    return names + [("rest", 0, 0)]


def chunk_shape(kind, layer):
    if kind == "rest":
        return REST, LANES, f32
    *outer, tall, wide = GRADS[kind]
    return tall * int(np.prod(outer)) // CHUNKS[kind][layer], wide, bf16


def chunk_place(kind, layer, part):
    tall = chunk_shape(kind, layer)[0]
    if len(GRADS[kind]) == 2:
        return (pl.ds(part * tall, tall),)
    cuts = GRADS[kind][1] // tall
    return part // cuts, pl.ds(part % cuts * tall, tall)


POOLS = (
    ("weights", 80), ("core", 8), ("side", 16), ("half", 16), ("quad", 16), ("spread", 16), ("share", 16), ("last", 3),
)


def scratch_specs(many, loaded):
    rows = lambda kind: pltpu.VMEM((LAYERS, CAN, WIDE), kind)
    specs = {}
    for kind in KINDS:
        specs["w" + kind] = pltpu.VMEM((BLOCKS, LAYERS, *SHAPES[kind]), bf16)
        specs["g" + kind] = pltpu.VMEM((BLOCKS, LAYERS, *GRADS[kind]), bf16)
    specs["small"] = pltpu.VMEM((BLOCKS, LAYERS, 56, LANES), f32)
    specs["lsmall"] = pltpu.VMEM((LAYERS, 56, LANES), f32)
    specs["grest"] = pltpu.VMEM((BLOCKS, REST, LANES), f32)
    for slot, (kind, layer, part) in enumerate(chunk_list()):
        tall, wide, dtype = chunk_shape(kind, layer)
        specs[f"core{slot}"] = pltpu.VMEM((2, tall, wide), dtype)
        specs[f"side{slot}"] = pltpu.VMEM((tall, wide), dtype)
        specs[f"half{slot}"] = pltpu.VMEM((tall // 2, wide), dtype)
        specs[f"quad{slot}"] = pltpu.VMEM((3, tall // 8, wide), dtype)
        specs[f"group{slot}"] = pltpu.VMEM((many.bit_length() - 1, tall // 8, wide), dtype) if many > 1 else None
    for name, dtype in (
        ("unit1", f32), ("normed1", bf16), ("queries", bf16), ("softs", bf16), ("exacts", f32), ("values", bf16),
        ("convs", f32), ("attended", bf16), ("unit2", f32), ("normed2", bf16),
    ):
        specs[name] = rows(dtype)
    specs["streams"] = pltpu.VMEM((LAYERS + 1, CAN, WIDE), f32)
    specs["inv1"] = pltpu.VMEM((LAYERS, CAN, 1), f32)
    specs["inv2"] = pltpu.VMEM((LAYERS, CAN, 1), f32)
    specs["active"] = pltpu.VMEM((LAYERS, BLOCKS, CAN, WIDE), bf16)
    specs["slope"] = pltpu.VMEM((LAYERS, BLOCKS, CAN, WIDE), f32)
    specs["taps"] = pltpu.VMEM((BLOCKS, 49, 8, LANES), f32)
    specs["wide7"] = pltpu.VMEM((7, 2, 56, WIDE), f32)
    specs["wide3"] = pltpu.VMEM((5, 3, 24, WIDE), f32)
    specs["place"] = pltpu.VMEM((CAN, ROWS_IMG), bf16)
    for name, dtype in (("work", f32), ("grads", f32), ("rel", bf16), ("gatt", bf16)):
        specs[name] = pltpu.VMEM((CAN, WIDE), dtype)
    specs["low"] = pltpu.VMEM((CAN, WIDE), bf16)
    specs["hidden"] = pltpu.VMEM((BLOCKS, CAN, WIDE), bf16)
    specs["out"] = pltpu.VMEM((ROWS_IMG, WIDE), bf16)
    specs["fgrad"] = pltpu.VMEM((ROWS_IMG, WIDE), f32)
    for kind in KINDS:
        specs["r" + kind] = pltpu.VMEM((LAYERS, *GRADS[kind]), bf16)
    specs["rrest"] = pltpu.VMEM((REST, LANES), f32)
    specs["rshared"] = pltpu.VMEM((BLOCKS, 32, LANES), f32)
    for name, item in loaded.items():
        specs[name] = pltpu.VMEM(item.shape, item.dtype)
    specs["load_sems"] = pltpu.SemaphoreType.DMA((len(loaded),))
    specs["store_sems"] = pltpu.SemaphoreType.DMA((3,))
    count = len(chunk_list())
    specs["final_sems"] = pltpu.SemaphoreType.DMA((9,))
    specs["weight_recv"] = pltpu.SemaphoreType.DMA((8, 6))
    specs["weight_own"] = pltpu.SemaphoreType.DMA((9,))
    specs["small_recv"] = pltpu.SemaphoreType.DMA((3,))
    specs["grad_recv"] = pltpu.SemaphoreType.DMA((count, 5 + many.bit_length()))
    if many > 1:
        specs["group_send"] = pltpu.SemaphoreType.DMA((many.bit_length() - 1,))
    specs["last_recv"] = pltpu.SemaphoreType.DMA((3,))
    for name, size in POOLS:
        specs["send_" + name] = pltpu.SemaphoreType.DMA((size,))
    return {name: spec for name, spec in specs.items() if spec is not None}


INPUTS = (
    "geometry", "crpe", "head_bias", "fc1_bias", "feats", "ograd", "same", "moves", "tap_mask", "cpe", "bias", "gain", "shift",
)
SHARDS = ("lqkv", "lproj", "lfc1", "lfc2")
OUTPUTS = ("out", "fgrad", "rqkv", "rproj", "rfc1", "rfc2", "rrest", "rshared")
STEPS = (
    Weights.F1, Weights.Y1, Weights.Z1, Weights.YD, Weights.ZD, Weights.XD,
    Gradient.CS, Gradient.CX, Gradient.CO, Gradient.XA, Gradient.YA, Gradient.ZA, Gradient.ZF, Gradient.FN,
)


def target_rows(geometry):
    packed = geometry[0:1]
    crops, sides, places = packed & 7, (packed >> 3) & 7, packed >> 6
    first = places == 0
    big = sides == 7
    code = crops + jnp.where(first, jnp.where(big, 8, 16), 0)
    square = (ROWS_IMG, ROWS_IMG)
    diagonal = lax.broadcasted_iota(jnp.int32, square, 0) == lax.broadcasted_iota(jnp.int32, square, 1)
    column = jnp.sum(jnp.where(diagonal, code.astype(f32), 0.0), axis=1, keepdims=True).astype(jnp.int32)
    earlier = (column & 7) < crops
    seven = jnp.sum(jnp.where(earlier & ((column & 8) > 0), 1.0, 0.0), axis=0, keepdims=True).astype(jnp.int32)
    three = jnp.sum(jnp.where(earlier & ((column & 16) > 0), 1.0, 0.0), axis=0, keepdims=True).astype(jnp.int32)
    cell = jnp.maximum(places - 1, 0)
    row = jnp.where(big, (cell * 37) >> 8, (cell * 43) >> 7)
    col = cell - row * sides
    in_seven = seven * 56 + row * 8 + col
    in_three = END7 + (three >> 1) * 24 + row * 8 + (three & 1) * 4 + col
    classes = END3 + jnp.where(big, seven, 2 + three)
    return jnp.where(first, classes, jnp.where(big, in_seven, in_three))


def step_kernel(many, names, *refs):
    outside = INPUTS + SHARDS + OUTPUTS
    hbm = types.SimpleNamespace(**dict(zip(outside, refs)))
    r = types.SimpleNamespace(**dict(zip(names, refs[len(outside) :])))
    links = Links(many)
    links.group_send = getattr(r, "group_send", None)
    for name, size in POOLS:
        links.pool(name, getattr(r, "send_" + name))
    loads = [
        pltpu.make_async_copy(getattr(hbm, name), getattr(r, name), r.load_sems.at[slot]) for slot, name in enumerate(INPUTS)
    ]
    for load in loads:
        load.start()
    links.meet()
    weights = {}
    for place, kind in enumerate(KINDS):
        local, full = getattr(hbm, "l" + kind), getattr(r, "w" + kind)
        for layer in range(LAYERS):
            slot = place * LAYERS + layer
            weights[kind, layer] = Weights(
                links, local.at[layer], functools.partial(lambda full, layer, block: full.at[block, layer], full, layer),
                r.weight_recv.at[slot], r.weight_own.at[slot], (kind, layer) in DIRECT,
            )
    for layer in range(LAYERS):
        for kind in KINDS:
            weights[kind, layer].start()
            weights[kind, layer].start_near()
    for load in loads[:4]:
        load.wait()
    for layer in range(LAYERS):
        r.lsmall[layer, 0:49] = r.crpe[:, layer]
        r.lsmall[layer, 49:52] = r.head_bias[:, layer]
        for part in range(4):
            r.lsmall[layer, 52 + part : 53 + part] = r.fc1_bias[layer : layer + 1, part * LANES : (part + 1) * LANES]
    small = Small(links, r.lsmall, r.small, r.small_recv, r.weight_own.at[8])
    small.start()
    for load in loads[4:]:
        load.wait()
    gradients = {}
    left = {kind: list(CHUNKS[kind]) for kind in KINDS}
    finals = []

    def write(kind, layer):
        if kind != "rest":
            left[kind][layer] -= 1
            if left[kind][layer]:
                return
        source, target = (
            (r.rrest, hbm.rrest) if kind == "rest" else (getattr(space, "r" + kind).at[layer] for space in (r, hbm))
        )
        finals.append(pltpu.make_async_copy(source, target, r.final_sems.at[len(finals)]))
        finals[-1].start()
        if kind != "rest":
            return
        mine = r.rshared.at[links.block]
        mine[...] = r.rrest[FIRST_SHARED : FIRST_SHARED + 32]
        for slot, other in enumerate((links.by_core, links.by_side, links.by_far)):
            links.send("last", [(mine, mine, other)], r.last_recv.at[slot])

    for slot, (kind, layer, part) in enumerate(chunk_list()):
        if kind == "rest":
            full = lambda block: r.grest.at[block]
            result = r.rrest
        else:
            place = (layer, *chunk_place(kind, layer, part))
            full = functools.partial(lambda whole, place, block: whole.at[(block, *place)], getattr(r, "g" + kind), place)
            result = getattr(r, "r" + kind).at[place]
        gradients[kind, layer, part] = Gradient(
            links, full, *(getattr(r, name + str(slot), None) for name in ("core", "side", "half", "quad", "group")), result,
            functools.partial(write, kind, layer), r.grad_recv.at[slot],
        )

    def point(which, layer, place):
        for code in ORDER.get((which, layer, place), ()):
            step, kind, of_layer, part = code // 1000, code // 100 % 10, code // 10 % 10, code % 10
            kind = (KINDS + ("rest",))[kind]
            STEPS[step](weights[kind, of_layer] if step < 6 else gradients[kind, of_layer, part])

    def forward_point(layer, place):
        point(0, layer, place)
        if layer == 0 and place == 0:
            small.wait()
        if place == 7 and layer == LAYERS - 1:
            fc2_gradients(r, layer, functools.partial(point, 1, layer))
        if place in NEEDED:
            weights[NEEDED[place], layer].wait()

    r.grest[...] = jnp.zeros_like(r.grest)
    target = target_rows(r.geometry[...])
    r.place[...] = (lax.broadcasted_iota(jnp.int32, (CAN, ROWS_IMG), 0) == target).astype(f32).astype(bf16)
    r.streams[0] = mm(r.place[...], r.feats[...])
    r.grads[...] = mm(r.place[...], r.ograd[...])
    for layer in range(LAYERS):
        forward(r, layer, functools.partial(forward_point, layer))
    for layer in reversed(range(LAYERS)):
        if layer < LAYERS - 1:
            fc2_gradients(r, layer, functools.partial(point, 1, layer))
        backward(r, layer, functools.partial(point, 1, layer))
    point(1, 0, 16)
    feed_forward_sum(r, LAYERS - 1)
    r.out[...] = mm_tn(r.place[...], r.work[...].astype(bf16)).astype(bf16)
    r.fgrad[...] = sum(mm_tn(r.place[...], part) for part in halves(r.grads[...]))
    stores = [
        pltpu.make_async_copy(getattr(r, name), getattr(hbm, name), r.store_sems.at[slot])
        for slot, name in enumerate(("out", "fgrad", "rshared"))
    ]
    stores[0].start()
    stores[1].start()
    point(2, 0, 0)
    for slot, block in enumerate((links.block_core, links.block_side, links.block_far)):
        links.arrived(r.rshared.at[block], r.last_recv.at[slot])
    stores[2].start()
    for store in stores:
        store.wait()
    for final in finals:
        final.wait()
    links.finish()


def proj_matrix(r, layer):
    return jnp.concatenate([r.wproj[SLOT[block], layer] for block in range(BLOCKS)], axis=0)


def forward(r, layer, point):
    real = real_rows()
    fill(stream_parts(r, layer), 1, r.moves, r.wide7, r.wide3)
    for block in range(BLOCKS):
        lanes = lanes_of(block)
        spread_taps(r.taps, block, r.cpe[:, layer, lanes])
        conv = convolve(r.taps, block, 1, 1, 1, False, r.wide7, r.wide3)
        r.work[0:END3, lanes] = r.streams[layer, 0:END3, lanes] + conv + r.bias[0, layer : layer + 1, lanes]
        r.work[END3:CAN, lanes] = r.streams[layer, END3:CAN, lanes]
    unit, inverse, normed = norm_forward(r.work[...], r.gain[layer, 0:1], r.shift[layer, 0:1])
    r.unit1[layer] = unit
    r.inv1[layer] = inverse
    r.normed1[layer] = normed
    point(0)
    for block in range(BLOCKS):
        lanes = lanes_of(block)
        project = mm(normed, side_by_side(r.wqkv[SLOT[block], layer]))
        r.queries[layer, :, lanes] = (project[:, :LANES] + r.small[SLOT[block], layer, 49:50]).astype(bf16)
        r.values[layer, :, lanes] = (project[:, 2 * LANES :] + r.small[SLOT[block], layer, 50:51]).astype(bf16)
        keys = project[:, LANES : 2 * LANES].astype(bf16).astype(f32)
        largest = jnp.max(jnp.where(real, keys, -1e30), axis=0, keepdims=True)
        exponent = jnp.exp(jnp.where(real, keys - largest, 0.0))
        exact = exponent / sum(mm(r.same[...], part) for part in halves(exponent))
        r.exacts[layer, :, lanes] = exact
        r.softs[layer, :, lanes] = exact.astype(bf16)
        spread_taps(r.taps, block, r.small[SLOT[block], layer, 0:49] * r.tap_mask[block, 0:49])
    point(1)
    fill([r.values[layer]], 3, r.moves, r.wide7, r.wide3)
    for block in range(BLOCKS):
        lanes = lanes_of(block)
        query = r.queries[layer, :, lanes]
        soft = r.softs[layer, :, lanes]
        value = r.values[layer, :, lanes]
        factors = []
        for head in range(2):
            masked = jnp.where(head_lanes(head), query, jnp.zeros_like(query))
            mixing = (mm_nt(masked, soft) * SCALE * r.same[...].astype(f32)).astype(bf16)
            factors.append(mm(mixing, value))
        factor = jnp.where(head_lanes(0), factors[0], factors[1])
        conv = convolve(r.taps, block, REACH7[block], REACH3[block], 3, False, r.wide7, r.wide3) + r.small[SLOT[block], layer, 51:52]
        r.convs[layer, 0:END3, lanes] = conv
        r.attended[layer, 0:END3, lanes] = (factor[0:END3] + query[0:END3].astype(f32) * conv).astype(bf16)
        r.attended[layer, END3:CAN, lanes] = factor[END3:CAN].astype(bf16)
        point(2 + block)
    after = r.work[...] + mm(r.attended[layer], proj_matrix(r, layer)) + r.bias[1, layer : layer + 1]
    unit, inverse, normed = norm_forward(after, r.gain[layer, 1:2], r.shift[layer, 1:2])
    r.unit2[layer] = unit
    r.inv2[layer] = inverse
    r.normed2[layer] = normed
    r.work[...] = after + r.bias[2, layer : layer + 1]
    point(6)

    def feed(block, carry):
        hidden = mm(r.normed2[layer], r.wfc1[block, layer]) + jnp.concatenate(
            [r.small[block, layer, 52 + part : 53 + part] for part in range(4)], axis=1
        )
        chance = 0.5 * (1.0 + lax.erf(hidden * np.float32(0.5**0.5)))
        density = jnp.exp(hidden * hidden * -0.5) * np.float32((2 * np.pi) ** -0.5)
        r.slope[layer, block] = chance + hidden * density
        r.active[layer, block] = (hidden * chance).astype(bf16)
        return carry

    lax.fori_loop(0, BLOCKS, feed, 0)
    point(7)

    if layer < LAYERS - 1:
        feed_forward_sum(r, layer)
        r.streams[layer + 1] = r.work[...]
    else:
        r.streams[LAYERS] = r.work[...]


def feed_forward_sum(r, layer):
    if layer == LAYERS - 1:
        r.work[...] = r.streams[LAYERS]

    def collect(block, carry):
        r.work[...] += mm(r.active[layer, block], r.wfc2[block, layer])
        return carry

    lax.fori_loop(0, BLOCKS, collect, 0)


def put_shared(r, layer, row, value):
    for block in range(BLOCKS):
        first = FIRST_SHARED + 16 * layer + row
        r.grest[SLOT[block], first : first + 1] = value[:, block * LANES : (block + 1) * LANES]


def fc2_gradients(r, layer, point):
    put_shared(r, layer, 11, column_sum(r.grads[...]))
    r.low[...] = r.grads[...].astype(bf16)
    for part in range(4):
        rows = lanes_of(part)
        joined = jnp.concatenate([r.active[layer, block, :, rows] for block in range(BLOCKS)], axis=1)
        product = mm_tn(joined, r.low[...]).astype(bf16)
        for block in range(BLOCKS):
            r.gfc2[block, layer, rows] = product[block * LANES : (block + 1) * LANES]
        point(part)


def backward(r, layer, point):
    def put_small(block, row, value):
        r.grest[block, 56 * layer + row : 56 * layer + row + value.shape[0]] = value

    r.work[...] = jnp.zeros_like(r.work)

    def feed(block, carry):
        hidden = (mm_nt(r.low[...], r.wfc2[block, layer]) * r.slope[layer, block]).astype(bf16)
        sums = column_sum(hidden.astype(f32))
        for part in range(4):
            row = 56 * layer + 52 + part
            r.grest[block, row : row + 1] = sums[:, part * LANES : (part + 1) * LANES]
        r.hidden[block] = hidden
        return carry

    lax.fori_loop(0, BLOCKS, feed, 0)
    point(4)
    for part in range(4):
        joined = jnp.concatenate([r.hidden[block, :, lanes_of(part)] for block in range(BLOCKS)], axis=1)
        product = mm_tn(r.normed2[layer], joined).astype(bf16)
        for block in range(BLOCKS):
            r.gfc1[block, layer, part] = product[:, block * LANES : (block + 1) * LANES]
        point(5 + part)

    def collect(block, carry):
        r.work[...] += mm_nt(r.hidden[block], r.wfc1[block, layer])
        return carry

    lax.fori_loop(0, BLOCKS, collect, 0)
    incoming = r.work[...]
    unit = r.unit2[layer]
    put_shared(r, layer, 13, column_sum(incoming * unit))
    put_shared(r, layer, 15, column_sum(incoming))
    r.grads[...] = r.grads[...] + norm_backward(incoming, unit, r.inv2[layer], r.gain[layer, 1:2])
    branch = r.grads[...]
    put_shared(r, layer, 10, column_sum(branch))
    branch = branch.astype(bf16)
    product = mm_tn(r.attended[layer], branch).astype(bf16)
    for block in range(BLOCKS):
        r.gproj[SLOT[block], layer] = product[block * LANES : (block + 1) * LANES]
    r.gatt[...] = mm_nt(branch, proj_matrix(r, layer)).astype(bf16)
    point(9)
    fill([r.values[layer]], 3, r.moves, r.wide7, r.wide3)
    for block in range(BLOCKS):
        lanes = lanes_of(block)
        product = r.gatt[0:END3, lanes].astype(f32) * r.queries[layer, 0:END3, lanes].astype(f32)
        r.rel[0:END3, lanes] = product.astype(bf16)
        r.rel[END3:CAN, lanes] = jnp.zeros((CAN - END3, LANES), bf16)
        put_small(SLOT[block], 51, column_sum(product))
        sums = tap_grads(product, block, REACH7[block], REACH3[block], 3, r.taps, r.wide7, r.wide3)
        put_small(SLOT[block], 0, sums * r.tap_mask[block, 0:49])
        spread_taps(r.taps, block, r.small[SLOT[block], layer, 0:49] * r.tap_mask[block, 0:49])
    point(10)
    fill([r.rel[...]], 3, r.moves, r.wide7, r.wide3)
    r.work[...] = jnp.zeros_like(r.work)
    for block in range(BLOCKS):
        lanes = lanes_of(block)
        query = r.queries[layer, :, lanes]
        soft = r.softs[layer, :, lanes]
        value = r.values[layer, :, lanes]
        grad = r.gatt[:, lanes]
        exact = r.exacts[layer, :, lanes]
        picked = []
        for head in range(2):
            chosen = head_lanes(head)
            zero = jnp.zeros_like(query)
            query_head = jnp.where(chosen, query, zero)
            grad_head = jnp.where(chosen, grad, zero)
            same_low = r.same[...]
            mixing_t = (mm_nt(soft, query_head) * SCALE * same_low.astype(f32)).astype(bf16)
            mix = mm_nt(grad_head, value).astype(bf16) * same_low
            mix_t = mm_nt(value, grad_head).astype(bf16) * same_low
            picked.append((mm(mixing_t, grad), SCALE * mm(mix, soft), SCALE * mm(mix_t, query)))
        grad_value, grad_query, grad_soft = (
            jnp.where(head_lanes(0), one, two) for one, two in zip(*picked)
        )
        grad_soft = grad_soft.astype(bf16).astype(f32)
        weighted = grad_soft * exact
        grad_key = weighted - exact * sum(mm(r.same[...], part) for part in halves(weighted))
        conv = convolve(r.taps, block, REACH7[block], REACH3[block], 3, True, r.wide7, r.wide3)
        grad_value = jnp.concatenate([grad_value[0:END3] + conv, grad_value[END3:CAN]], axis=0).astype(bf16)
        grad_query = jnp.concatenate(
            [grad_query[0:END3] + grad[0:END3].astype(f32) * r.convs[layer, 0:END3, lanes], grad_query[END3:CAN]], axis=0
        ).astype(bf16)
        put_small(SLOT[block], 49, column_sum(grad_query.astype(f32)))
        put_small(SLOT[block], 50, column_sum(grad_value.astype(f32)))
        joined = jnp.concatenate([grad_query, grad_key.astype(bf16), grad_value], axis=1)
        product = mm_tn(r.normed1[layer], joined).astype(bf16)
        for part in range(3):
            r.gqkv[SLOT[block], layer, part] = product[:, part * LANES : (part + 1) * LANES]
        r.work[...] += mm_nt(joined, side_by_side(r.wqkv[SLOT[block], layer]))
        point(11 + block)
    incoming = r.work[...]
    unit = r.unit1[layer]
    put_shared(r, layer, 12, column_sum(incoming * unit))
    put_shared(r, layer, 14, column_sum(incoming))
    r.grads[...] = r.grads[...] + norm_backward(incoming, unit, r.inv1[layer], r.gain[layer, 0:1])
    fill(stream_parts(r, layer), 1, r.moves, r.wide7, r.wide3)
    for block in range(BLOCKS):
        lanes = lanes_of(block)
        product = r.grads[0:END3, lanes]
        first = FIRST_SHARED + 16 * layer
        r.grest[SLOT[block], first + 9 : first + 10] = column_sum(product)
        r.grest[SLOT[block], first : first + 9] = tap_grads(product, block, 1, 1, 1, r.taps, r.wide7, r.wide3)
    fill(halves(r.grads[...]), 1, r.moves, r.wide7, r.wide3)
    for block in range(BLOCKS):
        lanes = lanes_of(block)
        spread_taps(r.taps, block, r.cpe[:, layer, lanes])
        conv = convolve(r.taps, block, 1, 1, 1, True, r.wide7, r.wide3)
        r.grads[0:END3, lanes] = r.grads[0:END3, lanes] + conv
    point(15)


def widen(target, source, layer):
    cut = len(source.shape) > len(target.shape)
    tall, wide = source.shape[-2:]
    for lead in np.ndindex(*source.shape[1:-2]):
        into = (slice(None), pl.ds(lead[0] * wide, wide)) if cut else (*lead, slice(None), slice(None))
        view, seen = target.at[(layer, *into)], source.at[(layer, *lead)]

        def body(index, carry):
            rows = pl.ds(pl.multiple_of(index * 128, 128), 128)
            view[rows] = seen[rows].astype(f32)
            return carry

        lax.fori_loop(0, tall // 128, body, 0)


def finish_kernel(count, *refs):
    taken, given = refs[:8], refs[8 : 8 + count]
    inside, made, load_sems, store_sems = refs[8 + count : 16 + count], refs[16 + count : -2], refs[-2], refs[-1]
    large = [(source, slot, layer) for source, slot in ((3, 10), (2, 8), (0, 4), (1, 7)) for layer in range(LAYERS)]
    large_loads = [
        pltpu.make_async_copy(taken[source].at[layer], inside[source].at[layer], load_sems.at[place])
        for place, (source, slot, layer) in enumerate(large)
    ]
    loads = {
        slot: pltpu.make_async_copy(taken[slot], inside[slot], load_sems.at[4 + slot]) for slot in range(4, 8)
    }
    for load in large_loads + list(loads.values()):
        load.start()
    stores = {
        slot: pltpu.make_async_copy(source, target, store_sems.at[slot])
        for slot, (source, target) in enumerate(zip(tuple(inside[6:]) + tuple(made), given))
        if slot - 2 not in (4, 7, 8, 10)
    }
    cpe, bias, gain, shift, qkv, head_bias, crpe, proj, fc1, fc1_bias, fc2 = made
    large_stores = []
    for place, (source, slot, layer) in enumerate(large):
        large_loads[place].wait()
        widen(made[slot], inside[source], layer)
        sem = store_sems.at[len(given) + place]
        large_stores.append(pltpu.make_async_copy(made[slot].at[layer], given[2 + slot].at[layer], sem))
        large_stores[-1].start()
    for slot in (6, 7):
        loads[slot].wait()
        stores[slot - 6].start()
    loads[4].wait()
    loads[5].wait()
    rrest, rshared = inside[4:6]
    for layer in range(LAYERS):
        for block in range(BLOCKS):
            lanes = lanes_of(block)
            first = layer * 16
            cpe[:, layer, lanes] = rshared[SLOT[block], first : first + 9]
            bias[:, layer, lanes] = rshared[SLOT[block], first + 9 : first + 12]
            gain[layer, :, lanes] = rshared[SLOT[block], first + 12 : first + 14]
            shift[layer, :, lanes] = rshared[SLOT[block], first + 14 : first + 16]
            fc1_bias[layer : layer + 1, lanes] = rrest[layer * 56 + 52 + block : layer * 56 + 53 + block]
        crpe[:, layer] = rrest[layer * 56 : layer * 56 + 49]
        head_bias[:, layer] = rrest[layer * 56 + 49 : layer * 56 + 52]
    for slot in (0, 1, 2, 3, 5, 6, 9):
        stores[2 + slot].start()
    for copy in large_stores + list(stores.values()):
        copy.wait()


def shards(
    data, features, crop_index, grid_size, position, cpe_weight, shared_bias, norm_gain, norm_bias,
    qkv_weight, head_bias, crpe_weight, proj_weight, fc1_weight, fc1_bias, fc2_weight, out_grad,
):
    many = data // 8
    assert data == 8 * many and many & (many - 1) == 0 and features.shape[0] == ROWS_IMG
    start = lax.axis_index("mp") * ROWS_IMG
    mine = [lax.dynamic_slice_in_dim(item, start, ROWS_IMG) for item in (crop_index, grid_size, position)]
    packed = (mine[0] & 7) + 8 * mine[1] + 64 * mine[2]
    geometry = jnp.broadcast_to(packed[None], (8, ROWS_IMG))
    same, moves = canonical_tables()
    swap = lambda item: jnp.transpose(item, (1, 0, 2))
    hbm = pl.BlockSpec(memory_space=pl.ANY)
    shape = jax.ShapeDtypeStruct
    loaded = dict(
        zip(
            INPUTS,
            (
                geometry, swap(crpe_weight), swap(head_bias), fc1_bias, features, out_grad, jnp.asarray(same, bf16),
                jnp.asarray(moves, bf16), jnp.asarray(tap_table()), swap(cpe_weight), swap(shared_bias), norm_gain, norm_bias,
            ),
        )
    )
    specs = scratch_specs(many, loaded)
    results = pl.pallas_call(
        functools.partial(step_kernel, many, tuple(specs)),
        out_shape=(
            shape((ROWS_IMG, WIDE), bf16),
            shape((ROWS_IMG, WIDE), f32),
            *(shape((LAYERS, *GRADS[kind]), bf16) for kind in KINDS),
            shape((REST, LANES), f32),
            shape((BLOCKS, 32, LANES), f32),
        ),
        in_specs=[hbm] * len(INPUTS + SHARDS),
        out_specs=(hbm,) * len(OUTPUTS),
        scratch_shapes=list(specs.values()),
        compiler_params=pltpu.CompilerParams(
            vmem_limit_bytes=63 * 2**20, collective_id=0, has_side_effects=True
        ),
        name="step",
    )(
        *loaded.values(), jnp.transpose(qkv_weight, (0, 2, 1, 3)), proj_weight, fc1_weight, fc2_weight
    )
    out, fgrad, rqkv, rproj, rfc1, rfc2, rrest, rshared = results
    taken = (rqkv, rproj, rfc1, rfc2, rrest, rshared, out, fgrad)
    swapped = lambda item: (item.shape[1], item.shape[0], item.shape[2])
    given = [
        shape(dims, f32)
        for dims in (
            fgrad.shape, swapped(cpe_weight), swapped(shared_bias), norm_gain.shape, norm_bias.shape, rqkv.shape,
            swapped(head_bias), swapped(crpe_weight), rproj.shape, fc1_weight.shape, fc1_bias.shape, rfc2.shape,
        )
    ]
    given = [shape(out.shape, bf16)] + given
    final = list(
        pl.pallas_call(
            functools.partial(finish_kernel, len(given)),
            out_shape=given,
            in_specs=[hbm] * len(taken),
            out_specs=[hbm] * len(given),
            scratch_shapes=[pltpu.VMEM(item.shape, item.dtype) for item in list(taken) + given[2:]]
            + [pltpu.SemaphoreType.DMA((12,)), pltpu.SemaphoreType.DMA((len(given) + 8,))],
            compiler_params=pltpu.CompilerParams(vmem_limit_bytes=63 * 2**20),
            name="finish",
        )(*taken)
    )
    for index in (2, 3, 7, 8):
        final[index] = swap(final[index])
    final[6] = jnp.transpose(final[6], (0, 2, 1, 3))
    return tuple(final)


def solution(mesh):
    placed = (
        P(("dp", "mp"), None),
        P("dp"),
        P("dp"),
        P("dp"),
        P(),
        P(),
        P(),
        P(),
        P(None, None, None, "mp"),
        P(None, None, "mp"),
        P(None, None, "mp"),
        P(None, "mp", None),
        P(None, None, "mp"),
        P(None, "mp"),
        P(None, "mp", None),
        P(("dp", "mp"), None),
    )
    return jax.shard_map(
        functools.partial(shards, mesh.shape["dp"]),
        mesh=mesh,
        in_specs=placed,
        out_specs=(
            P(("dp", "mp"), None),
            P(("dp", "mp"), None),
            P(),
            P(),
            P(),
            P(),
            P(None, None, None, "mp"),
            P(None, None, "mp"),
            P(None, None, "mp"),
            P(None, "mp", None),
            P(None, None, "mp"),
            P(None, "mp"),
            P(None, "mp", None),
        ),
        check_vma=False,
    )
```

```python
import functools
import types

import jax
import jax.numpy as jnp
import numpy as np
from jax import lax
from jax.experimental import pallas as pl
from jax.experimental.pallas import tpu as pltpu
from jax.sharding import PartitionSpec as P

HD = 64
LAYERS = 2
ROWS_IMG = 160
CAN = 192
END7 = 112
END3 = 184
LANES = 128
WIDE = 512
BLOCKS = 4
SLOT = (0, 2, 1, 3)
EPSILON = 1e-06
SCALE = HD ** (-0.5)
REACH7 = (1, 2, 3, 3)
REACH3 = (1, 2, 2, 2)
MESH = pl.DeviceIdType.MESH
f32 = jnp.float32
bf16 = jnp.bfloat16


def canonical_tables():
    crop = np.full(CAN, 100)
    col = np.full(CAN, -1)
    side = np.zeros(CAN, int)
    for t in range(END7):
        if t % 8 < 7:
            crop[t], col[t], side[t] = t // 56, t % 8, 7
    for t in range(END7, END3):
        u = t - END7
        if t % 4 < 3:
            crop[t], col[t], side[t] = 2 + 2 * (u // 24) + (t % 8) // 4, t % 4, 3
    for t in range(END3, CAN):
        crop[t] = t - END3
    same = (crop[:, None] == crop[None, :]).astype(np.float32)
    moves = np.zeros((7, CAN, CAN), np.float32)
    for b in range(-3, 4):
        for t in range(END3):
            if col[t] >= 0 and 0 <= col[t] + b < side[t]:
                moves[b + 3, t, t + b] = 1
    return same, moves


def tap_table():
    table = np.zeros((BLOCKS, 56, LANES), np.float32)
    for channel in range(WIDE):
        head = channel // HD
        reach = 1 if head < 2 else 2 if head < 5 else 3
        for tap in range(49):
            if max(abs(tap // 7 - 3), abs(tap % 7 - 3)) <= reach:
                table[channel // LANES, tap, channel % LANES] = 1
    return table


def mm(left, right):
    return jnp.dot(left, right, preferred_element_type=f32)


def mm_nt(left, right):
    return lax.dot_general(left, right, (((1,), (1,)), ((), ())), preferred_element_type=f32)


def mm_tn(left, right):
    return lax.dot_general(left, right, (((0,), (0,)), ((), ())), preferred_element_type=f32)


def side_by_side(parts):
    return jnp.concatenate([parts[index] for index in range(parts.shape[0])], axis=1)


def stream_parts(r, layer):
    return [r.streams[0].astype(bf16)] if layer == 0 else halves(r.streams[layer])


def halves(values):
    high = values.astype(bf16)
    return [high, (values - high.astype(f32)).astype(bf16)]


def lanes_of(block):
    return pl.ds(block * LANES, LANES)


def column_sum(values):
    return jnp.sum(values, axis=0, keepdims=True)


def fill(parts, reach, moves, wide7, wide3):
    for b in range(-reach, reach + 1):
        moved = sum(mm(moves[b + 3], part) if b else part.astype(f32) for part in parts)
        for grid in range(2):
            wide7[b + 3, grid] = moved[grid * 56 : grid * 56 + 56]
        if abs(b) <= 2:
            for pair in range(3):
                first = END7 + pair * 24
                wide3[b + 2, pair] = moved[first : first + 24]


def tap_row(a, b, half, flip):
    if flip:
        a, b = -a, -b
    return (a + half) * (2 * half + 1) + b + half


def spread_taps(spread, block, rows):
    for row in range(rows.shape[0]):
        spread[block, row] = jnp.broadcast_to(rows[row : row + 1], (8, LANES))


def grid_rows(wide, place, side, lanes):
    return [wide[place, :, row * 8 : row * 8 + 8, lanes] for row in range(side)]


def convolve(spread, block, reach7, reach3, half, flip, wide7, wide3):
    lanes = lanes_of(block)

    def loop(wide, offset, reach, grids, side):
        def body(step, sums):
            b = step - reach
            rows = grid_rows(wide, b + offset, side, lanes)
            sums = list(sums)
            for a in range(-reach, reach + 1):
                weight = spread[block, tap_row(a, b, half, flip)]
                for row in range(max(0, -a), min(side, side - a)):
                    sums[row] = sums[row] + weight * rows[row + a]
            return tuple(sums)

        start = tuple(jnp.zeros((grids, 8, LANES), f32) for _ in range(side))
        sums = lax.fori_loop(0, 2 * reach + 1, body, start)
        return [sums[row][grid] for grid in range(grids) for row in range(side)]

    return jnp.concatenate(loop(wide7, 3, reach7, 2, 7) + loop(wide3, 2, reach3, 3, 3), axis=0)


def tap_grads(grad, block, reach7, reach3, half, spread, wide7, wide3):
    lanes = lanes_of(block)
    count = (2 * half + 1) ** 2
    spread[block, 0:count] = jnp.zeros((count, 8, LANES), f32)

    def loop(wide, offset, reach, part, side):
        def body(step, carry):
            b = step - reach
            rows = grid_rows(wide, b + offset, side, lanes)
            for a in range(-reach, reach + 1):
                total = sum(part[:, row * 8 : row * 8 + 8] * rows[row + a] for row in range(max(0, -a), min(side, side - a)))
                spread[block, tap_row(a, b, half, False)] += jnp.sum(total, axis=0)
            return carry

        lax.fori_loop(0, 2 * reach + 1, body, 0)

    loop(wide7, 3, reach7, grad[:END7].reshape(2, 56, LANES), 7)
    loop(wide3, 2, reach3, grad[END7:END3].reshape(3, 24, LANES), 3)
    return jnp.sum(spread[block, 0:count], axis=1)


def norm_forward(values, gain, bias):
    center = values - jnp.mean(values, axis=-1, keepdims=True)
    spread = jnp.mean(center * center, axis=-1, keepdims=True)
    inverse = lax.rsqrt(spread + EPSILON)
    unit = center * inverse
    return unit, inverse, (unit * gain + bias).astype(bf16)


def norm_backward(incoming, unit, inverse, gain):
    scaled = incoming * gain
    mean_one = jnp.mean(scaled, axis=-1, keepdims=True)
    mean_two = jnp.mean(scaled * unit, axis=-1, keepdims=True)
    return inverse * (scaled - mean_one - unit * mean_two)


def real_rows():
    row = lax.broadcasted_iota(jnp.int32, (CAN, LANES), 0)
    seven = (row < END7) & ((row & 7) != 7)
    three = (row >= END7) & (row < END3) & ((row & 3) != 3)
    return seven | three | (row >= END3)


def head_lanes(head):
    lane = lax.broadcasted_iota(jnp.int32, (CAN, LANES), 1)
    return (lane >= HD) if head else (lane < HD)


def rows_of(ref, start, count):
    rows = pl.ds(pl.multiple_of(start, 8), count)
    return ref.at[rows] if len(ref.shape) == 2 else ref.at[:, rows]


def add_rows(target, start, source, first, count):
    step = next(size for size in (64, 48, 32, 24, 16, 8) if count % size == 0)

    def body(index, carry):
        into = pl.ds(pl.multiple_of(start + index * step, 8), step)
        target[into] = target[into] + source[pl.ds(pl.multiple_of(first + index * step, 8), step)]
        return carry

    lax.fori_loop(0, count // step, body, 0)


class Links:
    def __init__(self, many):
        dp, mp = lax.axis_index("dp"), lax.axis_index("mp")
        self.many = many
        self.core, self.side = lax.rem(mp, 2), lax.div(mp, 2)
        self.half, self.quad, self.group = lax.rem(dp, 2), lax.rem(lax.div(dp, 2), 4), lax.div(dp, 8)
        self.block = self.core * 2 + self.side
        self.block_core = (1 - self.core) * 2 + self.side
        self.block_side = self.core * 2 + 1 - self.side
        self.block_far = (1 - self.core) * 2 + 1 - self.side
        self.by_core = (dp, self.side * 2 + 1 - self.core)
        self.by_side = (dp, (1 - self.side) * 2 + self.core)
        self.by_far = (dp, (1 - self.side) * 2 + 1 - self.core)
        self.by_half = (dp + 1 - 2 * self.half, mp)
        self.by_quad = [
            (self.group * 8 + lax.rem(self.quad + step, 4) * 2 + self.half, mp) for step in range(1, 4)
        ]
        self.rounds = many.bit_length() - 1
        self.by_group = []
        for step in range(self.rounds):
            bit = lax.rem(lax.div(self.group, 1 << step), 2)
            partner = self.group + (1 - 2 * bit) * (1 << step)
            self.by_group.append((partner * 8 + self.quad * 2 + self.half, mp))
        self.pair = lax.rem(self.quad, 2)
        self.by_pair = (self.group * 8 + (self.quad + 1 - 2 * self.pair) * 2 + self.half, mp)
        self.pools = {}

    def meet(self):
        barrier = pltpu.get_barrier_semaphore()
        others = [self.by_core, self.by_side, self.by_far, self.by_half] + self.by_quad + self.by_group
        for other in others:
            pl.semaphore_signal(barrier, inc=1, device_id=other, device_id_type=MESH)
        pl.semaphore_wait(barrier, len(others))

    def pool(self, name, sems):
        self.pools[name] = [sems, [None] * sems.shape[0], 0]

    def take(self, name, waiter):
        sems, waiters, place = self.pools[name]
        if waiters[place] is not None:
            waiters[place]()
        waiters[place] = waiter
        self.pools[name][2] = (place + 1) % len(waiters)
        return sems.at[place]

    def copy(self, source, target, send_sem, recv_sem, other):
        return pltpu.make_async_remote_copy(
            src_ref=source, dst_ref=target, send_sem=send_sem, recv_sem=recv_sem, device_id=other, device_id_type=MESH
        )

    def send(self, name, items, recv_sem, whole=None):
        box = []
        send_sem = self.take(name, lambda: box[0].wait_send())
        copies = [self.copy(source, target, send_sem, recv_sem, other) for source, target, other in items]
        box.append(copies[0] if whole is None else self.copy(whole, whole, send_sem, recv_sem, self.by_core))
        for copy in copies:
            copy.start()

    def arrived(self, target, recv_sem):
        self.copy(target, target, recv_sem, recv_sem, self.by_core).wait_recv()

    def finish(self):
        for sems, waiters, place in self.pools.values():
            for waiter in waiters:
                if waiter is not None:
                    waiter()


class Weights:
    def __init__(self, links, local, full, recv_sems, own_sem, direct):
        self.links, self.local, self.full, self.direct = links, local, full, direct
        self.recv_sems, self.own_sem = recv_sems, own_sem
        self.count = local.shape[-2] // 4
        self.sub = self.count // 2

    def start_of(self, half, pair):
        return (half * 2 + pair) * self.count

    def places(self):
        links = self.links
        far = self.start_of(1 - links.half, 1 - links.pair)
        near = (
            (self.start_of(links.half, links.pair), self.count),
            (self.start_of(1 - links.half, links.pair), self.count),
            (self.start_of(links.half, 1 - links.pair), self.count),
        )
        return near + (((far, self.count),) if self.direct else ((far + self.sub, self.sub), (far, self.sub)))

    def push(self, part, slot, other):
        self.links.send("weights", [(part, part, other)], self.recv_sems.at[slot])

    def take(self, index):
        start, count = self.places()[index]
        part = rows_of(self.full(self.links.block_side), start, count)
        self.links.arrived(part, self.recv_sems.at[index])
        self.push(part, 5, self.links.by_core)
        return part

    def start(self):
        links = self.links
        for index in (0, 3) if self.direct else (0,):
            start, count = self.places()[index]
            target = rows_of(self.full(links.block), start, count)
            links.send("weights", [(rows_of(self.local, start, count), target, links.by_side)], self.recv_sems.at[index])

    def start_near(self):
        links = self.links
        links.send("weights", [(self.local, self.full(links.block), links.by_core)], self.recv_sems.at[5])
        self.own = pltpu.make_async_copy(self.local, self.full(links.block), self.own_sem)
        self.own.start()

    def F1(self):
        part = self.take(0)
        self.push(part, 1, self.links.by_half)
        self.push(part, 2, self.links.by_pair)

    def Y1(self):
        part = self.take(1)
        if not self.direct:
            self.push(rows_of(part, 0, self.sub), 4, self.links.by_pair)

    def Z1(self):
        part = self.take(2)
        if not self.direct:
            self.push(rows_of(part, self.sub, self.sub), 3, self.links.by_half)

    def YD(self):
        self.take(3)

    def ZD(self):
        self.take(4)

    def XD(self):
        self.take(3)

    def wait(self):
        self.own.wait()
        self.links.arrived(self.full(pl.ds((1 - self.links.core) * 2, 2)), self.recv_sems.at[5])


class Small:
    def __init__(self, links, local, full, recv_sems, own_sem):
        self.links, self.local, self.full, self.recv_sems, self.own_sem = links, local, full, recv_sems, own_sem

    def start(self):
        links = self.links
        for slot, other in enumerate((links.by_side, links.by_core)):
            links.send("weights", [(self.local, self.full.at[links.block], other)], self.recv_sems.at[slot])
        self.own = pltpu.make_async_copy(self.local, self.full.at[links.block], self.own_sem)
        self.own.start()

    def wait(self):
        links = self.links
        part = self.full.at[links.block_side]
        links.arrived(part, self.recv_sems.at[0])
        links.send("weights", [(part, part, links.by_core)], self.recv_sems.at[2])
        self.own.wait()
        links.arrived(self.full.at[links.block_core], self.recv_sems.at[1])
        links.arrived(self.full.at[links.block_far], self.recv_sems.at[2])


class Gradient:
    def __init__(self, links, full, core_in, side_in, half_in, quad_in, group_in, result, final, recv_sems):
        self.links, self.full, self.result, self.final = links, full, result, final
        self.core_in, self.side_in, self.half_in, self.quad_in, self.group_in = core_in, side_in, half_in, quad_in, group_in
        self.recv_sems = recv_sems
        self.tall = result.shape[0]
        self.half, self.piece = self.tall // 2, self.tall // 8
        self.here, self.there = links.half * self.half, (1 - links.half) * self.half
        self.mine = self.here + links.quad * self.piece

    def CS(self):
        links = self.links
        source = self.full(pl.ds((1 - links.core) * 2, 2))
        links.send("core", [(source, self.core_in, links.by_core)], self.recv_sems.at[0])

    def CX(self):
        links = self.links
        links.arrived(self.core_in, self.recv_sems.at[0])
        part = self.full(links.block_side)
        add_rows(part, 0, self.core_in.at[1 - links.side], 0, self.tall)
        links.send("side", [(part, self.side_in, links.by_side)], self.recv_sems.at[1])

    def CO(self):
        links = self.links
        add_rows(self.full(links.block), 0, self.core_in.at[links.side], 0, self.tall)

    def XA(self):
        links = self.links
        links.arrived(self.side_in, self.recv_sems.at[1])
        total = self.full(links.block)
        add_rows(total, self.there, self.side_in, self.there, self.half)
        links.send("half", [(rows_of(total, self.there, self.half), self.half_in, links.by_half)], self.recv_sems.at[2])
        add_rows(total, self.here, self.side_in, self.here, self.half)

    def YA(self):
        links = self.links
        links.arrived(self.half_in, self.recv_sems.at[2])
        total = self.full(links.block)
        add_rows(total, self.here, self.half_in, 0, self.half)
        items = []
        for step in range(3):
            start = self.here + lax.rem(links.quad + step + 1, 4) * self.piece
            items.append((rows_of(total, start, self.piece), self.quad_in.at[step], links.by_quad[step]))
        links.send("quad", items, self.recv_sems.at[3], self.quad_in)

    def ZA(self):
        links = self.links
        mine = pl.ds(pl.multiple_of(self.mine, 8), self.piece)
        total = self.full(links.block)
        links.arrived(self.quad_in, self.recv_sems.at[3])
        value = total[mine].astype(f32)
        for step in range(3):
            value = value + self.quad_in[step].astype(f32)
        if links.many > 1:
            for step in range(links.rounds):
                total[mine] = value.astype(total.dtype)
                copy = links.copy(
                    total.at[mine], self.group_in.at[step], links.group_send.at[step], self.recv_sems.at[6 + step],
                    links.by_group[step],
                )
                copy.start()
                copy.wait()
                value = total[mine].astype(f32) + self.group_in[step].astype(f32)
        part = self.result.at[mine]
        part[...] = value.astype(self.result.dtype)
        links.send("spread", [(part, part, other) for other in links.by_quad], self.recv_sems.at[4], self.quad_in)

    def ZF(self):
        links = self.links
        links.arrived(self.quad_in, self.recv_sems.at[4])
        part = rows_of(self.result, self.here, self.half)
        links.send("share", [(part, part, links.by_half)], self.recv_sems.at[5])

    def FN(self):
        self.links.arrived(rows_of(self.result, self.there, self.half), self.recv_sems.at[5])
        self.final()


ORDER = {
    (0, 0, 0): (
        0, 100, 200, 1000, 1100, 300, 2000, 2100, 10, 110, 1200, 2200, 210, 4000, 1300, 4100, 3000,
    ),
    (0, 0, 1): (310, 2300, 1010, 1110, 2010, 3100,),
    (0, 0, 2): (2110, 3200,),
    (0, 0, 4): (4200,),
    (0, 0, 6): (1210,),
    (0, 0, 7): (2210, 1310, 4300, 3300,),
    (0, 1, 0): (2310, 3010, 3110, 4010, 3210, 4110, 4210,),
    (0, 1, 1): (4310,),
    (0, 1, 2): (3310,),
    (1, 1, 0): (6310,),
    (1, 1, 1): (6311,),
    (1, 1, 2): (6312,),
    (1, 1, 3): (6313,),
    (1, 1, 4): (7310, 8310,),
    (1, 1, 5): (7311, 8311, 7312, 6210, 8312,),
    (1, 1, 6): (7313, 8313, 6211,),
    (1, 1, 7): (6212,),
    (1, 1, 8): (6213,),
    (1, 1, 9): (7210, 7211, 7212, 9310, 8210, 7213, 8211, 8212, 8213, 6110,),
    (1, 1, 10): (9311,),
    (1, 1, 11): (7110, 8110,),
    (1, 1, 12): (9312, 10310,),
    (1, 1, 14): (9313, 10311, 6010, 6011, 6012,),
    (1, 0, 0): (10312, 7010, 9210, 8010, 6300, 7011,),
    (1, 0, 1): (7012, 11310, 8011, 8012, 6301,),
    (1, 0, 2): (10313, 6302,),
    (1, 0, 3): (7300, 9211, 8300, 6303,),
    (1, 0, 4): (7301, 11311, 8301, 7302, 10210, 8302, 9212,),
    (1, 0, 5): (7303, 11312, 8303, 6200,),
    (1, 0, 6): (6201,),
    (1, 0, 7): (6202, 12310,),
    (1, 0, 8): (9213, 10211, 6203,),
    (1, 0, 9): (
        7200, 7201, 7202, 10212, 7203, 9110, 11313, 12311, 8200, 8201, 8202, 8203, 6100,
    ),
    (1, 0, 10): (9010, 10213, 7100, 11210, 11211, 12312, 8100, 13310,),
    (1, 0, 11): (9011, 10110,),
    (1, 0, 12): (11212, 13311,),
    (1, 0, 13): (9012, 10010, 12313,),
    (1, 0, 14): (11213, 13312, 6000, 6001, 6002, 6003, 6004, 6005,),
    (1, 0, 15): (9300, 10011, 12210, 12211,),
    (1, 0, 16): (6400,),
    (2, 0, 0): (
        9301, 10012, 11110, 13313, 7400, 7000, 7001, 7002, 7003, 7004, 7005, 12212, 8000, 8001, 8002, 8003, 8004, 8005,
        8400, 9302, 11010, 10300, 12213, 13210, 9303, 11011, 13211, 11012, 10301, 9200, 12110, 13212, 12010, 10302, 9201, 11300,
        13213, 12011, 10303, 9202, 12012, 10200, 11301, 13110, 9203, 11302, 13010, 12300, 10201, 9100, 11303, 13011, 11200, 10202,
        9400, 12301, 13012, 9000, 12302, 10203, 9001, 11201, 13300, 9002, 12303, 10100, 9003, 10400, 12200, 9004, 13301, 11202,
        9005, 10000, 11203, 13302, 10001, 12201, 10002, 11100, 13303, 11400, 10003, 12202, 13200, 11000, 10004, 10005, 12203, 11001,
        13201, 11002, 12100, 13202, 12400, 11003, 13203, 12000, 11004, 11005, 12001, 13100, 12002, 13400, 13000, 12003, 12004, 13001,
        12005, 13002, 13003, 13004, 13005,
    ),
}
NEEDED = {0: "qkv", 5: "proj", 6: "fc1", 7: "fc2"}
DIRECT = ()
KINDS = ("qkv", "proj", "fc1", "fc2")
SHAPES = {"qkv": (3, WIDE, LANES), "proj": (LANES, WIDE), "fc1": (WIDE, WIDE), "fc2": (WIDE, WIDE)}
GRADS = SHAPES | {"fc1": (4, WIDE, LANES)}
CHUNKS = {"qkv": (6, 3), "proj": (1, 1), "fc1": (4, 4), "fc2": (4, 4)}
REST = 192
FIRST_SHARED = 112


def chunk_list():
    names = [(kind, layer, part) for kind in KINDS for layer in range(LAYERS) for part in range(CHUNKS[kind][layer])]
    return names + [("rest", 0, 0)]


def chunk_shape(kind, layer):
    if kind == "rest":
        return REST, LANES, f32
    *outer, tall, wide = GRADS[kind]
    return tall * int(np.prod(outer)) // CHUNKS[kind][layer], wide, bf16


def chunk_place(kind, layer, part):
    tall = chunk_shape(kind, layer)[0]
    if len(GRADS[kind]) == 2:
        return (pl.ds(part * tall, tall),)
    cuts = GRADS[kind][1] // tall
    return part // cuts, pl.ds(part % cuts * tall, tall)


POOLS = (
    ("weights", 80), ("core", 8), ("side", 16), ("half", 16), ("quad", 16), ("spread", 16), ("share", 16), ("last", 3),
)


def scratch_specs(many, loaded):
    rows = lambda kind: pltpu.VMEM((LAYERS, CAN, WIDE), kind)
    specs = {}
    for kind in KINDS:
        specs["w" + kind] = pltpu.VMEM((BLOCKS, LAYERS, *SHAPES[kind]), bf16)
        specs["g" + kind] = pltpu.VMEM((BLOCKS, LAYERS, *GRADS[kind]), bf16)
    specs["small"] = pltpu.VMEM((BLOCKS, LAYERS, 56, LANES), f32)
    specs["lsmall"] = pltpu.VMEM((LAYERS, 56, LANES), f32)
    specs["grest"] = pltpu.VMEM((BLOCKS, REST, LANES), f32)
    for slot, (kind, layer, part) in enumerate(chunk_list()):
        tall, wide, dtype = chunk_shape(kind, layer)
        specs[f"core{slot}"] = pltpu.VMEM((2, tall, wide), dtype)
        specs[f"side{slot}"] = pltpu.VMEM((tall, wide), dtype)
        specs[f"half{slot}"] = pltpu.VMEM((tall // 2, wide), dtype)
        specs[f"quad{slot}"] = pltpu.VMEM((3, tall // 8, wide), dtype)
        specs[f"group{slot}"] = pltpu.VMEM((many.bit_length() - 1, tall // 8, wide), dtype) if many > 1 else None
    for name, dtype in (
        ("unit1", f32), ("normed1", bf16), ("queries", bf16), ("softs", bf16), ("exacts", f32), ("values", bf16),
        ("convs", f32), ("attended", bf16), ("unit2", f32), ("normed2", bf16),
    ):
        specs[name] = rows(dtype)
    specs["streams"] = pltpu.VMEM((LAYERS + 1, CAN, WIDE), f32)
    specs["inv1"] = pltpu.VMEM((LAYERS, CAN, 1), f32)
    specs["inv2"] = pltpu.VMEM((LAYERS, CAN, 1), f32)
    specs["active"] = pltpu.VMEM((LAYERS, BLOCKS, CAN, WIDE), bf16)
    specs["slope"] = pltpu.VMEM((LAYERS, BLOCKS, CAN, WIDE), f32)
    specs["taps"] = pltpu.VMEM((BLOCKS, 49, 8, LANES), f32)
    specs["wide7"] = pltpu.VMEM((7, 2, 56, WIDE), f32)
    specs["wide3"] = pltpu.VMEM((5, 3, 24, WIDE), f32)
    specs["place"] = pltpu.VMEM((CAN, ROWS_IMG), bf16)
    for name, dtype in (("work", f32), ("grads", f32), ("rel", bf16), ("gatt", bf16)):
        specs[name] = pltpu.VMEM((CAN, WIDE), dtype)
    specs["low"] = pltpu.VMEM((CAN, WIDE), bf16)
    specs["hidden"] = pltpu.VMEM((BLOCKS, CAN, WIDE), bf16)
    specs["out"] = pltpu.VMEM((ROWS_IMG, WIDE), bf16)
    specs["fgrad"] = pltpu.VMEM((ROWS_IMG, WIDE), f32)
    for kind in KINDS:
        specs["r" + kind] = pltpu.VMEM((LAYERS, *GRADS[kind]), bf16)
    specs["rrest"] = pltpu.VMEM((REST, LANES), f32)
    specs["rshared"] = pltpu.VMEM((BLOCKS, 32, LANES), f32)
    for name, item in loaded.items():
        specs[name] = pltpu.VMEM(item.shape, item.dtype)
    specs["load_sems"] = pltpu.SemaphoreType.DMA((len(loaded),))
    specs["store_sems"] = pltpu.SemaphoreType.DMA((3,))
    count = len(chunk_list())
    specs["final_sems"] = pltpu.SemaphoreType.DMA((9,))
    specs["weight_recv"] = pltpu.SemaphoreType.DMA((8, 6))
    specs["weight_own"] = pltpu.SemaphoreType.DMA((9,))
    specs["small_recv"] = pltpu.SemaphoreType.DMA((3,))
    specs["grad_recv"] = pltpu.SemaphoreType.DMA((count, 5 + many.bit_length()))
    if many > 1:
        specs["group_send"] = pltpu.SemaphoreType.DMA((many.bit_length() - 1,))
    specs["last_recv"] = pltpu.SemaphoreType.DMA((3,))
    for name, size in POOLS:
        specs["send_" + name] = pltpu.SemaphoreType.DMA((size,))
    return {name: spec for name, spec in specs.items() if spec is not None}


INPUTS = (
    "geometry", "crpe", "head_bias", "fc1_bias", "feats", "ograd", "same", "moves", "tap_mask", "cpe", "bias", "gain", "shift",
)
SHARDS = ("lqkv", "lproj", "lfc1", "lfc2")
OUTPUTS = ("out", "fgrad", "rqkv", "rproj", "rfc1", "rfc2", "rrest", "rshared")
STEPS = (
    Weights.F1, Weights.Y1, Weights.Z1, Weights.YD, Weights.ZD, Weights.XD,
    Gradient.CS, Gradient.CX, Gradient.CO, Gradient.XA, Gradient.YA, Gradient.ZA, Gradient.ZF, Gradient.FN,
)


def target_rows(geometry):
    packed = geometry[0:1]
    crops, sides, places = packed & 7, (packed >> 3) & 7, packed >> 6
    first = places == 0
    big = sides == 7
    code = crops + jnp.where(first, jnp.where(big, 8, 16), 0)
    square = (ROWS_IMG, ROWS_IMG)
    diagonal = lax.broadcasted_iota(jnp.int32, square, 0) == lax.broadcasted_iota(jnp.int32, square, 1)
    column = jnp.sum(jnp.where(diagonal, code.astype(f32), 0.0), axis=1, keepdims=True).astype(jnp.int32)
    earlier = (column & 7) < crops
    seven = jnp.sum(jnp.where(earlier & ((column & 8) > 0), 1.0, 0.0), axis=0, keepdims=True).astype(jnp.int32)
    three = jnp.sum(jnp.where(earlier & ((column & 16) > 0), 1.0, 0.0), axis=0, keepdims=True).astype(jnp.int32)
    cell = jnp.maximum(places - 1, 0)
    row = jnp.where(big, (cell * 37) >> 8, (cell * 43) >> 7)
    col = cell - row * sides
    in_seven = seven * 56 + row * 8 + col
    in_three = END7 + (three >> 1) * 24 + row * 8 + (three & 1) * 4 + col
    classes = END3 + jnp.where(big, seven, 2 + three)
    return jnp.where(first, classes, jnp.where(big, in_seven, in_three))


def step_kernel(many, names, *refs):
    outside = INPUTS + SHARDS + OUTPUTS
    hbm = types.SimpleNamespace(**dict(zip(outside, refs)))
    r = types.SimpleNamespace(**dict(zip(names, refs[len(outside) :])))
    links = Links(many)
    links.group_send = getattr(r, "group_send", None)
    for name, size in POOLS:
        links.pool(name, getattr(r, "send_" + name))
    loads = [
        pltpu.make_async_copy(getattr(hbm, name), getattr(r, name), r.load_sems.at[slot]) for slot, name in enumerate(INPUTS)
    ]
    for load in loads:
        load.start()
    links.meet()
    weights = {}
    for place, kind in enumerate(KINDS):
        local, full = getattr(hbm, "l" + kind), getattr(r, "w" + kind)
        for layer in range(LAYERS):
            slot = place * LAYERS + layer
            weights[kind, layer] = Weights(
                links, local.at[layer], functools.partial(lambda full, layer, block: full.at[block, layer], full, layer),
                r.weight_recv.at[slot], r.weight_own.at[slot], (kind, layer) in DIRECT,
            )
    for layer in range(LAYERS):
        for kind in KINDS:
            weights[kind, layer].start()
            weights[kind, layer].start_near()
    for load in loads[:4]:
        load.wait()
    for layer in range(LAYERS):
        r.lsmall[layer, 0:49] = r.crpe[:, layer]
        r.lsmall[layer, 49:52] = r.head_bias[:, layer]
        for part in range(4):
            r.lsmall[layer, 52 + part : 53 + part] = r.fc1_bias[layer : layer + 1, part * LANES : (part + 1) * LANES]
    small = Small(links, r.lsmall, r.small, r.small_recv, r.weight_own.at[8])
    small.start()
    for load in loads[4:]:
        load.wait()
    gradients = {}
    left = {kind: list(CHUNKS[kind]) for kind in KINDS}
    finals = []

    def write(kind, layer):
        if kind != "rest":
            left[kind][layer] -= 1
            if left[kind][layer]:
                return
        source, target = (
            (r.rrest, hbm.rrest) if kind == "rest" else (getattr(space, "r" + kind).at[layer] for space in (r, hbm))
        )
        finals.append(pltpu.make_async_copy(source, target, r.final_sems.at[len(finals)]))
        finals[-1].start()
        if kind != "rest":
            return
        mine = r.rshared.at[links.block]
        mine[...] = r.rrest[FIRST_SHARED : FIRST_SHARED + 32]
        for slot, other in enumerate((links.by_core, links.by_side, links.by_far)):
            links.send("last", [(mine, mine, other)], r.last_recv.at[slot])

    for slot, (kind, layer, part) in enumerate(chunk_list()):
        if kind == "rest":
            full = lambda block: r.grest.at[block]
            result = r.rrest
        else:
            place = (layer, *chunk_place(kind, layer, part))
            full = functools.partial(lambda whole, place, block: whole.at[(block, *place)], getattr(r, "g" + kind), place)
            result = getattr(r, "r" + kind).at[place]
        gradients[kind, layer, part] = Gradient(
            links, full, *(getattr(r, name + str(slot), None) for name in ("core", "side", "half", "quad", "group")), result,
            functools.partial(write, kind, layer), r.grad_recv.at[slot],
        )

    def point(which, layer, place):
        for code in ORDER.get((which, layer, place), ()):
            step, kind, of_layer, part = code // 1000, code // 100 % 10, code // 10 % 10, code % 10
            kind = (KINDS + ("rest",))[kind]
            STEPS[step](weights[kind, of_layer] if step < 6 else gradients[kind, of_layer, part])

    def forward_point(layer, place):
        point(0, layer, place)
        if layer == 0 and place == 0:
            small.wait()
        if place == 7 and layer == LAYERS - 1:
            fc2_gradients(r, layer, functools.partial(point, 1, layer))
        if place in NEEDED:
            weights[NEEDED[place], layer].wait()

    r.grest[...] = jnp.zeros_like(r.grest)
    target = target_rows(r.geometry[...])
    r.place[...] = (lax.broadcasted_iota(jnp.int32, (CAN, ROWS_IMG), 0) == target).astype(f32).astype(bf16)
    r.streams[0] = mm(r.place[...], r.feats[...])
    r.grads[...] = mm(r.place[...], r.ograd[...])
    for layer in range(LAYERS):
        forward(r, layer, functools.partial(forward_point, layer))
    for layer in reversed(range(LAYERS)):
        if layer < LAYERS - 1:
            fc2_gradients(r, layer, functools.partial(point, 1, layer))
        backward(r, layer, functools.partial(point, 1, layer))
    point(1, 0, 16)
    feed_forward_sum(r, LAYERS - 1)
    r.out[...] = mm_tn(r.place[...], r.work[...].astype(bf16)).astype(bf16)
    r.fgrad[...] = sum(mm_tn(r.place[...], part) for part in halves(r.grads[...]))
    stores = [
        pltpu.make_async_copy(getattr(r, name), getattr(hbm, name), r.store_sems.at[slot])
        for slot, name in enumerate(("out", "fgrad", "rshared"))
    ]
    stores[0].start()
    stores[1].start()
    point(2, 0, 0)
    for slot, block in enumerate((links.block_core, links.block_side, links.block_far)):
        links.arrived(r.rshared.at[block], r.last_recv.at[slot])
    stores[2].start()
    for store in stores:
        store.wait()
    for final in finals:
        final.wait()
    links.finish()


def proj_matrix(r, layer):
    return jnp.concatenate([r.wproj[SLOT[block], layer] for block in range(BLOCKS)], axis=0)


def forward(r, layer, point):
    real = real_rows()
    fill(stream_parts(r, layer), 1, r.moves, r.wide7, r.wide3)
    for block in range(BLOCKS):
        lanes = lanes_of(block)
        spread_taps(r.taps, block, r.cpe[:, layer, lanes])
        conv = convolve(r.taps, block, 1, 1, 1, False, r.wide7, r.wide3)
        r.work[0:END3, lanes] = r.streams[layer, 0:END3, lanes] + conv + r.bias[0, layer : layer + 1, lanes]
        r.work[END3:CAN, lanes] = r.streams[layer, END3:CAN, lanes]
    unit, inverse, normed = norm_forward(r.work[...], r.gain[layer, 0:1], r.shift[layer, 0:1])
    r.unit1[layer] = unit
    r.inv1[layer] = inverse
    r.normed1[layer] = normed
    point(0)
    for block in range(BLOCKS):
        lanes = lanes_of(block)
        project = mm(normed, side_by_side(r.wqkv[SLOT[block], layer]))
        r.queries[layer, :, lanes] = (project[:, :LANES] + r.small[SLOT[block], layer, 49:50]).astype(bf16)
        r.values[layer, :, lanes] = (project[:, 2 * LANES :] + r.small[SLOT[block], layer, 50:51]).astype(bf16)
        keys = project[:, LANES : 2 * LANES].astype(bf16).astype(f32)
        largest = jnp.max(jnp.where(real, keys, -1e30), axis=0, keepdims=True)
        exponent = jnp.exp(jnp.where(real, keys - largest, 0.0))
        exact = exponent / sum(mm(r.same[...], part) for part in halves(exponent))
        r.exacts[layer, :, lanes] = exact
        r.softs[layer, :, lanes] = exact.astype(bf16)
        spread_taps(r.taps, block, r.small[SLOT[block], layer, 0:49] * r.tap_mask[block, 0:49])
    point(1)
    fill([r.values[layer]], 3, r.moves, r.wide7, r.wide3)
    for block in range(BLOCKS):
        lanes = lanes_of(block)
        query = r.queries[layer, :, lanes]
        soft = r.softs[layer, :, lanes]
        value = r.values[layer, :, lanes]
        factors = []
        for head in range(2):
            masked = jnp.where(head_lanes(head), query, jnp.zeros_like(query))
            mixing = (mm_nt(masked, soft) * SCALE * r.same[...].astype(f32)).astype(bf16)
            factors.append(mm(mixing, value))
        factor = jnp.where(head_lanes(0), factors[0], factors[1])
        conv = convolve(r.taps, block, REACH7[block], REACH3[block], 3, False, r.wide7, r.wide3) + r.small[SLOT[block], layer, 51:52]
        r.convs[layer, 0:END3, lanes] = conv
        r.attended[layer, 0:END3, lanes] = (factor[0:END3] + query[0:END3].astype(f32) * conv).astype(bf16)
        r.attended[layer, END3:CAN, lanes] = factor[END3:CAN].astype(bf16)
        point(2 + block)
    after = r.work[...] + mm(r.attended[layer], proj_matrix(r, layer)) + r.bias[1, layer : layer + 1]
    unit, inverse, normed = norm_forward(after, r.gain[layer, 1:2], r.shift[layer, 1:2])
    r.unit2[layer] = unit
    r.inv2[layer] = inverse
    r.normed2[layer] = normed
    r.work[...] = after + r.bias[2, layer : layer + 1]
    point(6)

    def feed(block, carry):
        hidden = mm(r.normed2[layer], r.wfc1[block, layer]) + jnp.concatenate(
            [r.small[block, layer, 52 + part : 53 + part] for part in range(4)], axis=1
        )
        chance = 0.5 * (1.0 + lax.erf(hidden * np.float32(0.5**0.5)))
        density = jnp.exp(hidden * hidden * -0.5) * np.float32((2 * np.pi) ** -0.5)
        r.slope[layer, block] = chance + hidden * density
        r.active[layer, block] = (hidden * chance).astype(bf16)
        return carry

    lax.fori_loop(0, BLOCKS, feed, 0)
    point(7)

    if layer < LAYERS - 1:
        feed_forward_sum(r, layer)
        r.streams[layer + 1] = r.work[...]
    else:
        r.streams[LAYERS] = r.work[...]


def feed_forward_sum(r, layer):
    if layer == LAYERS - 1:
        r.work[...] = r.streams[LAYERS]

    def collect(block, carry):
        r.work[...] += mm(r.active[layer, block], r.wfc2[block, layer])
        return carry

    lax.fori_loop(0, BLOCKS, collect, 0)


def put_shared(r, layer, row, value):
    for block in range(BLOCKS):
        first = FIRST_SHARED + 16 * layer + row
        r.grest[SLOT[block], first : first + 1] = value[:, block * LANES : (block + 1) * LANES]


def fc2_gradients(r, layer, point):
    put_shared(r, layer, 11, column_sum(r.grads[...]))
    r.low[...] = r.grads[...].astype(bf16)
    for part in range(4):
        rows = lanes_of(part)
        joined = jnp.concatenate([r.active[layer, block, :, rows] for block in range(BLOCKS)], axis=1)
        product = mm_tn(joined, r.low[...]).astype(bf16)
        for block in range(BLOCKS):
            r.gfc2[block, layer, rows] = product[block * LANES : (block + 1) * LANES]
        point(part)


def backward(r, layer, point):
    def put_small(block, row, value):
        r.grest[block, 56 * layer + row : 56 * layer + row + value.shape[0]] = value

    r.work[...] = jnp.zeros_like(r.work)

    def feed(block, carry):
        hidden = (mm_nt(r.low[...], r.wfc2[block, layer]) * r.slope[layer, block]).astype(bf16)
        sums = column_sum(hidden.astype(f32))
        for part in range(4):
            row = 56 * layer + 52 + part
            r.grest[block, row : row + 1] = sums[:, part * LANES : (part + 1) * LANES]
        r.hidden[block] = hidden
        return carry

    lax.fori_loop(0, BLOCKS, feed, 0)
    point(4)
    for part in range(4):
        joined = jnp.concatenate([r.hidden[block, :, lanes_of(part)] for block in range(BLOCKS)], axis=1)
        product = mm_tn(r.normed2[layer], joined).astype(bf16)
        for block in range(BLOCKS):
            r.gfc1[block, layer, part] = product[:, block * LANES : (block + 1) * LANES]
        point(5 + part)

    def collect(block, carry):
        r.work[...] += mm_nt(r.hidden[block], r.wfc1[block, layer])
        return carry

    lax.fori_loop(0, BLOCKS, collect, 0)
    incoming = r.work[...]
    unit = r.unit2[layer]
    put_shared(r, layer, 13, column_sum(incoming * unit))
    put_shared(r, layer, 15, column_sum(incoming))
    r.grads[...] = r.grads[...] + norm_backward(incoming, unit, r.inv2[layer], r.gain[layer, 1:2])
    branch = r.grads[...]
    put_shared(r, layer, 10, column_sum(branch))
    branch = branch.astype(bf16)
    product = mm_tn(r.attended[layer], branch).astype(bf16)
    for block in range(BLOCKS):
        r.gproj[SLOT[block], layer] = product[block * LANES : (block + 1) * LANES]
    r.gatt[...] = mm_nt(branch, proj_matrix(r, layer)).astype(bf16)
    point(9)
    fill([r.values[layer]], 3, r.moves, r.wide7, r.wide3)
    for block in range(BLOCKS):
        lanes = lanes_of(block)
        product = r.gatt[0:END3, lanes].astype(f32) * r.queries[layer, 0:END3, lanes].astype(f32)
        r.rel[0:END3, lanes] = product.astype(bf16)
        r.rel[END3:CAN, lanes] = jnp.zeros((CAN - END3, LANES), bf16)
        put_small(SLOT[block], 51, column_sum(product))
        sums = tap_grads(product, block, REACH7[block], REACH3[block], 3, r.taps, r.wide7, r.wide3)
        put_small(SLOT[block], 0, sums * r.tap_mask[block, 0:49])
        spread_taps(r.taps, block, r.small[SLOT[block], layer, 0:49] * r.tap_mask[block, 0:49])
    point(10)
    fill([r.rel[...]], 3, r.moves, r.wide7, r.wide3)
    r.work[...] = jnp.zeros_like(r.work)
    for block in range(BLOCKS):
        lanes = lanes_of(block)
        query = r.queries[layer, :, lanes]
        soft = r.softs[layer, :, lanes]
        value = r.values[layer, :, lanes]
        grad = r.gatt[:, lanes]
        exact = r.exacts[layer, :, lanes]
        picked = []
        for head in range(2):
            chosen = head_lanes(head)
            zero = jnp.zeros_like(query)
            query_head = jnp.where(chosen, query, zero)
            grad_head = jnp.where(chosen, grad, zero)
            same_low = r.same[...]
            mixing_t = (mm_nt(soft, query_head) * SCALE * same_low.astype(f32)).astype(bf16)
            mix = mm_nt(grad_head, value).astype(bf16) * same_low
            mix_t = mm_nt(value, grad_head).astype(bf16) * same_low
            picked.append((mm(mixing_t, grad), SCALE * mm(mix, soft), SCALE * mm(mix_t, query)))
        grad_value, grad_query, grad_soft = (
            jnp.where(head_lanes(0), one, two) for one, two in zip(*picked)
        )
        grad_soft = grad_soft.astype(bf16).astype(f32)
        weighted = grad_soft * exact
        grad_key = weighted - exact * sum(mm(r.same[...], part) for part in halves(weighted))
        conv = convolve(r.taps, block, REACH7[block], REACH3[block], 3, True, r.wide7, r.wide3)
        grad_value = jnp.concatenate([grad_value[0:END3] + conv, grad_value[END3:CAN]], axis=0).astype(bf16)
        grad_query = jnp.concatenate(
            [grad_query[0:END3] + grad[0:END3].astype(f32) * r.convs[layer, 0:END3, lanes], grad_query[END3:CAN]], axis=0
        ).astype(bf16)
        put_small(SLOT[block], 49, column_sum(grad_query.astype(f32)))
        put_small(SLOT[block], 50, column_sum(grad_value.astype(f32)))
        joined = jnp.concatenate([grad_query, grad_key.astype(bf16), grad_value], axis=1)
        product = mm_tn(r.normed1[layer], joined).astype(bf16)
        for part in range(3):
            r.gqkv[SLOT[block], layer, part] = product[:, part * LANES : (part + 1) * LANES]
        r.work[...] += mm_nt(joined, side_by_side(r.wqkv[SLOT[block], layer]))
        point(11 + block)
    incoming = r.work[...]
    unit = r.unit1[layer]
    put_shared(r, layer, 12, column_sum(incoming * unit))
    put_shared(r, layer, 14, column_sum(incoming))
    r.grads[...] = r.grads[...] + norm_backward(incoming, unit, r.inv1[layer], r.gain[layer, 0:1])
    fill(stream_parts(r, layer), 1, r.moves, r.wide7, r.wide3)
    for block in range(BLOCKS):
        lanes = lanes_of(block)
        product = r.grads[0:END3, lanes]
        first = FIRST_SHARED + 16 * layer
        r.grest[SLOT[block], first + 9 : first + 10] = column_sum(product)
        r.grest[SLOT[block], first : first + 9] = tap_grads(product, block, 1, 1, 1, r.taps, r.wide7, r.wide3)
    fill(halves(r.grads[...]), 1, r.moves, r.wide7, r.wide3)
    for block in range(BLOCKS):
        lanes = lanes_of(block)
        spread_taps(r.taps, block, r.cpe[:, layer, lanes])
        conv = convolve(r.taps, block, 1, 1, 1, True, r.wide7, r.wide3)
        r.grads[0:END3, lanes] = r.grads[0:END3, lanes] + conv
    point(15)


def widen(target, source, layer):
    cut = len(source.shape) > len(target.shape)
    tall, wide = source.shape[-2:]
    for lead in np.ndindex(*source.shape[1:-2]):
        into = (slice(None), pl.ds(lead[0] * wide, wide)) if cut else (*lead, slice(None), slice(None))
        view, seen = target.at[(layer, *into)], source.at[(layer, *lead)]

        def body(index, carry):
            rows = pl.ds(pl.multiple_of(index * 128, 128), 128)
            view[rows] = seen[rows].astype(f32)
            return carry

        lax.fori_loop(0, tall // 128, body, 0)


def finish_kernel(count, *refs):
    taken, given = refs[:8], refs[8 : 8 + count]
    inside, made, load_sems, store_sems = refs[8 + count : 16 + count], refs[16 + count : -2], refs[-2], refs[-1]
    large = [(source, slot, layer) for source, slot in ((3, 10), (2, 8), (0, 4), (1, 7)) for layer in range(LAYERS)]
    large_loads = [
        pltpu.make_async_copy(taken[source].at[layer], inside[source].at[layer], load_sems.at[place])
        for place, (source, slot, layer) in enumerate(large)
    ]
    loads = {
        slot: pltpu.make_async_copy(taken[slot], inside[slot], load_sems.at[4 + slot]) for slot in range(4, 8)
    }
    for load in large_loads + list(loads.values()):
        load.start()
    stores = {
        slot: pltpu.make_async_copy(source, target, store_sems.at[slot])
        for slot, (source, target) in enumerate(zip(tuple(inside[6:]) + tuple(made), given))
        if slot - 2 not in (4, 7, 8, 10)
    }
    cpe, bias, gain, shift, qkv, head_bias, crpe, proj, fc1, fc1_bias, fc2 = made
    large_stores = []
    for place, (source, slot, layer) in enumerate(large):
        large_loads[place].wait()
        widen(made[slot], inside[source], layer)
        sem = store_sems.at[len(given) + place]
        large_stores.append(pltpu.make_async_copy(made[slot].at[layer], given[2 + slot].at[layer], sem))
        large_stores[-1].start()
    for slot in (6, 7):
        loads[slot].wait()
        stores[slot - 6].start()
    loads[4].wait()
    loads[5].wait()
    rrest, rshared = inside[4:6]
    for layer in range(LAYERS):
        for block in range(BLOCKS):
            lanes = lanes_of(block)
            first = layer * 16
            cpe[:, layer, lanes] = rshared[SLOT[block], first : first + 9]
            bias[:, layer, lanes] = rshared[SLOT[block], first + 9 : first + 12]
            gain[layer, :, lanes] = rshared[SLOT[block], first + 12 : first + 14]
            shift[layer, :, lanes] = rshared[SLOT[block], first + 14 : first + 16]
            fc1_bias[layer : layer + 1, lanes] = rrest[layer * 56 + 52 + block : layer * 56 + 53 + block]
        crpe[:, layer] = rrest[layer * 56 : layer * 56 + 49]
        head_bias[:, layer] = rrest[layer * 56 + 49 : layer * 56 + 52]
    for slot in (0, 1, 2, 3, 5, 6, 9):
        stores[2 + slot].start()
    for copy in large_stores + list(stores.values()):
        copy.wait()


def shards(
    data, features, crop_index, grid_size, position, cpe_weight, shared_bias, norm_gain, norm_bias,
    qkv_weight, head_bias, crpe_weight, proj_weight, fc1_weight, fc1_bias, fc2_weight, out_grad,
):
    many = data // 8
    assert data == 8 * many and many & (many - 1) == 0 and features.shape[0] == ROWS_IMG
    start = lax.axis_index("mp") * ROWS_IMG
    mine = [lax.dynamic_slice_in_dim(item, start, ROWS_IMG) for item in (crop_index, grid_size, position)]
    packed = (mine[0] & 7) + 8 * mine[1] + 64 * mine[2]
    geometry = jnp.broadcast_to(packed[None], (8, ROWS_IMG))
    same, moves = canonical_tables()
    swap = lambda item: jnp.transpose(item, (1, 0, 2))
    hbm = pl.BlockSpec(memory_space=pl.ANY)
    shape = jax.ShapeDtypeStruct
    loaded = dict(
        zip(
            INPUTS,
            (
                geometry, swap(crpe_weight), swap(head_bias), fc1_bias, features, out_grad, jnp.asarray(same, bf16),
                jnp.asarray(moves, bf16), jnp.asarray(tap_table()), swap(cpe_weight), swap(shared_bias), norm_gain, norm_bias,
            ),
        )
    )
    specs = scratch_specs(many, loaded)
    results = pl.pallas_call(
        functools.partial(step_kernel, many, tuple(specs)),
        out_shape=(
            shape((ROWS_IMG, WIDE), bf16),
            shape((ROWS_IMG, WIDE), f32),
            *(shape((LAYERS, *GRADS[kind]), bf16) for kind in KINDS),
            shape((REST, LANES), f32),
            shape((BLOCKS, 32, LANES), f32),
        ),
        in_specs=[hbm] * len(INPUTS + SHARDS),
        out_specs=(hbm,) * len(OUTPUTS),
        scratch_shapes=list(specs.values()),
        compiler_params=pltpu.CompilerParams(
            vmem_limit_bytes=63 * 2**20, collective_id=0, has_side_effects=True
        ),
        name="step",
    )(
        *loaded.values(), jnp.transpose(qkv_weight, (0, 2, 1, 3)), proj_weight, fc1_weight, fc2_weight
    )
    out, fgrad, rqkv, rproj, rfc1, rfc2, rrest, rshared = results
    taken = (rqkv, rproj, rfc1, rfc2, rrest, rshared, out, fgrad)
    swapped = lambda item: (item.shape[1], item.shape[0], item.shape[2])
    given = [
        shape(dims, f32)
        for dims in (
            fgrad.shape, swapped(cpe_weight), swapped(shared_bias), norm_gain.shape, norm_bias.shape, rqkv.shape,
            swapped(head_bias), swapped(crpe_weight), rproj.shape, fc1_weight.shape, fc1_bias.shape, rfc2.shape,
        )
    ]
    given = [shape(out.shape, bf16)] + given
    final = list(
        pl.pallas_call(
            functools.partial(finish_kernel, len(given)),
            out_shape=given,
            in_specs=[hbm] * len(taken),
            out_specs=[hbm] * len(given),
            scratch_shapes=[pltpu.VMEM(item.shape, item.dtype) for item in list(taken) + given[2:]]
            + [pltpu.SemaphoreType.DMA((12,)), pltpu.SemaphoreType.DMA((len(given) + 8,))],
            compiler_params=pltpu.CompilerParams(vmem_limit_bytes=63 * 2**20),
            name="finish",
        )(*taken)
    )
    for index in (2, 3, 7, 8):
        final[index] = swap(final[index])
    final[6] = jnp.transpose(final[6], (0, 2, 1, 3))
    return tuple(final)


def solution(mesh):
    placed = (
        P(("dp", "mp"), None),
        P("dp"),
        P("dp"),
        P("dp"),
        P(),
        P(),
        P(),
        P(),
        P(None, None, None, "mp"),
        P(None, None, "mp"),
        P(None, None, "mp"),
        P(None, "mp", None),
        P(None, None, "mp"),
        P(None, "mp"),
        P(None, "mp", None),
        P(("dp", "mp"), None),
    )
    return jax.shard_map(
        functools.partial(shards, mesh.shape["dp"]),
        mesh=mesh,
        in_specs=placed,
        out_specs=(
            P(("dp", "mp"), None),
            P(("dp", "mp"), None),
            P(),
            P(),
            P(),
            P(),
            P(None, None, None, "mp"),
            P(None, None, "mp"),
            P(None, None, "mp"),
            P(None, "mp", None),
            P(None, None, "mp"),
            P(None, "mp"),
            P(None, "mp", None),
        ),
        check_vma=False,
    )
```

```python
import functools
import types

import jax
import jax.numpy as jnp
import numpy as np
from jax import lax
from jax.experimental import pallas as pl
from jax.experimental.pallas import tpu as pltpu
from jax.sharding import PartitionSpec as P

HD = 64
LAYERS = 2
ROWS_IMG = 160
CAN = 192
END7 = 112
END3 = 184
LANES = 128
WIDE = 512
BLOCKS = 4
SLOT = (0, 2, 1, 3)
EPSILON = 1e-06
SCALE = HD ** (-0.5)
REACH7 = (1, 2, 3, 3)
REACH3 = (1, 2, 2, 2)
MESH = pl.DeviceIdType.MESH
f32 = jnp.float32
bf16 = jnp.bfloat16


def canonical_tables():
    crop = np.full(CAN, 100)
    col = np.full(CAN, -1)
    side = np.zeros(CAN, int)
    for t in range(END7):
        if t % 8 < 7:
            crop[t], col[t], side[t] = t // 56, t % 8, 7
    for t in range(END7, END3):
        u = t - END7
        if t % 4 < 3:
            crop[t], col[t], side[t] = 2 + 2 * (u // 24) + (t % 8) // 4, t % 4, 3
    for t in range(END3, CAN):
        crop[t] = t - END3
    same = (crop[:, None] == crop[None, :]).astype(np.float32)
    moves = np.zeros((7, CAN, CAN), np.float32)
    for b in range(-3, 4):
        for t in range(END3):
            if col[t] >= 0 and 0 <= col[t] + b < side[t]:
                moves[b + 3, t, t + b] = 1
    return same, moves


def tap_table():
    table = np.zeros((BLOCKS, 56, LANES), np.float32)
    for channel in range(WIDE):
        head = channel // HD
        reach = 1 if head < 2 else 2 if head < 5 else 3
        for tap in range(49):
            if max(abs(tap // 7 - 3), abs(tap % 7 - 3)) <= reach:
                table[channel // LANES, tap, channel % LANES] = 1
    return table


def mm(left, right):
    return jnp.dot(left, right, preferred_element_type=f32)


def mm_nt(left, right):
    return lax.dot_general(left, right, (((1,), (1,)), ((), ())), preferred_element_type=f32)


def mm_tn(left, right):
    return lax.dot_general(left, right, (((0,), (0,)), ((), ())), preferred_element_type=f32)


def side_by_side(parts):
    return jnp.concatenate([parts[index] for index in range(parts.shape[0])], axis=1)


def stream_parts(r, layer):
    return [r.streams[0].astype(bf16)] if layer == 0 else halves(r.streams[layer])


def halves(values):
    high = values.astype(bf16)
    return [high, (values - high.astype(f32)).astype(bf16)]


def lanes_of(block):
    return pl.ds(block * LANES, LANES)


def column_sum(values):
    return jnp.sum(values, axis=0, keepdims=True)


def fill(parts, reach, moves, wide7, wide3):
    for b in range(-reach, reach + 1):
        moved = sum(mm(moves[b + 3], part) if b else part.astype(f32) for part in parts)
        for grid in range(2):
            wide7[b + 3, grid] = moved[grid * 56 : grid * 56 + 56]
        if abs(b) <= 2:
            for pair in range(3):
                first = END7 + pair * 24
                wide3[b + 2, pair] = moved[first : first + 24]


def tap_row(a, b, half, flip):
    if flip:
        a, b = -a, -b
    return (a + half) * (2 * half + 1) + b + half


def spread_taps(spread, block, rows):
    for row in range(rows.shape[0]):
        spread[block, row] = jnp.broadcast_to(rows[row : row + 1], (8, LANES))


def grid_rows(wide, place, side, lanes):
    return [wide[place, :, row * 8 : row * 8 + 8, lanes] for row in range(side)]


def convolve(spread, block, reach7, reach3, half, flip, wide7, wide3):
    lanes = lanes_of(block)

    def loop(wide, offset, reach, grids, side):
        def body(step, sums):
            b = step - reach
            rows = grid_rows(wide, b + offset, side, lanes)
            sums = list(sums)
            for a in range(-reach, reach + 1):
                weight = spread[block, tap_row(a, b, half, flip)]
                for row in range(max(0, -a), min(side, side - a)):
                    sums[row] = sums[row] + weight * rows[row + a]
            return tuple(sums)

        start = tuple(jnp.zeros((grids, 8, LANES), f32) for _ in range(side))
        sums = lax.fori_loop(0, 2 * reach + 1, body, start)
        return [sums[row][grid] for grid in range(grids) for row in range(side)]

    return jnp.concatenate(loop(wide7, 3, reach7, 2, 7) + loop(wide3, 2, reach3, 3, 3), axis=0)


def tap_grads(grad, block, reach7, reach3, half, spread, wide7, wide3):
    lanes = lanes_of(block)
    count = (2 * half + 1) ** 2
    spread[block, 0:count] = jnp.zeros((count, 8, LANES), f32)

    def loop(wide, offset, reach, part, side):
        def body(step, carry):
            b = step - reach
            rows = grid_rows(wide, b + offset, side, lanes)
            for a in range(-reach, reach + 1):
                total = sum(part[:, row * 8 : row * 8 + 8] * rows[row + a] for row in range(max(0, -a), min(side, side - a)))
                spread[block, tap_row(a, b, half, False)] += jnp.sum(total, axis=0)
            return carry

        lax.fori_loop(0, 2 * reach + 1, body, 0)

    loop(wide7, 3, reach7, grad[:END7].reshape(2, 56, LANES), 7)
    loop(wide3, 2, reach3, grad[END7:END3].reshape(3, 24, LANES), 3)
    return jnp.sum(spread[block, 0:count], axis=1)


def norm_forward(values, gain, bias):
    center = values - jnp.mean(values, axis=-1, keepdims=True)
    spread = jnp.mean(center * center, axis=-1, keepdims=True)
    inverse = lax.rsqrt(spread + EPSILON)
    unit = center * inverse
    return unit, inverse, (unit * gain + bias).astype(bf16)


def norm_backward(incoming, unit, inverse, gain):
    scaled = incoming * gain
    mean_one = jnp.mean(scaled, axis=-1, keepdims=True)
    mean_two = jnp.mean(scaled * unit, axis=-1, keepdims=True)
    return inverse * (scaled - mean_one - unit * mean_two)


def real_rows():
    row = lax.broadcasted_iota(jnp.int32, (CAN, LANES), 0)
    seven = (row < END7) & ((row & 7) != 7)
    three = (row >= END7) & (row < END3) & ((row & 3) != 3)
    return seven | three | (row >= END3)


def head_lanes(head):
    lane = lax.broadcasted_iota(jnp.int32, (CAN, LANES), 1)
    return (lane >= HD) if head else (lane < HD)


def rows_of(ref, start, count):
    rows = pl.ds(pl.multiple_of(start, 8), count)
    return ref.at[rows] if len(ref.shape) == 2 else ref.at[:, rows]


def add_rows(target, start, source, first, count):
    step = next(size for size in (64, 48, 32, 24, 16, 8) if count % size == 0)

    def body(index, carry):
        into = pl.ds(pl.multiple_of(start + index * step, 8), step)
        target[into] = target[into] + source[pl.ds(pl.multiple_of(first + index * step, 8), step)]
        return carry

    lax.fori_loop(0, count // step, body, 0)


class Links:
    def __init__(self, many):
        dp, mp = lax.axis_index("dp"), lax.axis_index("mp")
        self.many = many
        self.core, self.side = lax.rem(mp, 2), lax.div(mp, 2)
        self.half, self.quad, self.group = lax.rem(dp, 2), lax.rem(lax.div(dp, 2), 4), lax.div(dp, 8)
        self.block = self.core * 2 + self.side
        self.block_core = (1 - self.core) * 2 + self.side
        self.block_side = self.core * 2 + 1 - self.side
        self.block_far = (1 - self.core) * 2 + 1 - self.side
        self.by_core = (dp, self.side * 2 + 1 - self.core)
        self.by_side = (dp, (1 - self.side) * 2 + self.core)
        self.by_far = (dp, (1 - self.side) * 2 + 1 - self.core)
        self.by_half = (dp + 1 - 2 * self.half, mp)
        self.by_quad = [
            (self.group * 8 + lax.rem(self.quad + step, 4) * 2 + self.half, mp) for step in range(1, 4)
        ]
        self.rounds = many.bit_length() - 1
        self.by_group = []
        for step in range(self.rounds):
            bit = lax.rem(lax.div(self.group, 1 << step), 2)
            partner = self.group + (1 - 2 * bit) * (1 << step)
            self.by_group.append((partner * 8 + self.quad * 2 + self.half, mp))
        self.pair = lax.rem(self.quad, 2)
        self.by_pair = (self.group * 8 + (self.quad + 1 - 2 * self.pair) * 2 + self.half, mp)
        self.pools = {}

    def meet(self):
        barrier = pltpu.get_barrier_semaphore()
        others = [self.by_core, self.by_side, self.by_far, self.by_half] + self.by_quad + self.by_group
        for other in others:
            pl.semaphore_signal(barrier, inc=1, device_id=other, device_id_type=MESH)
        pl.semaphore_wait(barrier, len(others))

    def pool(self, name, sems):
        self.pools[name] = [sems, [None] * sems.shape[0], 0]

    def take(self, name, waiter):
        sems, waiters, place = self.pools[name]
        if waiters[place] is not None:
            waiters[place]()
        waiters[place] = waiter
        self.pools[name][2] = (place + 1) % len(waiters)
        return sems.at[place]

    def copy(self, source, target, send_sem, recv_sem, other):
        return pltpu.make_async_remote_copy(
            src_ref=source, dst_ref=target, send_sem=send_sem, recv_sem=recv_sem, device_id=other, device_id_type=MESH
        )

    def send(self, name, items, recv_sem, whole=None):
        box = []
        send_sem = self.take(name, lambda: box[0].wait_send())
        copies = [self.copy(source, target, send_sem, recv_sem, other) for source, target, other in items]
        box.append(copies[0] if whole is None else self.copy(whole, whole, send_sem, recv_sem, self.by_core))
        for copy in copies:
            copy.start()

    def arrived(self, target, recv_sem):
        self.copy(target, target, recv_sem, recv_sem, self.by_core).wait_recv()

    def finish(self):
        for sems, waiters, place in self.pools.values():
            for waiter in waiters:
                if waiter is not None:
                    waiter()


class Weights:
    def __init__(self, links, local, full, recv_sems, own_sem, direct):
        self.links, self.local, self.full, self.direct = links, local, full, direct
        self.recv_sems, self.own_sem = recv_sems, own_sem
        self.count = local.shape[-2] // 4
        self.sub = self.count // 2

    def start_of(self, half, pair):
        return (half * 2 + pair) * self.count

    def places(self):
        links = self.links
        far = self.start_of(1 - links.half, 1 - links.pair)
        near = (
            (self.start_of(links.half, links.pair), self.count),
            (self.start_of(1 - links.half, links.pair), self.count),
            (self.start_of(links.half, 1 - links.pair), self.count),
        )
        return near + (((far, self.count),) if self.direct else ((far + self.sub, self.sub), (far, self.sub)))

    def push(self, part, slot, other):
        self.links.send("weights", [(part, part, other)], self.recv_sems.at[slot])

    def take(self, index):
        start, count = self.places()[index]
        part = rows_of(self.full(self.links.block_side), start, count)
        self.links.arrived(part, self.recv_sems.at[index])
        self.push(part, 5, self.links.by_core)
        return part

    def start(self):
        links = self.links
        for index in (0, 3) if self.direct else (0,):
            start, count = self.places()[index]
            target = rows_of(self.full(links.block), start, count)
            links.send("weights", [(rows_of(self.local, start, count), target, links.by_side)], self.recv_sems.at[index])

    def start_near(self):
        links = self.links
        links.send("weights", [(self.local, self.full(links.block), links.by_core)], self.recv_sems.at[5])
        self.own = pltpu.make_async_copy(self.local, self.full(links.block), self.own_sem)
        self.own.start()

    def F1(self):
        part = self.take(0)
        self.push(part, 1, self.links.by_half)
        self.push(part, 2, self.links.by_pair)

    def Y1(self):
        part = self.take(1)
        if not self.direct:
            self.push(rows_of(part, 0, self.sub), 4, self.links.by_pair)

    def Z1(self):
        part = self.take(2)
        if not self.direct:
            self.push(rows_of(part, self.sub, self.sub), 3, self.links.by_half)

    def YD(self):
        self.take(3)

    def ZD(self):
        self.take(4)

    def XD(self):
        self.take(3)

    def wait(self):
        self.own.wait()
        self.links.arrived(self.full(pl.ds((1 - self.links.core) * 2, 2)), self.recv_sems.at[5])


class Small:
    def __init__(self, links, local, full, recv_sems, own_sem):
        self.links, self.local, self.full, self.recv_sems, self.own_sem = links, local, full, recv_sems, own_sem

    def start(self):
        links = self.links
        for slot, other in enumerate((links.by_side, links.by_core)):
            links.send("weights", [(self.local, self.full.at[links.block], other)], self.recv_sems.at[slot])
        self.own = pltpu.make_async_copy(self.local, self.full.at[links.block], self.own_sem)
        self.own.start()

    def wait(self):
        links = self.links
        part = self.full.at[links.block_side]
        links.arrived(part, self.recv_sems.at[0])
        links.send("weights", [(part, part, links.by_core)], self.recv_sems.at[2])
        self.own.wait()
        links.arrived(self.full.at[links.block_core], self.recv_sems.at[1])
        links.arrived(self.full.at[links.block_far], self.recv_sems.at[2])


class Gradient:
    def __init__(self, links, full, core_in, side_in, half_in, quad_in, group_in, result, final, recv_sems):
        self.links, self.full, self.result, self.final = links, full, result, final
        self.core_in, self.side_in, self.half_in, self.quad_in, self.group_in = core_in, side_in, half_in, quad_in, group_in
        self.recv_sems = recv_sems
        self.tall = result.shape[0]
        self.half, self.piece = self.tall // 2, self.tall // 8
        self.here, self.there = links.half * self.half, (1 - links.half) * self.half
        self.mine = self.here + links.quad * self.piece

    def CS(self):
        links = self.links
        source = self.full(pl.ds((1 - links.core) * 2, 2))
        links.send("core", [(source, self.core_in, links.by_core)], self.recv_sems.at[0])

    def CX(self):
        links = self.links
        links.arrived(self.core_in, self.recv_sems.at[0])
        part = self.full(links.block_side)
        add_rows(part, 0, self.core_in.at[1 - links.side], 0, self.tall)
        links.send("side", [(part, self.side_in, links.by_side)], self.recv_sems.at[1])

    def CO(self):
        links = self.links
        add_rows(self.full(links.block), 0, self.core_in.at[links.side], 0, self.tall)

    def XA(self):
        links = self.links
        links.arrived(self.side_in, self.recv_sems.at[1])
        total = self.full(links.block)
        add_rows(total, self.there, self.side_in, self.there, self.half)
        links.send("half", [(rows_of(total, self.there, self.half), self.half_in, links.by_half)], self.recv_sems.at[2])
        add_rows(total, self.here, self.side_in, self.here, self.half)

    def YA(self):
        links = self.links
        links.arrived(self.half_in, self.recv_sems.at[2])
        total = self.full(links.block)
        add_rows(total, self.here, self.half_in, 0, self.half)
        items = []
        for step in range(3):
            start = self.here + lax.rem(links.quad + step + 1, 4) * self.piece
            items.append((rows_of(total, start, self.piece), self.quad_in.at[step], links.by_quad[step]))
        links.send("quad", items, self.recv_sems.at[3], self.quad_in)

    def ZA(self):
        links = self.links
        mine = pl.ds(pl.multiple_of(self.mine, 8), self.piece)
        total = self.full(links.block)
        links.arrived(self.quad_in, self.recv_sems.at[3])
        value = total[mine].astype(f32)
        for step in range(3):
            value = value + self.quad_in[step].astype(f32)
        if links.many > 1:
            for step in range(links.rounds):
                total[mine] = value.astype(total.dtype)
                copy = links.copy(
                    total.at[mine], self.group_in.at[step], links.group_send.at[step], self.recv_sems.at[6 + step],
                    links.by_group[step],
                )
                copy.start()
                copy.wait()
                value = total[mine].astype(f32) + self.group_in[step].astype(f32)
        part = self.result.at[mine]
        part[...] = value.astype(self.result.dtype)
        links.send("spread", [(part, part, other) for other in links.by_quad], self.recv_sems.at[4], self.quad_in)

    def ZF(self):
        links = self.links
        links.arrived(self.quad_in, self.recv_sems.at[4])
        part = rows_of(self.result, self.here, self.half)
        links.send("share", [(part, part, links.by_half)], self.recv_sems.at[5])

    def FN(self):
        self.links.arrived(rows_of(self.result, self.there, self.half), self.recv_sems.at[5])
        self.final()


ORDER = {
    (0, 0, 0): (
        0, 100, 200, 1000, 1100, 300, 2000, 2100, 10, 110, 1200, 2200, 210, 4000, 1300, 4100, 3000,
    ),
    (0, 0, 1): (310, 2300, 1010, 1110, 2010, 3100,),
    (0, 0, 2): (2110, 3200,),
    (0, 0, 4): (4200,),
    (0, 0, 5): (1210,),
    (0, 0, 7): (2210, 1310, 4300, 3300,),
    (0, 1, 0): (2310, 3010, 3110, 4010, 4110, 3210, 4210,),
    (0, 1, 1): (4310,),
    (0, 1, 2): (3310,),
    (1, 1, 0): (6310,),
    (1, 1, 1): (6311,),
    (1, 1, 2): (6312,),
    (1, 1, 3): (6313,),
    (1, 1, 4): (7310, 7311, 8310, 8311,),
    (1, 1, 5): (7312, 8312, 7313, 6210, 8313,),
    (1, 1, 6): (6211,),
    (1, 1, 7): (6212,),
    (1, 1, 8): (6213,),
    (1, 1, 9): (7210, 7211, 7212, 7213, 9310, 8210, 8211, 8212, 8213, 6110,),
    (1, 1, 10): (7110, 9311, 8110,),
    (1, 1, 11): (9312, 10310,),
    (1, 1, 13): (9313,),
    (1, 1, 14): (10311, 6010, 6011, 6012,),
    (1, 1, 15): (9210, 10312, 7010, 11310, 8010,),
    (1, 0, 0): (7011, 10313, 7012, 9211, 8011, 8012, 6300,),
    (1, 0, 1): (6301,),
    (1, 0, 2): (6302,),
    (1, 0, 3): (6303, 11311,),
    (1, 0, 4): (7300, 7301, 9212, 7302, 10210, 8300, 8301, 7303, 11312, 10211, 8302, 8303,),
    (1, 0, 5): (9213, 12310, 6200,),
    (1, 0, 6): (6201,),
    (1, 0, 7): (6202, 11313,),
    (1, 0, 8): (6203,),
    (1, 0, 9): (
        7200, 7201, 7202, 7203, 9110, 10212, 9010, 10213, 11210, 12311, 8200, 12312, 8201, 8202, 8203, 13310, 6100,
    ),
    (1, 0, 10): (7100, 9011, 11211, 12313, 8100, 10110,),
    (1, 0, 11): (9012, 10010, 11212,),
    (1, 0, 12): (11213, 13311,),
    (1, 0, 13): (9300, 12210, 13312,),
    (1, 0, 14): (10011, 12211, 6000, 6001, 6002, 6003, 6004, 6005, 9301, 13313,),
    (1, 0, 15): (10012, 11110, 9302, 11010, 10300,),
    (1, 0, 16): (6400, 12212,),
    (2, 0, 0): (
        9303, 12213, 7400, 7000, 7001, 7002, 7003, 7004, 7005, 11011, 8000, 8001, 8002, 8003, 8004, 8005, 8400, 13210,
        13211, 10301, 9200, 10302, 11012, 13212, 12110, 9201, 10303, 12010, 13213, 11300, 9202, 10200, 12011, 13110, 11301, 9203,
        10201, 11302, 13010, 12012, 9100, 10202, 11303, 13011, 12300, 9400, 10203, 11200, 9000, 13012, 12301, 9001, 10100, 11201,
        9002, 13300, 12302, 9003, 10400, 11202, 9004, 10000, 12303, 9005, 13301, 10001, 11203, 10002, 12200, 13302, 10003, 11100,
        10004, 12201, 13303, 10005, 11400, 13200, 12202, 11000, 11001, 13201, 12203, 11002, 11003, 13202, 12100, 11004, 11005, 13203,
        12400, 12000, 12001, 12002, 13100, 12003, 12004, 12005, 13400, 13000, 13001, 13002, 13003, 13004, 13005,
    ),
}
NEEDED = {0: "qkv", 5: "proj", 6: "fc1", 7: "fc2"}
DIRECT = ()
KINDS = ("qkv", "proj", "fc1", "fc2")
SHAPES = {"qkv": (3, WIDE, LANES), "proj": (LANES, WIDE), "fc1": (WIDE, WIDE), "fc2": (WIDE, WIDE)}
GRADS = SHAPES | {"fc1": (4, WIDE, LANES)}
CHUNKS = {"qkv": (6, 3), "proj": (1, 1), "fc1": (4, 4), "fc2": (4, 4)}
REST = 192
FIRST_SHARED = 112


def chunk_list():
    names = [(kind, layer, part) for kind in KINDS for layer in range(LAYERS) for part in range(CHUNKS[kind][layer])]
    return names + [("rest", 0, 0)]


def chunk_shape(kind, layer):
    if kind == "rest":
        return REST, LANES, f32
    *outer, tall, wide = GRADS[kind]
    return tall * int(np.prod(outer)) // CHUNKS[kind][layer], wide, bf16


def chunk_place(kind, layer, part):
    tall = chunk_shape(kind, layer)[0]
    if len(GRADS[kind]) == 2:
        return (pl.ds(part * tall, tall),)
    cuts = GRADS[kind][1] // tall
    return part // cuts, pl.ds(part % cuts * tall, tall)


POOLS = (
    ("weights", 80), ("core", 8), ("side", 16), ("half", 16), ("quad", 16), ("spread", 16), ("share", 16), ("last", 3),
)


def scratch_specs(many, loaded):
    rows = lambda kind: pltpu.VMEM((LAYERS, CAN, WIDE), kind)
    specs = {}
    for kind in KINDS:
        specs["w" + kind] = pltpu.VMEM((BLOCKS, LAYERS, *SHAPES[kind]), bf16)
        specs["g" + kind] = pltpu.VMEM((BLOCKS, LAYERS, *GRADS[kind]), bf16)
    specs["small"] = pltpu.VMEM((BLOCKS, LAYERS, 56, LANES), f32)
    specs["lsmall"] = pltpu.VMEM((LAYERS, 56, LANES), f32)
    specs["grest"] = pltpu.VMEM((BLOCKS, REST, LANES), f32)
    for slot, (kind, layer, part) in enumerate(chunk_list()):
        tall, wide, dtype = chunk_shape(kind, layer)
        specs[f"core{slot}"] = pltpu.VMEM((2, tall, wide), dtype)
        specs[f"side{slot}"] = pltpu.VMEM((tall, wide), dtype)
        specs[f"half{slot}"] = pltpu.VMEM((tall // 2, wide), dtype)
        specs[f"quad{slot}"] = pltpu.VMEM((3, tall // 8, wide), dtype)
        specs[f"group{slot}"] = pltpu.VMEM((many.bit_length() - 1, tall // 8, wide), dtype) if many > 1 else None
    for name, dtype in (
        ("unit1", f32), ("normed1", bf16), ("queries", bf16), ("softs", bf16), ("exacts", f32), ("values", bf16),
        ("convs", f32), ("attended", bf16), ("unit2", f32), ("normed2", bf16),
    ):
        specs[name] = rows(dtype)
    specs["streams"] = pltpu.VMEM((LAYERS + 1, CAN, WIDE), f32)
    specs["inv1"] = pltpu.VMEM((LAYERS, CAN, 1), f32)
    specs["inv2"] = pltpu.VMEM((LAYERS, CAN, 1), f32)
    specs["active"] = pltpu.VMEM((LAYERS, BLOCKS, CAN, WIDE), bf16)
    specs["slope"] = pltpu.VMEM((LAYERS, BLOCKS, CAN, WIDE), f32)
    specs["taps"] = pltpu.VMEM((BLOCKS, 49, 8, LANES), f32)
    specs["wide7"] = pltpu.VMEM((7, 2, 56, WIDE), f32)
    specs["wide3"] = pltpu.VMEM((5, 3, 24, WIDE), f32)
    specs["place"] = pltpu.VMEM((CAN, ROWS_IMG), bf16)
    for name, dtype in (("work", f32), ("grads", f32), ("rel", bf16), ("gatt", bf16)):
        specs[name] = pltpu.VMEM((CAN, WIDE), dtype)
    specs["low"] = pltpu.VMEM((CAN, WIDE), bf16)
    specs["hidden"] = pltpu.VMEM((BLOCKS, CAN, WIDE), bf16)
    specs["out"] = pltpu.VMEM((ROWS_IMG, WIDE), bf16)
    specs["fgrad"] = pltpu.VMEM((ROWS_IMG, WIDE), f32)
    for kind in KINDS:
        specs["r" + kind] = pltpu.VMEM((LAYERS, *GRADS[kind]), bf16)
    specs["rrest"] = pltpu.VMEM((REST, LANES), f32)
    specs["rshared"] = pltpu.VMEM((BLOCKS, 32, LANES), f32)
    for name, item in loaded.items():
        specs[name] = pltpu.VMEM(item.shape, item.dtype)
    specs["load_sems"] = pltpu.SemaphoreType.DMA((len(loaded),))
    specs["store_sems"] = pltpu.SemaphoreType.DMA((3,))
    count = len(chunk_list())
    specs["final_sems"] = pltpu.SemaphoreType.DMA((9,))
    specs["weight_recv"] = pltpu.SemaphoreType.DMA((8, 6))
    specs["weight_own"] = pltpu.SemaphoreType.DMA((9,))
    specs["small_recv"] = pltpu.SemaphoreType.DMA((3,))
    specs["grad_recv"] = pltpu.SemaphoreType.DMA((count, 5 + many.bit_length()))
    if many > 1:
        specs["group_send"] = pltpu.SemaphoreType.DMA((many.bit_length() - 1,))
    specs["last_recv"] = pltpu.SemaphoreType.DMA((3,))
    for name, size in POOLS:
        specs["send_" + name] = pltpu.SemaphoreType.DMA((size,))
    return {name: spec for name, spec in specs.items() if spec is not None}


INPUTS = (
    "geometry", "crpe", "head_bias", "fc1_bias", "feats", "ograd", "same", "moves", "tap_mask", "cpe", "bias", "gain", "shift",
)
SHARDS = ("lqkv", "lproj", "lfc1", "lfc2")
OUTPUTS = ("out", "fgrad", "rqkv", "rproj", "rfc1", "rfc2", "rrest", "rshared")
STEPS = (
    Weights.F1, Weights.Y1, Weights.Z1, Weights.YD, Weights.ZD, Weights.XD,
    Gradient.CS, Gradient.CX, Gradient.CO, Gradient.XA, Gradient.YA, Gradient.ZA, Gradient.ZF, Gradient.FN,
)


def target_rows(geometry):
    packed = geometry[0:1]
    crops, sides, places = packed & 7, (packed >> 3) & 7, packed >> 6
    first = places == 0
    big = sides == 7
    code = crops + jnp.where(first, jnp.where(big, 8, 16), 0)
    square = (ROWS_IMG, ROWS_IMG)
    diagonal = lax.broadcasted_iota(jnp.int32, square, 0) == lax.broadcasted_iota(jnp.int32, square, 1)
    column = jnp.sum(jnp.where(diagonal, code.astype(f32), 0.0), axis=1, keepdims=True).astype(jnp.int32)
    earlier = (column & 7) < crops
    seven = jnp.sum(jnp.where(earlier & ((column & 8) > 0), 1.0, 0.0), axis=0, keepdims=True).astype(jnp.int32)
    three = jnp.sum(jnp.where(earlier & ((column & 16) > 0), 1.0, 0.0), axis=0, keepdims=True).astype(jnp.int32)
    cell = jnp.maximum(places - 1, 0)
    row = jnp.where(big, (cell * 37) >> 8, (cell * 43) >> 7)
    col = cell - row * sides
    in_seven = seven * 56 + row * 8 + col
    in_three = END7 + (three >> 1) * 24 + row * 8 + (three & 1) * 4 + col
    classes = END3 + jnp.where(big, seven, 2 + three)
    return jnp.where(first, classes, jnp.where(big, in_seven, in_three))


def step_kernel(many, names, *refs):
    outside = INPUTS + SHARDS + OUTPUTS
    hbm = types.SimpleNamespace(**dict(zip(outside, refs)))
    r = types.SimpleNamespace(**dict(zip(names, refs[len(outside) :])))
    links = Links(many)
    links.group_send = getattr(r, "group_send", None)
    for name, size in POOLS:
        links.pool(name, getattr(r, "send_" + name))
    loads = [
        pltpu.make_async_copy(getattr(hbm, name), getattr(r, name), r.load_sems.at[slot]) for slot, name in enumerate(INPUTS)
    ]
    for load in loads:
        load.start()
    links.meet()
    weights = {}
    for place, kind in enumerate(KINDS):
        local, full = getattr(hbm, "l" + kind), getattr(r, "w" + kind)
        for layer in range(LAYERS):
            slot = place * LAYERS + layer
            weights[kind, layer] = Weights(
                links, local.at[layer], functools.partial(lambda full, layer, block: full.at[block, layer], full, layer),
                r.weight_recv.at[slot], r.weight_own.at[slot], (kind, layer) in DIRECT,
            )
    for layer in range(LAYERS):
        for kind in KINDS:
            weights[kind, layer].start()
            weights[kind, layer].start_near()
    for load in loads[:4]:
        load.wait()
    for layer in range(LAYERS):
        r.lsmall[layer, 0:49] = r.crpe[:, layer]
        r.lsmall[layer, 49:52] = r.head_bias[:, layer]
        for part in range(4):
            r.lsmall[layer, 52 + part : 53 + part] = r.fc1_bias[layer : layer + 1, part * LANES : (part + 1) * LANES]
    small = Small(links, r.lsmall, r.small, r.small_recv, r.weight_own.at[8])
    small.start()
    for load in loads[4:]:
        load.wait()
    gradients = {}
    left = {kind: list(CHUNKS[kind]) for kind in KINDS}
    finals = []

    def write(kind, layer):
        if kind != "rest":
            left[kind][layer] -= 1
            if left[kind][layer]:
                return
        source, target = (
            (r.rrest, hbm.rrest) if kind == "rest" else (getattr(space, "r" + kind).at[layer] for space in (r, hbm))
        )
        finals.append(pltpu.make_async_copy(source, target, r.final_sems.at[len(finals)]))
        finals[-1].start()
        if kind != "rest":
            return
        mine = r.rshared.at[links.block]
        mine[...] = r.rrest[FIRST_SHARED : FIRST_SHARED + 32]
        for slot, other in enumerate((links.by_core, links.by_side, links.by_far)):
            links.send("last", [(mine, mine, other)], r.last_recv.at[slot])

    for slot, (kind, layer, part) in enumerate(chunk_list()):
        if kind == "rest":
            full = lambda block: r.grest.at[block]
            result = r.rrest
        else:
            place = (layer, *chunk_place(kind, layer, part))
            full = functools.partial(lambda whole, place, block: whole.at[(block, *place)], getattr(r, "g" + kind), place)
            result = getattr(r, "r" + kind).at[place]
        gradients[kind, layer, part] = Gradient(
            links, full, *(getattr(r, name + str(slot), None) for name in ("core", "side", "half", "quad", "group")), result,
            functools.partial(write, kind, layer), r.grad_recv.at[slot],
        )

    def point(which, layer, place):
        for code in ORDER.get((which, layer, place), ()):
            step, kind, of_layer, part = code // 1000, code // 100 % 10, code // 10 % 10, code % 10
            kind = (KINDS + ("rest",))[kind]
            STEPS[step](weights[kind, of_layer] if step < 6 else gradients[kind, of_layer, part])

    def forward_point(layer, place):
        point(0, layer, place)
        if layer == 0 and place == 0:
            small.wait()
        if place == 7 and layer == LAYERS - 1:
            fc2_gradients(r, layer, functools.partial(point, 1, layer))
        if place in NEEDED:
            weights[NEEDED[place], layer].wait()

    r.grest[...] = jnp.zeros_like(r.grest)
    target = target_rows(r.geometry[...])
    r.place[...] = (lax.broadcasted_iota(jnp.int32, (CAN, ROWS_IMG), 0) == target).astype(f32).astype(bf16)
    r.streams[0] = mm(r.place[...], r.feats[...])
    r.grads[...] = mm(r.place[...], r.ograd[...])
    for layer in range(LAYERS):
        forward(r, layer, functools.partial(forward_point, layer))
    for layer in reversed(range(LAYERS)):
        if layer < LAYERS - 1:
            fc2_gradients(r, layer, functools.partial(point, 1, layer))
        backward(r, layer, functools.partial(point, 1, layer))
    point(1, 0, 16)
    feed_forward_sum(r, LAYERS - 1)
    r.out[...] = mm_tn(r.place[...], r.work[...].astype(bf16)).astype(bf16)
    r.fgrad[...] = sum(mm_tn(r.place[...], part) for part in halves(r.grads[...]))
    stores = [
        pltpu.make_async_copy(getattr(r, name), getattr(hbm, name), r.store_sems.at[slot])
        for slot, name in enumerate(("out", "fgrad", "rshared"))
    ]
    stores[0].start()
    stores[1].start()
    point(2, 0, 0)
    for slot, block in enumerate((links.block_core, links.block_side, links.block_far)):
        links.arrived(r.rshared.at[block], r.last_recv.at[slot])
    stores[2].start()
    for store in stores:
        store.wait()
    for final in finals:
        final.wait()
    links.finish()


def proj_matrix(r, layer):
    return jnp.concatenate([r.wproj[SLOT[block], layer] for block in range(BLOCKS)], axis=0)


def forward(r, layer, point):
    real = real_rows()
    fill(stream_parts(r, layer), 1, r.moves, r.wide7, r.wide3)
    for block in range(BLOCKS):
        lanes = lanes_of(block)
        spread_taps(r.taps, block, r.cpe[:, layer, lanes])
        conv = convolve(r.taps, block, 1, 1, 1, False, r.wide7, r.wide3)
        r.work[0:END3, lanes] = r.streams[layer, 0:END3, lanes] + conv + r.bias[0, layer : layer + 1, lanes]
        r.work[END3:CAN, lanes] = r.streams[layer, END3:CAN, lanes]
    unit, inverse, normed = norm_forward(r.work[...], r.gain[layer, 0:1], r.shift[layer, 0:1])
    r.unit1[layer] = unit
    r.inv1[layer] = inverse
    r.normed1[layer] = normed
    point(0)
    for block in range(BLOCKS):
        lanes = lanes_of(block)
        project = mm(normed, side_by_side(r.wqkv[SLOT[block], layer]))
        r.queries[layer, :, lanes] = (project[:, :LANES] + r.small[SLOT[block], layer, 49:50]).astype(bf16)
        r.values[layer, :, lanes] = (project[:, 2 * LANES :] + r.small[SLOT[block], layer, 50:51]).astype(bf16)
        keys = project[:, LANES : 2 * LANES].astype(bf16).astype(f32)
        largest = jnp.max(jnp.where(real, keys, -1e30), axis=0, keepdims=True)
        exponent = jnp.exp(jnp.where(real, keys - largest, 0.0))
        exact = exponent / sum(mm(r.same[...], part) for part in halves(exponent))
        r.exacts[layer, :, lanes] = exact
        r.softs[layer, :, lanes] = exact.astype(bf16)
        spread_taps(r.taps, block, r.small[SLOT[block], layer, 0:49] * r.tap_mask[block, 0:49])
    point(1)
    fill([r.values[layer]], 3, r.moves, r.wide7, r.wide3)
    for block in range(BLOCKS):
        lanes = lanes_of(block)
        query = r.queries[layer, :, lanes]
        soft = r.softs[layer, :, lanes]
        value = r.values[layer, :, lanes]
        factors = []
        for head in range(2):
            masked = jnp.where(head_lanes(head), query, jnp.zeros_like(query))
            mixing = (mm_nt(masked, soft) * SCALE * r.same[...].astype(f32)).astype(bf16)
            factors.append(mm(mixing, value))
        factor = jnp.where(head_lanes(0), factors[0], factors[1])
        conv = convolve(r.taps, block, REACH7[block], REACH3[block], 3, False, r.wide7, r.wide3) + r.small[SLOT[block], layer, 51:52]
        r.convs[layer, 0:END3, lanes] = conv
        r.attended[layer, 0:END3, lanes] = (factor[0:END3] + query[0:END3].astype(f32) * conv).astype(bf16)
        r.attended[layer, END3:CAN, lanes] = factor[END3:CAN].astype(bf16)
        point(2 + block)
    after = r.work[...] + mm(r.attended[layer], proj_matrix(r, layer)) + r.bias[1, layer : layer + 1]
    unit, inverse, normed = norm_forward(after, r.gain[layer, 1:2], r.shift[layer, 1:2])
    r.unit2[layer] = unit
    r.inv2[layer] = inverse
    r.normed2[layer] = normed
    r.work[...] = after + r.bias[2, layer : layer + 1]
    point(6)

    def feed(block, carry):
        hidden = mm(r.normed2[layer], r.wfc1[block, layer]) + jnp.concatenate(
            [r.small[block, layer, 52 + part : 53 + part] for part in range(4)], axis=1
        )
        chance = 0.5 * (1.0 + lax.erf(hidden * np.float32(0.5**0.5)))
        density = jnp.exp(hidden * hidden * -0.5) * np.float32((2 * np.pi) ** -0.5)
        r.slope[layer, block] = chance + hidden * density
        r.active[layer, block] = (hidden * chance).astype(bf16)
        return carry

    lax.fori_loop(0, BLOCKS, feed, 0)
    point(7)

    if layer < LAYERS - 1:
        feed_forward_sum(r, layer)
        r.streams[layer + 1] = r.work[...]
    else:
        r.streams[LAYERS] = r.work[...]


def feed_forward_sum(r, layer):
    if layer == LAYERS - 1:
        r.work[...] = r.streams[LAYERS]

    def collect(block, carry):
        r.work[...] += mm(r.active[layer, block], r.wfc2[block, layer])
        return carry

    lax.fori_loop(0, BLOCKS, collect, 0)


def put_shared(r, layer, row, value):
    for block in range(BLOCKS):
        first = FIRST_SHARED + 16 * layer + row
        r.grest[SLOT[block], first : first + 1] = value[:, block * LANES : (block + 1) * LANES]


def fc2_gradients(r, layer, point):
    put_shared(r, layer, 11, column_sum(r.grads[...]))
    r.low[...] = r.grads[...].astype(bf16)
    for part in range(4):
        rows = lanes_of(part)
        joined = jnp.concatenate([r.active[layer, block, :, rows] for block in range(BLOCKS)], axis=1)
        product = mm_tn(joined, r.low[...]).astype(bf16)
        for block in range(BLOCKS):
            r.gfc2[block, layer, rows] = product[block * LANES : (block + 1) * LANES]
        point(part)


def backward(r, layer, point):
    def put_small(block, row, value):
        r.grest[block, 56 * layer + row : 56 * layer + row + value.shape[0]] = value

    r.work[...] = jnp.zeros_like(r.work)

    def feed(block, carry):
        hidden = (mm_nt(r.low[...], r.wfc2[block, layer]) * r.slope[layer, block]).astype(bf16)
        sums = column_sum(hidden.astype(f32))
        for part in range(4):
            row = 56 * layer + 52 + part
            r.grest[block, row : row + 1] = sums[:, part * LANES : (part + 1) * LANES]
        r.hidden[block] = hidden
        return carry

    lax.fori_loop(0, BLOCKS, feed, 0)
    point(4)
    for part in range(4):
        joined = jnp.concatenate([r.hidden[block, :, lanes_of(part)] for block in range(BLOCKS)], axis=1)
        product = mm_tn(r.normed2[layer], joined).astype(bf16)
        for block in range(BLOCKS):
            r.gfc1[block, layer, part] = product[:, block * LANES : (block + 1) * LANES]
        point(5 + part)

    def collect(block, carry):
        r.work[...] += mm_nt(r.hidden[block], r.wfc1[block, layer])
        return carry

    lax.fori_loop(0, BLOCKS, collect, 0)
    incoming = r.work[...]
    unit = r.unit2[layer]
    put_shared(r, layer, 13, column_sum(incoming * unit))
    put_shared(r, layer, 15, column_sum(incoming))
    r.grads[...] = r.grads[...] + norm_backward(incoming, unit, r.inv2[layer], r.gain[layer, 1:2])
    branch = r.grads[...]
    put_shared(r, layer, 10, column_sum(branch))
    branch = branch.astype(bf16)
    product = mm_tn(r.attended[layer], branch).astype(bf16)
    for block in range(BLOCKS):
        r.gproj[SLOT[block], layer] = product[block * LANES : (block + 1) * LANES]
    r.gatt[...] = mm_nt(branch, proj_matrix(r, layer)).astype(bf16)
    point(9)
    fill([r.values[layer]], 3, r.moves, r.wide7, r.wide3)
    for block in range(BLOCKS):
        lanes = lanes_of(block)
        product = r.gatt[0:END3, lanes].astype(f32) * r.queries[layer, 0:END3, lanes].astype(f32)
        r.rel[0:END3, lanes] = product.astype(bf16)
        r.rel[END3:CAN, lanes] = jnp.zeros((CAN - END3, LANES), bf16)
        put_small(SLOT[block], 51, column_sum(product))
        sums = tap_grads(product, block, REACH7[block], REACH3[block], 3, r.taps, r.wide7, r.wide3)
        put_small(SLOT[block], 0, sums * r.tap_mask[block, 0:49])
        spread_taps(r.taps, block, r.small[SLOT[block], layer, 0:49] * r.tap_mask[block, 0:49])
    point(10)
    fill([r.rel[...]], 3, r.moves, r.wide7, r.wide3)
    r.work[...] = jnp.zeros_like(r.work)
    for block in range(BLOCKS):
        lanes = lanes_of(block)
        query = r.queries[layer, :, lanes]
        soft = r.softs[layer, :, lanes]
        value = r.values[layer, :, lanes]
        grad = r.gatt[:, lanes]
        exact = r.exacts[layer, :, lanes]
        picked = []
        for head in range(2):
            chosen = head_lanes(head)
            zero = jnp.zeros_like(query)
            query_head = jnp.where(chosen, query, zero)
            grad_head = jnp.where(chosen, grad, zero)
            same_low = r.same[...]
            mixing_t = (mm_nt(soft, query_head) * SCALE * same_low.astype(f32)).astype(bf16)
            mix = mm_nt(grad_head, value).astype(bf16) * same_low
            mix_t = mm_nt(value, grad_head).astype(bf16) * same_low
            picked.append((mm(mixing_t, grad), SCALE * mm(mix, soft), SCALE * mm(mix_t, query)))
        grad_value, grad_query, grad_soft = (
            jnp.where(head_lanes(0), one, two) for one, two in zip(*picked)
        )
        grad_soft = grad_soft.astype(bf16).astype(f32)
        weighted = grad_soft * exact
        grad_key = weighted - exact * sum(mm(r.same[...], part) for part in halves(weighted))
        conv = convolve(r.taps, block, REACH7[block], REACH3[block], 3, True, r.wide7, r.wide3)
        grad_value = jnp.concatenate([grad_value[0:END3] + conv, grad_value[END3:CAN]], axis=0).astype(bf16)
        grad_query = jnp.concatenate(
            [grad_query[0:END3] + grad[0:END3].astype(f32) * r.convs[layer, 0:END3, lanes], grad_query[END3:CAN]], axis=0
        ).astype(bf16)
        put_small(SLOT[block], 49, column_sum(grad_query.astype(f32)))
        put_small(SLOT[block], 50, column_sum(grad_value.astype(f32)))
        joined = jnp.concatenate([grad_query, grad_key.astype(bf16), grad_value], axis=1)
        product = mm_tn(r.normed1[layer], joined).astype(bf16)
        for part in range(3):
            r.gqkv[SLOT[block], layer, part] = product[:, part * LANES : (part + 1) * LANES]
        r.work[...] += mm_nt(joined, side_by_side(r.wqkv[SLOT[block], layer]))
        point(11 + block)
    incoming = r.work[...]
    unit = r.unit1[layer]
    put_shared(r, layer, 12, column_sum(incoming * unit))
    put_shared(r, layer, 14, column_sum(incoming))
    r.grads[...] = r.grads[...] + norm_backward(incoming, unit, r.inv1[layer], r.gain[layer, 0:1])
    fill(stream_parts(r, layer), 1, r.moves, r.wide7, r.wide3)
    for block in range(BLOCKS):
        lanes = lanes_of(block)
        product = r.grads[0:END3, lanes]
        first = FIRST_SHARED + 16 * layer
        r.grest[SLOT[block], first + 9 : first + 10] = column_sum(product)
        r.grest[SLOT[block], first : first + 9] = tap_grads(product, block, 1, 1, 1, r.taps, r.wide7, r.wide3)
    fill(halves(r.grads[...]), 1, r.moves, r.wide7, r.wide3)
    for block in range(BLOCKS):
        lanes = lanes_of(block)
        spread_taps(r.taps, block, r.cpe[:, layer, lanes])
        conv = convolve(r.taps, block, 1, 1, 1, True, r.wide7, r.wide3)
        r.grads[0:END3, lanes] = r.grads[0:END3, lanes] + conv
    point(15)


def widen(target, source, layer):
    cut = len(source.shape) > len(target.shape)
    tall, wide = source.shape[-2:]
    for lead in np.ndindex(*source.shape[1:-2]):
        into = (slice(None), pl.ds(lead[0] * wide, wide)) if cut else (*lead, slice(None), slice(None))
        view, seen = target.at[(layer, *into)], source.at[(layer, *lead)]

        def body(index, carry):
            rows = pl.ds(pl.multiple_of(index * 128, 128), 128)
            view[rows] = seen[rows].astype(f32)
            return carry

        lax.fori_loop(0, tall // 128, body, 0)


def finish_kernel(count, *refs):
    taken, given = refs[:8], refs[8 : 8 + count]
    inside, made, load_sems, store_sems = refs[8 + count : 16 + count], refs[16 + count : -2], refs[-2], refs[-1]
    large = [(source, slot, layer) for source, slot in ((3, 10), (2, 8), (0, 4), (1, 7)) for layer in range(LAYERS)]
    large_loads = [
        pltpu.make_async_copy(taken[source].at[layer], inside[source].at[layer], load_sems.at[place])
        for place, (source, slot, layer) in enumerate(large)
    ]
    loads = {
        slot: pltpu.make_async_copy(taken[slot], inside[slot], load_sems.at[4 + slot]) for slot in range(4, 8)
    }
    for load in large_loads + list(loads.values()):
        load.start()
    stores = {
        slot: pltpu.make_async_copy(source, target, store_sems.at[slot])
        for slot, (source, target) in enumerate(zip(tuple(inside[6:]) + tuple(made), given))
        if slot - 2 not in (4, 7, 8, 10)
    }
    cpe, bias, gain, shift, qkv, head_bias, crpe, proj, fc1, fc1_bias, fc2 = made
    large_stores = []
    for place, (source, slot, layer) in enumerate(large):
        large_loads[place].wait()
        widen(made[slot], inside[source], layer)
        sem = store_sems.at[len(given) + place]
        large_stores.append(pltpu.make_async_copy(made[slot].at[layer], given[2 + slot].at[layer], sem))
        large_stores[-1].start()
    for slot in (6, 7):
        loads[slot].wait()
        stores[slot - 6].start()
    loads[4].wait()
    loads[5].wait()
    rrest, rshared = inside[4:6]
    for layer in range(LAYERS):
        for block in range(BLOCKS):
            lanes = lanes_of(block)
            first = layer * 16
            cpe[:, layer, lanes] = rshared[SLOT[block], first : first + 9]
            bias[:, layer, lanes] = rshared[SLOT[block], first + 9 : first + 12]
            gain[layer, :, lanes] = rshared[SLOT[block], first + 12 : first + 14]
            shift[layer, :, lanes] = rshared[SLOT[block], first + 14 : first + 16]
            fc1_bias[layer : layer + 1, lanes] = rrest[layer * 56 + 52 + block : layer * 56 + 53 + block]
        crpe[:, layer] = rrest[layer * 56 : layer * 56 + 49]
        head_bias[:, layer] = rrest[layer * 56 + 49 : layer * 56 + 52]
    for slot in (0, 1, 2, 3, 5, 6, 9):
        stores[2 + slot].start()
    for copy in large_stores + list(stores.values()):
        copy.wait()


def shards(
    data, features, crop_index, grid_size, position, cpe_weight, shared_bias, norm_gain, norm_bias,
    qkv_weight, head_bias, crpe_weight, proj_weight, fc1_weight, fc1_bias, fc2_weight, out_grad,
):
    many = data // 8
    assert data == 8 * many and many & (many - 1) == 0 and features.shape[0] == ROWS_IMG
    start = lax.axis_index("mp") * ROWS_IMG
    mine = [lax.dynamic_slice_in_dim(item, start, ROWS_IMG) for item in (crop_index, grid_size, position)]
    packed = (mine[0] & 7) + 8 * mine[1] + 64 * mine[2]
    geometry = jnp.broadcast_to(packed[None], (8, ROWS_IMG))
    same, moves = canonical_tables()
    swap = lambda item: jnp.transpose(item, (1, 0, 2))
    hbm = pl.BlockSpec(memory_space=pl.ANY)
    shape = jax.ShapeDtypeStruct
    loaded = dict(
        zip(
            INPUTS,
            (
                geometry, swap(crpe_weight), swap(head_bias), fc1_bias, features, out_grad, jnp.asarray(same, bf16),
                jnp.asarray(moves, bf16), jnp.asarray(tap_table()), swap(cpe_weight), swap(shared_bias), norm_gain, norm_bias,
            ),
        )
    )
    specs = scratch_specs(many, loaded)
    results = pl.pallas_call(
        functools.partial(step_kernel, many, tuple(specs)),
        out_shape=(
            shape((ROWS_IMG, WIDE), bf16),
            shape((ROWS_IMG, WIDE), f32),
            *(shape((LAYERS, *GRADS[kind]), bf16) for kind in KINDS),
            shape((REST, LANES), f32),
            shape((BLOCKS, 32, LANES), f32),
        ),
        in_specs=[hbm] * len(INPUTS + SHARDS),
        out_specs=(hbm,) * len(OUTPUTS),
        scratch_shapes=list(specs.values()),
        compiler_params=pltpu.CompilerParams(
            vmem_limit_bytes=63 * 2**20, collective_id=0, has_side_effects=True
        ),
        name="step",
    )(
        *loaded.values(), jnp.transpose(qkv_weight, (0, 2, 1, 3)), proj_weight, fc1_weight, fc2_weight
    )
    out, fgrad, rqkv, rproj, rfc1, rfc2, rrest, rshared = results
    taken = (rqkv, rproj, rfc1, rfc2, rrest, rshared, out, fgrad)
    swapped = lambda item: (item.shape[1], item.shape[0], item.shape[2])
    given = [
        shape(dims, f32)
        for dims in (
            fgrad.shape, swapped(cpe_weight), swapped(shared_bias), norm_gain.shape, norm_bias.shape, rqkv.shape,
            swapped(head_bias), swapped(crpe_weight), rproj.shape, fc1_weight.shape, fc1_bias.shape, rfc2.shape,
        )
    ]
    given = [shape(out.shape, bf16)] + given
    final = list(
        pl.pallas_call(
            functools.partial(finish_kernel, len(given)),
            out_shape=given,
            in_specs=[hbm] * len(taken),
            out_specs=[hbm] * len(given),
            scratch_shapes=[pltpu.VMEM(item.shape, item.dtype) for item in list(taken) + given[2:]]
            + [pltpu.SemaphoreType.DMA((12,)), pltpu.SemaphoreType.DMA((len(given) + 8,))],
            compiler_params=pltpu.CompilerParams(vmem_limit_bytes=63 * 2**20),
            name="finish",
        )(*taken)
    )
    for index in (2, 3, 7, 8):
        final[index] = swap(final[index])
    final[6] = jnp.transpose(final[6], (0, 2, 1, 3))
    return tuple(final)


def solution(mesh):
    placed = (
        P(("dp", "mp"), None),
        P("dp"),
        P("dp"),
        P("dp"),
        P(),
        P(),
        P(),
        P(),
        P(None, None, None, "mp"),
        P(None, None, "mp"),
        P(None, None, "mp"),
        P(None, "mp", None),
        P(None, None, "mp"),
        P(None, "mp"),
        P(None, "mp", None),
        P(("dp", "mp"), None),
    )
    return jax.shard_map(
        functools.partial(shards, mesh.shape["dp"]),
        mesh=mesh,
        in_specs=placed,
        out_specs=(
            P(("dp", "mp"), None),
            P(("dp", "mp"), None),
            P(),
            P(),
            P(),
            P(),
            P(None, None, None, "mp"),
            P(None, None, "mp"),
            P(None, None, "mp"),
            P(None, "mp", None),
            P(None, None, "mp"),
            P(None, "mp"),
            P(None, "mp", None),
        ),
        check_vma=False,
    )
```
